32 devices in a mesh: branch: 2 (over core), frames: 16 (over z, y, x).
Axes of the slice: x: 2, y: 2, z: 4, core: 2. Of those that a mesh axis runs over, the one named last changes fastest.
Arguments:
- frames_in: bfloat16 [2, 16384, 384], P('branch', 'frames'), may hold values from -6 to 6
- seg_ids: int32 [2, 16384], P(None, 'frames'), may hold values from 0 to 63, as said below
- cotangent: bfloat16 [2, 16384, 384], P('branch', 'frames'), may hold values from -6 to 6
- params: float32 [2, 2363520], P('branch', 'frames')
- first_moment: float32 [2, 2363520], P('branch', 'frames')
- second_moment: float32 [2, 2363520], P('branch', 'frames'), as said below
Outputs:
- out_frames: bfloat16 [2, 16384, 384], P('branch', 'frames')
- input_grad: float32 [2, 16384, 384], P('branch', 'frames')
- clipped_grad: float32 [2, 2363520], P('branch', 'frames')
- vector_grad: float32 [2, 4224], P('branch', 'frames')
- grad_norm: float32 [], replicated
- first_new: float32 [2, 2363520], P('branch', 'frames')
- second_new: float32 [2, 2363520], P('branch', 'frames')
- new_params: float32 [2, 2363520], P('branch', 'frames')
The draws below stay inside these ranges and needn't reach their ends.
Inputs may be any that keep to these rules, and one draw needn't show every extreme that they name: `seg_ids`: in each aligned block of 1024 frames of a branch (the same blocks in both branches) the segment numbers are whole segments, numbered without gaps, never decreasing, and starting at (block index) * 4; both branches' blocks hold the same numbers, 1 to 4 of them; the last block holds 4. `second_moment`: positive.
All inputs are finite; a program needn't handle non-finite values.
Results may differ from the reference program's by a relative error of at most 0.012.
Values may be sent and summed in bfloat16 or wider, within the bound.
A program may use at most 256 MiB of HBM per device.

```python
import math
import jax
import jax.numpy as jnp
from jax import lax

HEADS = 8
HEAD_DIM = 48
D = 384
FF = 1536
NV = 11
TOK_DEV = 1024
SEGS = 4
STEP = 5
TOKENS = 16384
P_SIZE = 2363520
N_FRAMES = 16


def matrix_scale(col):
    sizes = (3 * D * D, D * D, D * D, 2 * D * D, D * D, D * FF, FF * D)
    scales = (1.0 / math.sqrt(D), 6.0 / math.sqrt(D), 1.0 / math.sqrt(D), 1.0 / math.sqrt(D), 6.0 / math.sqrt(D), 1.0 / math.sqrt(D), 1.0 / math.sqrt(FF))
    bounds = []
    running = 0
    for size_at in sizes:
        running += size_at // N_FRAMES
        bounds.append(running)
    result = jnp.zeros(col.shape, jnp.float32)
    for bound_at, scale_at in zip(bounds[::-1], scales[::-1]):
        result = jnp.where(col < bound_at, scale_at, result)
    return result


def base_draw(key, shape):
    return jax.random.normal(key, shape, jnp.float32)


def draw_params(key, part):
    slice_len = P_SIZE // N_FRAMES
    index = jnp.arange(P_SIZE)
    col = index % slice_len
    row = index // slice_len
    first_key, second_key = jax.random.split(key)
    base = base_draw(first_key, (2, P_SIZE))
    vec_col = (8 * D * D + 2 * D * FF) // N_FRAMES
    is_vector = col >= vec_col
    within = row * (NV * D // N_FRAMES) + (col - vec_col)
    which = within // D
    is_gain = is_vector & ((which % 2 == 0) | (which >= 8))
    gains = 1.0 + 0.25 * jax.random.uniform(second_key, (2, P_SIZE), jnp.float32, -1.0, 1.0)
    values = jnp.where(is_gain, gains, jnp.where(is_vector, 0.3 * base, matrix_scale(col) * base))
    return values.astype(jnp.float32)


def draw_first_moment(key, part):
    grad_size = 0.01 * math.sqrt(TOKENS)
    return (0.1 / 0.9 * grad_size * base_draw(key, (2, P_SIZE))).astype(jnp.float32)


def draw_second_moment(key, part):
    grad_size = 0.01 * math.sqrt(TOKENS)
    factor = jnp.exp(jax.random.uniform(key, (2, P_SIZE), jnp.float32, 0.0, math.log(4.0)))
    return (0.001 / 0.999 * grad_size * grad_size * factor).astype(jnp.float32)


def draw_seg_ids(key, part):
    blocks = TOKENS // TOK_DEV
    count_key, time_key, spec_key = jax.random.split(key, 3)
    counts = jax.random.randint(count_key, (blocks,), 1, SEGS + 1)
    counts = counts.at[blocks - 1].set(SEGS)

    def one_block(block_key, count):
        ranks = jax.random.permutation(block_key, TOK_DEV - 1)
        starts = (ranks < count - 1).astype(jnp.int32)
        return jnp.concatenate([jnp.zeros((1,), jnp.int32), jnp.cumsum(starts).astype(jnp.int32)])
    time_ids = jax.vmap(one_block)(jax.random.split(time_key, blocks), counts)
    spec_ids = jax.vmap(one_block)(jax.random.split(spec_key, blocks), counts)
    offsets = (jnp.arange(blocks) * SEGS).astype(jnp.int32)
    both_ids = jnp.stack([time_ids, spec_ids]) + offsets[None, :, None]
    return both_ids.reshape(2, TOKENS).astype(jnp.int32)


def block_scale(stream_key, extent, cuts, low, largest):
    def one(dim, parts):
        steps = jax.random.uniform(jax.random.fold_in(jax.random.fold_in(stream_key, 6), dim), (parts,), jnp.float32, low / len(cuts), largest / len(cuts))
        return jnp.repeat(jnp.exp(steps), extent[dim] // parts).reshape((-1,) + (1,) * (len(extent) - dim - 1))

    level = one(*cuts[0])
    for cut in cuts[1:]:
        level = level * one(*cut)
    return level


def scatter_about(own_key, extent, deviation, most, shards=(), kind=jnp.bfloat16):
    drawn = jax.random.normal(own_key, extent, jnp.float32) * deviation
    if len(shards) > 0:
        drawn = block_scale(own_key, extent, shards, -0.22, 0.18) * drawn
    return jnp.clip(drawn, min=-most, max=most).astype(kind)


def setup_inputs(seed: int = 0) -> dict:
    streams_of = jax.random.split(jax.random.key(seed), 7)
    frames_in = scatter_about(streams_of[0], (2, TOKENS, D), 1.0, 6.0, ((0, 2), (1, 16)))
    seg_ids = draw_seg_ids(jax.random.fold_in(streams_of[6], 71), 0)
    cotangent = scatter_about(streams_of[2], (2, TOKENS, D), 1.0, 6.0, ((0, 2), (1, 16)))
    params = draw_params(jax.random.fold_in(streams_of[6], 71), 0)
    first_moment = draw_first_moment(jax.random.fold_in(streams_of[6], 71), 0)
    second_moment = draw_second_moment(jax.random.fold_in(streams_of[6], 71), 0)
    return {"frames_in": frames_in, "seg_ids": seg_ids, "cotangent": cotangent, "params": params, "first_moment": first_moment, "second_moment": second_moment}


@jax.custom_vjp
def low(v):
    return lax.optimization_barrier(v.astype(jnp.bfloat16)).astype(jnp.float32)

@jax.custom_vjp
def low_back(v):
    return v

def low_keep(v):
    return (low(v), None)

def low_pass(kept, grad):
    return (grad,)

def back_keep(v):
    return (v, None)

def back_low(kept, grad):
    return (low(grad),)
low.defvjp(low_keep, low_pass)
low_back.defvjp(back_keep, back_low)
BETA_ONE = 0.9
BETA_TWO = 0.999
LEARN_RATE = 0.05
DECAY_RATE = 0.01
ADAM_EPS = 1e-08
NORM_EPS = 1e-05
MASKED = -1e+30

def both_round(values):
    return low_back(low(values))

def layer_norm(values, gain, shift):
    centre = values - lax.optimization_barrier(jnp.mean(values, -1, keepdims=True))
    spread = lax.optimization_barrier(jnp.mean(centre * centre, -1, keepdims=True))
    return centre * lax.rsqrt(spread + NORM_EPS) * gain + shift

def unpack(flat):
    shapes = ((D, 3 * D), (D, D), (D, D), (D, 2 * D), (D, D), (D, FF), (FF, D), (NV, D))
    sliced = flat.reshape(flat.shape[:-1] + (N_FRAMES, P_SIZE // N_FRAMES))
    pieces = []
    offset = 0
    for rows_in, cols_out in shapes:
        width = rows_in * cols_out // N_FRAMES
        pieces.append(sliced[..., offset:offset + width].reshape(flat.shape[:-1] + (rows_in, cols_out)))
        offset += width
    return pieces

def project(inputs, weight):
    return jnp.einsum('brd,bde->bre', inputs, weight, precision=lax.Precision.HIGHEST)

def split_heads(tensor):
    return tensor.reshape(tensor.shape[:-1] + (HEADS, HEAD_DIM))

def merge_heads(tensor):
    return tensor.reshape(tensor.shape[:-2] + (D,))

def attention(queries, keys_in, values_in, allowed):
    scale = 1.0 / math.sqrt(HEAD_DIM)
    scores = low_back(jnp.einsum('bqhe,bkhe->bhqk', queries, keys_in, precision=lax.Precision.HIGHEST) * scale)
    scores = jnp.where(allowed[:, None], scores, MASKED)
    row_max = lax.optimization_barrier(jnp.max(scores, -1, keepdims=True))
    raised = jnp.exp(scores - row_max)
    weights = low(raised / lax.optimization_barrier(jnp.sum(raised, -1, keepdims=True)))
    return both_round(jnp.einsum('bhqk,bkhe->bqhe', weights, values_in, precision=lax.Precision.HIGHEST))

def layer_block(frames, segments, mats, vectors):
    w_qkv, w_self, w_query, w_keyval, w_cross, w_up, w_down = mats

    def column(index):
        return vectors[:, index][:, None, :]
    self_mask = segments[:, :, None] == segments[:, None, :]
    cross_mask = segments[:, :, None] == segments[::-1][:, None, :]
    normed = low(layer_norm(frames, column(0), column(1)))
    joined = both_round(project(normed, w_qkv))
    attended = merge_heads(attention(split_heads(joined[..., :D]), split_heads(joined[..., D:2 * D]), split_heads(joined[..., 2 * D:]), self_mask))
    hidden = frames + column(8) * low_back(project(attended, w_self))
    cross_q = both_round(project(low(layer_norm(hidden, column(2), column(3))), w_query))
    keyval = both_round(project(low(layer_norm(hidden, column(4), column(5))), w_keyval))
    far_kv = keyval[::-1]
    mixed = merge_heads(attention(split_heads(cross_q), split_heads(far_kv[..., :D]), split_heads(far_kv[..., D:]), cross_mask))
    second_h = hidden + column(9) * low_back(project(mixed, w_cross))
    ffn_in = low(layer_norm(second_h, column(6), column(7)))
    pre_act = low_back(project(ffn_in, w_up))
    activated = low(jax.nn.gelu(pre_act, approximate=False))
    return second_h + column(10) * low_back(project(activated, w_down))

def forward(frames, flat_params, segments):
    used = unpack(low(flat_params))
    mats = used[:7]
    vectors = used[7]
    blocks = TOKENS // TOK_DEV
    frame_blocks = frames.reshape(2, blocks, TOK_DEV, D).transpose(1, 0, 2, 3)
    seg_blocks = segments.reshape(2, blocks, TOK_DEV).transpose(1, 0, 2)
    step_fn = jax.checkpoint(lambda block_pair: layer_block(block_pair[0], block_pair[1], mats, vectors))
    outputs = lax.map(step_fn, (frame_blocks, seg_blocks))
    return outputs.transpose(1, 0, 2, 3).reshape(2, TOKENS, D)

def reference(frames_in, seg_ids, cotangent, params, first_moment, second_moment):
    frames = frames_in.astype(jnp.float32)
    output, pullback = jax.vjp(lambda values, weights: forward(values, weights, seg_ids), frames, params)
    input_grad, raw_grad = pullback(cotangent.astype(jnp.float32))
    grad_norm = jnp.sqrt(jnp.sum(raw_grad * raw_grad))
    threshold = 0.01 * math.sqrt(2.0 * P_SIZE * TOKENS)
    clipped = raw_grad * jnp.minimum(1.0, threshold / grad_norm)
    slice_len = P_SIZE // N_FRAMES
    vec_width = NV * D // N_FRAMES
    vector_grad = clipped.reshape(2, N_FRAMES, slice_len)[:, :, slice_len - vec_width:].reshape(2, NV * D)
    first_new = BETA_ONE * first_moment + (1.0 - BETA_ONE) * clipped
    second_new = BETA_TWO * second_moment + (1.0 - BETA_TWO) * clipped * clipped
    mean_hat = first_new / (1.0 - BETA_ONE ** STEP)
    square_hat = second_new / (1.0 - BETA_TWO ** STEP)
    new_params = params - LEARN_RATE * (mean_hat / (jnp.sqrt(square_hat) + ADAM_EPS) + DECAY_RATE * params)
    return (output.astype(jnp.bfloat16), input_grad, clipped, vector_grad, grad_norm, first_new, second_new, new_params)
```

```python
from functools import partial
import math

import jax
import jax.numpy as jnp
from jax import lax
from jax.experimental import pallas as pl
from jax.experimental.pallas import tpu as pltpu
from jax.sharding import PartitionSpec as P

HEADS = 8
HEAD_DIM = 48
D = 384
FF = 1536
NV = 11
STEP = 5


BETA_ONE = 0.9
BETA_TWO = 0.999
LEARN_RATE = 0.05
DECAY_RATE = 0.01
ADAM_EPS = 1e-08
NORM_EPS = 1e-05
MASKED = -1e30


def from_partner(array, axis, apart):
    return lax.ppermute(array, axis, [(i, i ^ 1 << apart) for i in range(lax.axis_size(axis))])


def layer_norm(values, gain, shift):
    centre = values - jnp.mean(values, -1, keepdims=True)
    spread = jnp.mean(centre * centre, -1, keepdims=True)
    return centre * lax.rsqrt(spread + NORM_EPS) * gain + shift


def unpack(flat, count):
    shapes = ((D, 3 * D), (D, D), (D, D), (D, 2 * D), (D, D), (D, FF), (FF, D), (NV, D))
    sliced = flat.reshape(count, flat.shape[0] // count)
    pieces = []
    offset = 0
    for rows_in, cols_out in shapes:
        width = rows_in * cols_out // count
        pieces.append(sliced[:, offset : offset + width].reshape(rows_in, cols_out))
        offset += width
    return pieces


def split_heads(tensor):
    return tensor.reshape(tensor.shape[0], HEADS, HEAD_DIM)


def matmul(left, right):
    return jnp.dot(left, right, preferred_element_type=jnp.float32)


def weight_grad(inputs, grads):
    return jnp.einsum("ri,rj->ij", inputs, grads, preferred_element_type=jnp.float32)


def back_input(grads, weight):
    return jnp.einsum("rj,ij->ri", grads, weight, preferred_element_type=jnp.float32)


def masked_scores(queries, keys_in, allowed, scale):
    scores = (
        jnp.einsum("qhe,khe->hqk", queries, keys_in, preferred_element_type=jnp.float32) * scale
    )
    return jnp.where(allowed[None], scores, MASKED)


def attend(queries, keys_in, values_in, allowed, scale):
    scores = masked_scores(queries, keys_in, allowed, scale)
    row_max = jnp.max(scores, -1, keepdims=True)
    raised = jnp.exp(scores - row_max)
    row_sum = jnp.sum(raised, -1, keepdims=True)
    weights = (raised / row_sum).astype(jnp.bfloat16)
    output = jnp.einsum("hqk,khe->qhe", weights, values_in, preferred_element_type=jnp.float32)
    return (output, row_max + jnp.log(row_sum))


def attend_back(queries, keys_in, values_in, allowed, scale, log_sum, grad_out):
    probs = jnp.exp(masked_scores(queries, keys_in, allowed, scale) - log_sum)
    grad_probs = jnp.einsum("qhe,khe->hqk", grad_out, values_in, preferred_element_type=jnp.float32)
    grad_values = jnp.einsum(
        "hqk,qhe->khe", probs.astype(jnp.bfloat16), grad_out, preferred_element_type=jnp.float32
    )
    centred = grad_probs - jnp.sum(probs * grad_probs, -1, keepdims=True)
    grad_scores = (probs * centred).astype(jnp.bfloat16)
    grad_queries = (
        jnp.einsum("hqk,khe->qhe", grad_scores, keys_in, preferred_element_type=jnp.float32) * scale
    )
    grad_keys = (
        jnp.einsum("hqk,qhe->khe", grad_scores, queries, preferred_element_type=jnp.float32) * scale
    )
    return (
        grad_queries.astype(jnp.bfloat16),
        grad_keys.astype(jnp.bfloat16),
        grad_values.astype(jnp.bfloat16),
    )


def on_device(frames_in, seg_ids, cotangent, params, first_moment, second_moment):
    frames = frames_in[0].astype(jnp.float32)
    rows = frames.shape[0]
    count = lax.axis_size("frames")
    side = lax.axis_index("branch")
    own_seg = jnp.where(side == 0, seg_ids[0], seg_ids[1])
    far_seg = jnp.where(side == 0, seg_ids[1], seg_ids[0])
    self_mask = own_seg[:, None] == own_seg[None, :]
    cross_mask = own_seg[:, None] == far_seg[None, :]
    scale = 1.0 / math.sqrt(HEAD_DIM)
    shard16 = params.astype(jnp.bfloat16)
    whole = lax.all_gather(shard16, "frames", axis=1, tiled=True)[0]
    w_qkv, w_self, w_query, w_keyval, w_cross, w_up, w_down, vec16 = unpack(whole, count)
    vectors = vec16.astype(jnp.float32)
    normed, norm1_back = jax.vjp(layer_norm, frames, vectors[0], vectors[1])
    normed16 = normed.astype(jnp.bfloat16)
    joined16 = matmul(normed16, w_qkv).astype(jnp.bfloat16)
    query16 = split_heads(joined16[:, :D])
    key16 = split_heads(joined16[:, D : 2 * D])
    value16 = split_heads(joined16[:, 2 * D :])
    attended, self_lse = attend(query16, key16, value16, self_mask, scale)
    attended16 = attended.reshape(rows, D).astype(jnp.bfloat16)
    self_out = matmul(attended16, w_self)
    hidden = frames + vectors[8] * self_out
    cross_in, norm2_back = jax.vjp(layer_norm, hidden, vectors[2], vectors[3])
    cross_in16 = cross_in.astype(jnp.bfloat16)
    cross_q16 = matmul(cross_in16, w_query).astype(jnp.bfloat16)
    source, norm3_back = jax.vjp(layer_norm, hidden, vectors[4], vectors[5])
    source16 = source.astype(jnp.bfloat16)
    keyval16 = matmul(source16, w_keyval).astype(jnp.bfloat16)
    far_kv = from_partner(keyval16, "branch", 0)
    far_keys = split_heads(far_kv[:, :D])
    far_values = split_heads(far_kv[:, D:])
    cross_heads = split_heads(cross_q16)
    mixed, cross_lse = attend(cross_heads, far_keys, far_values, cross_mask, scale)
    mixed16 = mixed.reshape(rows, D).astype(jnp.bfloat16)
    cross_out = matmul(mixed16, w_cross)
    second_h = hidden + vectors[9] * cross_out
    ffn_in, norm4_back = jax.vjp(layer_norm, second_h, vectors[6], vectors[7])
    ffn_in16 = ffn_in.astype(jnp.bfloat16)
    pre_act = matmul(ffn_in16, w_up)
    activated, gelu_back = jax.vjp(partial(jax.nn.gelu, approximate=False), pre_act)
    activated16 = activated.astype(jnp.bfloat16)
    ffn_out = matmul(activated16, w_down)
    result = second_h + vectors[10] * ffn_out
    grad_out = cotangent[0].astype(jnp.float32)
    grad_ls3 = jnp.sum(grad_out * ffn_out, 0)
    grad_ffn16 = (grad_out * vectors[10]).astype(jnp.bfloat16)
    grad_down = weight_grad(activated16, grad_ffn16)
    grad_act = back_input(grad_ffn16, w_down)
    grad_pre16 = gelu_back(grad_act)[0].astype(jnp.bfloat16)
    grad_up = weight_grad(ffn_in16, grad_pre16)
    grad_h2_ln, grad_g4, grad_c4 = norm4_back(back_input(grad_pre16, w_up))
    grad_h2 = grad_out + grad_h2_ln
    grad_ls2 = jnp.sum(grad_h2 * cross_out, 0)
    grad_cross16 = (grad_h2 * vectors[9]).astype(jnp.bfloat16)
    grad_wcross = weight_grad(mixed16, grad_cross16)
    grad_mixed16 = back_input(grad_cross16, w_cross).astype(jnp.bfloat16)
    grad_cq16, grad_far_keys, grad_far_values = attend_back(
        cross_heads, far_keys, far_values, cross_mask, scale, cross_lse, split_heads(grad_mixed16)
    )
    returned = jnp.concatenate(
        [grad_far_keys.reshape(rows, D), grad_far_values.reshape(rows, D)], 1
    )
    grad_keyval16 = from_partner(returned, "branch", 0)
    grad_wkeyval = weight_grad(source16, grad_keyval16)
    grad_h_kv, grad_g3, grad_c3 = norm3_back(back_input(grad_keyval16, w_keyval))
    grad_cq_flat = grad_cq16.reshape(rows, D)
    grad_wquery = weight_grad(cross_in16, grad_cq_flat)
    grad_h_q, grad_g2, grad_c2 = norm2_back(back_input(grad_cq_flat, w_query))
    grad_hidden = grad_h2 + grad_h_q + grad_h_kv
    grad_ls1 = jnp.sum(grad_hidden * self_out, 0)
    grad_self16 = (grad_hidden * vectors[8]).astype(jnp.bfloat16)
    grad_wself = weight_grad(attended16, grad_self16)
    grad_att16 = back_input(grad_self16, w_self).astype(jnp.bfloat16)
    grad_q16, grad_k16, grad_v16 = attend_back(
        query16, key16, value16, self_mask, scale, self_lse, split_heads(grad_att16)
    )
    grad_joined16 = jnp.concatenate(
        [grad_q16.reshape(rows, D), grad_k16.reshape(rows, D), grad_v16.reshape(rows, D)], 1
    )
    grad_wqkv = weight_grad(normed16, grad_joined16)
    grad_x_ln, grad_g1, grad_c1 = norm1_back(back_input(grad_joined16, w_qkv))
    input_grad = grad_hidden + grad_x_ln
    grad_vectors = jnp.stack(
        [
            grad_g1,
            grad_c1,
            grad_g2,
            grad_c2,
            grad_g3,
            grad_c3,
            grad_g4,
            grad_c4,
            grad_ls1,
            grad_ls2,
            grad_ls3,
        ]
    )
    pieces = [
        grad_wqkv,
        grad_wself,
        grad_wquery,
        grad_wkeyval,
        grad_wcross,
        grad_up,
        grad_down,
        grad_vectors,
    ]
    flat_grad = jnp.concatenate([piece.reshape(count, -1) for piece in pieces], 1).reshape(1, -1)
    reduced = lax.psum_scatter(flat_grad, "frames", scatter_dimension=1, tiled=True)
    local_square = jnp.sum(reduced * reduced)
    square_sum = lax.psum(local_square, ("branch", "frames"))
    grad_norm = jnp.sqrt(square_sum)
    total_params = params.shape[1] * count
    total_rows = rows * count
    threshold = 0.01 * math.sqrt(2.0 * total_params * total_rows)
    clipped = reduced * jnp.minimum(1.0, threshold / grad_norm)
    vec_width = NV * D // count
    vector_grad = clipped[:, clipped.shape[1] - vec_width :]
    first_new = BETA_ONE * first_moment + (1.0 - BETA_ONE) * clipped
    second_new = BETA_TWO * second_moment + (1.0 - BETA_TWO) * clipped * clipped
    mean_hat = first_new / (1.0 - BETA_ONE**STEP)
    square_hat = second_new / (1.0 - BETA_TWO**STEP)
    new_params = params - LEARN_RATE * (
        mean_hat / (jnp.sqrt(square_hat) + ADAM_EPS) + DECAY_RATE * params
    )
    return (
        result.astype(jnp.bfloat16)[None],
        input_grad[None],
        clipped,
        vector_grad,
        grad_norm,
        first_new,
        second_new,
        new_params,
    )


MESH = pl.DeviceIdType.MESH
ROWS = 1168
PIECES = ((864, 304), (576, 288), (288, 288), (0, 288))
BF = jnp.bfloat16
F32 = jnp.float32
C2 = math.log2(math.e) / math.sqrt(HEAD_DIM)


def remote(src, dst, send, recv, **device):
    return pltpu.make_async_remote_copy(
        src_ref=src, dst_ref=dst, send_sem=send, recv_sem=recv, device_id=device, device_id_type=MESH
    )


def place():
    j = lax.axis_index("frames")
    return j // 4, j % 4


def greet(cores):
    z, p = place()
    b = lax.axis_index("branch")
    bar = pltpu.get_barrier_semaphore()
    n = 0
    for k in (1, 2, 3):
        pl.semaphore_signal(bar, inc=1, device_id={"frames": (z + k) % 4 * 4 + p}, device_id_type=MESH)
        pl.semaphore_signal(bar, inc=1, device_id={"frames": z * 4 + (p + k) % 4}, device_id_type=MESH)
        n += 2
    if cores:
        for k in range(4):
            pl.semaphore_signal(
                bar, inc=1, device_id={"branch": 1 - b, "frames": z * 4 + (p + k) % 4}, device_id_type=MESH
            )
            n += 1
    pl.semaphore_wait(bar, n)


def gather_kernel(pieces, wire, out, ss1, rs1, ss2, rs2, lsem):
    z, p = place()
    own = pltpu.make_async_copy(wire, out.at[z, p], lsem)
    own.start()
    greet(False)
    c1 = {}
    c2 = {}

    def first(i):
        a, n = pieces[i]
        for k in (1, 2, 3):
            c1[i, k] = remote(
                wire.at[pl.ds(a, n)], out.at[z, p, pl.ds(a, n)], ss1.at[i, k - 1], rs1.at[i, k - 1],
                frames=(z + k) % 4 * 4 + p,
            )
            c1[i, k].start()

    def second(i):
        a, n = pieces[i]
        for k in (1, 2, 3):
            c1[i, k].wait_recv()
        for k in (1, 2, 3):
            part = out.at[:, p, pl.ds(a, n)]
            c2[i, k] = remote(part, part, ss2.at[i, k - 1], rs2.at[i, k - 1], frames=z * 4 + (p + k) % 4)
            c2[i, k].start()

    first(0)
    own.wait()
    for i in range(len(pieces)):
        second(i)
        if i + 1 < len(pieces):
            first(i + 1)
    for i in range(len(pieces)):
        for k in (1, 2, 3):
            c2[i, k].wait_recv()
    for c in list(c1.values()) + list(c2.values()):
        c.wait_send()


def gather(wire):
    n = len(PIECES)
    dma = pltpu.SemaphoreType.DMA
    whole = pl.BlockSpec(memory_space=pltpu.VMEM)
    return pl.pallas_call(
        partial(gather_kernel, PIECES),
        out_shape=jax.ShapeDtypeStruct((4, 4, ROWS, 128), BF),
        in_specs=[whole],
        out_specs=whole,
        scratch_shapes=[dma((n, 3)), dma((n, 3)), dma((n, 3)), dma((n, 3)), dma(())],
        compiler_params=pltpu.CompilerParams(collective_id=0, has_side_effects=True),
        name="gather",
    )(wire)


def reduce_kernel(pieces, g, out, norm, r1, r2, s2, nb, nb2, ss1, rs1, ss2, rs2, ns1, nr1, ns2, nr2):
    z, p = place()
    b = lax.axis_index("branch")
    greet(True)
    c1 = {}
    c2 = {}
    cn = []

    def first(i):
        a, n = pieces[i]
        for k in (1, 2, 3):
            c1[i, k] = remote(
                g.at[:, (p + k) % 4, pl.ds(a, n)], r1.at[k - 1, :, pl.ds(a, n)], ss1.at[i, k - 1], rs1.at[i, k - 1],
                frames=z * 4 + (p + k) % 4,
            )
            c1[i, k].start()

    def second(i):
        a, n = pieces[i]
        for k in (1, 2, 3):
            c1[i, k].wait_recv()
        for k in (1, 2, 3, 0):
            far = (z + k) % 4
            total = g[far, p, pl.ds(a, n), :].astype(F32)
            for q in range(3):
                total = total + r1[q, far, pl.ds(a, n), :].astype(F32)
            if k:
                s2[k - 1, pl.ds(a, n), :] = total.astype(BF)
                part = pl.ds(a, n)
                c2[i, k] = remote(
                    s2.at[k - 1, part], r2.at[k - 1, part], ss2.at[i, k - 1], rs2.at[i, k - 1], frames=far * 4 + p
                )
                c2[i, k].start()
            else:
                out[pl.ds(a, n), :] = total

    first(0)
    for i in range(len(pieces)):
        if i + 1 < len(pieces):
            first(i + 1)
        second(i)
    square = jnp.zeros((8, 128), F32)
    for i, (a, n) in enumerate(pieces):
        for k in (1, 2, 3):
            c2[i, k].wait_recv()
        total = out[pl.ds(a, n), :]
        for k in range(3):
            total = total + r2[k, pl.ds(a, n), :].astype(F32)
        out[pl.ds(a, n), :] = total
        square = square + jnp.sum((total * total).reshape(n // 8, 8, 128), 0)
    me = 2 * p + b
    nb[pl.ds(me, 1)] = square[None]
    for k in range(4):
        for c in (0, 1):
            if k or c:
                i = 2 * k + c
                cn.append(
                    remote(
                        nb.at[me], nb.at[me], ns1.at[i - 1], nr1.at[i - 1],
                        frames=z * 4 + (p + k) % 4, branch=(b + c) % 2,
                    )
                )
                cn[-1].start()
    for c in cn:
        c.wait_recv()
    square = jnp.sum(nb[...], 0)
    nb2[pl.ds(z, 1)] = square[None]
    cz = []
    for k in (1, 2, 3):
        cz.append(remote(nb2.at[z], nb2.at[z], ns2.at[k - 1], nr2.at[k - 1], frames=(z + k) % 4 * 4 + p))
        cz[-1].start()
    for c in cz:
        c.wait_recv()
    norm[...] = jnp.sum(nb2[...], 0)
    for c in list(c1.values()) + list(c2.values()) + cn + cz:
        c.wait_send()


def reduce(wire):
    n = len(PIECES)
    dma = pltpu.SemaphoreType.DMA
    vmem = pltpu.VMEM
    whole = pl.BlockSpec(memory_space=vmem)
    return pl.pallas_call(
        partial(reduce_kernel, PIECES),
        out_shape=(jax.ShapeDtypeStruct((ROWS, 128), F32), jax.ShapeDtypeStruct((8, 128), F32)),
        in_specs=[whole],
        out_specs=(whole, whole),
        scratch_shapes=[
            vmem((3, 4, ROWS, 128), BF), vmem((3, ROWS, 128), BF), vmem((3, ROWS, 128), BF),
            vmem((8, 8, 128), F32), vmem((4, 8, 128), F32),
            dma((n, 3)), dma((n, 3)), dma((n, 3)), dma((n, 3)), dma((7,)), dma((7,)), dma((3,)), dma((3,)),
        ],
        compiler_params=pltpu.CompilerParams(collective_id=1, has_side_effects=True),
        name="reduce",
    )(wire)


def to_wire(flat):
    left = flat[: 24 * 4608]
    mats = []
    at = 0
    for cols in (3 * D, D, D, 2 * D, D, FF):
        mats.append(left[at : at + 24 * cols].reshape(24, cols // 128, 128))
        at += 24 * cols
    left = jnp.concatenate(mats, 1).transpose(1, 0, 2).reshape(864, 128)
    down = flat[24 * 4608 :].reshape(96, 3, 128).transpose(1, 0, 2).reshape(288, 128)
    return jnp.concatenate([left, down], 0)


def from_wire(wire):
    left = wire[:864].reshape(36, 24, 128).transpose(1, 0, 2)
    mats = []
    at = 0
    for cols in (3 * D, D, D, 2 * D, D, FF):
        mats.append(left[:, at // 128 : (at + cols) // 128].reshape(-1))
        at += cols
    down = wire[864:1152].reshape(3, 96, 128).transpose(1, 0, 2).reshape(-1)
    return jnp.concatenate(mats + [down])


def mm(a, b):
    return lax.dot_general(a, b, (((1,), (0,)), ((), ())), preferred_element_type=F32)


def mm_nt(a, b):
    return lax.dot_general(a, b, (((1,), (1,)), ((), ())), preferred_element_type=F32)


def att_kernel(tile, q_ref, k_ref, v_ref, hot_ref, mask_ref, o_ref, e_ref, inv_ref):
    n = k_ref.shape[1]
    k32 = k_ref[...].astype(F32) * C2
    high = k32.astype(BF)
    low = (k32 - high.astype(F32)).astype(BF)
    keys = jnp.concatenate([high, low, hot_ref[...]], 0).T
    values = jnp.concatenate([v_ref[...], jnp.ones((16, n), BF)], 0)
    for t in range(n // tile):
        at = slice(t * tile, (t + 1) * tile)
        q = q_ref[:, at]
        scores = mm(keys, jnp.concatenate([q, q, mask_ref[:, at]], 0))
        top = jnp.max(scores, 0, keepdims=True)
        e = jnp.exp2(scores - top).astype(BF)
        e_ref[0, :, at] = e
        o = mm(values, e)
        inv = 1.0 / o[48:49]
        o_ref[:, at] = o[:48] * inv
        inv_ref[0, :, at] = jnp.broadcast_to(inv, (8, tile))


def att(q, qo, kv, ko, vo, hot, mask):
    n = q.shape[1]
    head = lambda o: pl.BlockSpec((48, n), lambda h: (h + o, 0))
    fixed = pl.BlockSpec((32, n), lambda h: (0, 0))
    return pl.pallas_call(
        partial(att_kernel, n),
        grid=(HEADS,),
        in_specs=[head(qo), head(ko), head(vo), fixed, fixed],
        out_specs=[head(0), pl.BlockSpec((1, n, n), lambda h: (h, 0, 0)), pl.BlockSpec((1, 8, n), lambda h: (h, 0, 0))],
        out_shape=[
            jax.ShapeDtypeStruct((D, n), F32), jax.ShapeDtypeStruct((HEADS, n, n), BF),
            jax.ShapeDtypeStruct((HEADS, 8, n), F32),
        ],
        name="att",
    )(q, kv, kv, hot, mask)


def att_back_kernel(tile, q_ref, k_ref, v_ref, o_ref, do_ref, e_ref, inv_ref, dq_ref, dk_ref, dv_ref):
    n = k_ref.shape[1]
    scale = 1.0 / math.sqrt(HEAD_DIM)
    v = v_ref[...]
    values = jnp.concatenate([v, v, jnp.ones((32, n), BF)], 0).T
    k = k_ref[...]
    inv = inv_ref[0, 0:1, :]
    do = do_ref[...].astype(F32)
    minus = -jnp.sum(do * o_ref[...], 0, keepdims=True) * inv
    do = do * inv
    high = do.astype(BF)
    low = (do - high.astype(F32)).astype(BF)
    minus_high = minus.astype(BF).astype(F32)
    row = lax.broadcasted_iota(jnp.int32, (32, n), 0)
    extra = jnp.where(row == 0, minus_high, jnp.where(row == 1, minus - minus_high, 0.0)).astype(BF)
    grads = jnp.concatenate([high, low, extra], 0)
    for t in range(n // tile):
        at = slice(t * tile, (t + 1) * tile)
        dp = mm(values, grads[:, at])
        e = e_ref[0, :, at]
        ds = (e.astype(F32) * dp).astype(BF)
        a = mm_nt(q_ref[:, at], ds)
        b = mm_nt(high[:, at], e)
        if t == 0:
            dk, dv = a, b
        else:
            dk, dv = dk + a, dv + b
        dq_ref[:, at] = (mm(k, ds) * scale).astype(BF)
    dk_ref[...] = (dk * scale).astype(BF)
    dv_ref[...] = dv.astype(BF)


def att_back(q, qo, kv, ko, vo, o, do, e, inv):
    n = q.shape[1]
    head = lambda o: pl.BlockSpec((48, n), lambda h: (h + o, 0))
    return pl.pallas_call(
        partial(att_back_kernel, n // 2),
        grid=(HEADS,),
        in_specs=[
            head(qo), head(ko), head(vo), head(0), head(0), pl.BlockSpec((1, n, n), lambda h: (h, 0, 0)),
            pl.BlockSpec((1, 8, n), lambda h: (h, 0, 0)),
        ],
        out_specs=[head(0)] * 3,
        out_shape=[jax.ShapeDtypeStruct((D, n), BF)] * 3,
        name="att_back",
    )(q, kv, kv, o, do, e, inv)


def fast_device(frames_in, seg_ids, cotangent, params, first_moment, second_moment):
    frames = frames_in[0].astype(F32)
    count = lax.axis_size("frames")
    side = lax.axis_index("branch")
    own_seg = jnp.where(side == 0, seg_ids[0], seg_ids[1])
    far_seg = jnp.where(side == 0, seg_ids[1], seg_ids[0])
    number = lax.broadcasted_iota(jnp.int32, (32, 1), 0) + 4 * lax.axis_index("frames")
    own_hot = number == own_seg[None, :]
    far_hot = (number == far_seg[None, :]).astype(BF)
    rest = lax.broadcasted_iota(jnp.int32, (32, 1), 0) < 4
    mask = jnp.where(rest & ~own_hot, MASKED, 0.0).astype(BF)
    own_hot = own_hot.astype(BF)
    shard16 = params[0].astype(BF)
    wire = jnp.concatenate([to_wire(shard16[:147456]), jnp.pad(shard16[147456:], (0, 2048 - 264)).reshape(16, 128)], 0)
    got = gather(wire).reshape(16, ROWS, 128)
    w6 = got[:, :864].reshape(16, 36, 24, 128).transpose(0, 2, 1, 3).reshape(384, 4608)
    w_qkv, w_self, w_query, w_keyval, w_cross, w_up = (
        w6[:, :1152], w6[:, 1152:1536], w6[:, 1536:1920], w6[:, 1920:2688], w6[:, 2688:3072], w6[:, 3072:],
    )
    w_down = got[:, 864:1152].reshape(16, 3, 96, 128).transpose(0, 2, 1, 3).reshape(1536, 384)
    vectors = got[:, 1152:1155].reshape(16, 384)[:, :264].reshape(NV, D).astype(F32)
    normed, norm1_back = jax.vjp(layer_norm, frames, vectors[0], vectors[1])
    normed16 = normed.astype(BF)
    qkv = jnp.einsum("io,ri->or", w_qkv, normed16, preferred_element_type=F32).astype(BF)
    o1, e1, inv1 = att(qkv, 0, qkv, 8, 16, own_hot, mask)
    attended16 = o1.astype(BF)
    self_out = jnp.einsum("ir,io->ro", attended16, w_self, preferred_element_type=F32)
    hidden = frames + vectors[8] * self_out
    cross_in, norm2_back = jax.vjp(layer_norm, hidden, vectors[2], vectors[3])
    cross_in16 = cross_in.astype(BF)
    cq = jnp.einsum("io,ri->or", w_query, cross_in16, preferred_element_type=F32).astype(BF)
    source, norm3_back = jax.vjp(layer_norm, hidden, vectors[4], vectors[5])
    source16 = source.astype(BF)
    kv = jnp.einsum("io,ri->or", w_keyval, source16, preferred_element_type=F32).astype(BF)
    kv = from_partner(kv, "branch", 0)
    o2, e2, inv2 = att(cq, 0, kv, 0, 8, far_hot, mask)
    mixed16 = o2.astype(BF)
    cross_out = jnp.einsum("ir,io->ro", mixed16, w_cross, preferred_element_type=F32)
    second_h = hidden + vectors[9] * cross_out
    ffn_in, norm4_back = jax.vjp(layer_norm, second_h, vectors[6], vectors[7])
    ffn_in16 = ffn_in.astype(BF)
    pre_act = matmul(ffn_in16, w_up)
    activated, gelu_back = jax.vjp(partial(jax.nn.gelu, approximate=False), pre_act)
    activated16 = activated.astype(BF)
    ffn_out = matmul(activated16, w_down)
    result = second_h + vectors[10] * ffn_out
    grad_out = cotangent[0].astype(F32)
    grad_ls3 = jnp.sum(grad_out * ffn_out, 0)
    grad_ffn16 = (grad_out * vectors[10]).astype(BF)
    grad_down = weight_grad(activated16, grad_ffn16)
    grad_act = back_input(grad_ffn16, w_down)
    grad_pre16 = gelu_back(grad_act)[0].astype(BF)
    grad_up = weight_grad(ffn_in16, grad_pre16)
    grad_h2_ln, grad_g4, grad_c4 = norm4_back(back_input(grad_pre16, w_up))
    grad_h2 = grad_out + grad_h2_ln
    grad_ls2 = jnp.sum(grad_h2 * cross_out, 0)
    grad_cross16 = (grad_h2 * vectors[9]).astype(BF)
    grad_wcross = jnp.einsum("ir,ro->io", mixed16, grad_cross16, preferred_element_type=F32)
    do2 = jnp.einsum("io,ro->ir", w_cross, grad_cross16, preferred_element_type=F32).astype(BF)
    dq2, dk2, dv2 = att_back(cq, 0, kv, 0, 8, o2, do2, e2, inv2)
    dkv = from_partner(jnp.concatenate([dk2, dv2], 0), "branch", 0)
    grad_wkeyval = jnp.einsum("ri,or->io", source16, dkv, preferred_element_type=F32)
    grad_h_kv, grad_g3, grad_c3 = norm3_back(jnp.einsum("io,or->ri", w_keyval, dkv, preferred_element_type=F32))
    grad_wquery = jnp.einsum("ri,or->io", cross_in16, dq2, preferred_element_type=F32)
    grad_h_q, grad_g2, grad_c2 = norm2_back(jnp.einsum("io,or->ri", w_query, dq2, preferred_element_type=F32))
    grad_hidden = grad_h2 + grad_h_q + grad_h_kv
    grad_ls1 = jnp.sum(grad_hidden * self_out, 0)
    grad_self16 = (grad_hidden * vectors[8]).astype(BF)
    grad_wself = jnp.einsum("ir,ro->io", attended16, grad_self16, preferred_element_type=F32)
    do1 = jnp.einsum("io,ro->ir", w_self, grad_self16, preferred_element_type=F32).astype(BF)
    dqkv = jnp.concatenate(att_back(qkv, 0, qkv, 8, 16, o1, do1, e1, inv1), 0)
    grad_wqkv = jnp.einsum("ri,or->io", normed16, dqkv, preferred_element_type=F32)
    grad_x_ln, grad_g1, grad_c1 = norm1_back(jnp.einsum("io,or->ri", w_qkv, dqkv, preferred_element_type=F32))
    input_grad = grad_hidden + grad_x_ln
    grad_vectors = jnp.stack([
        grad_g1, grad_c1, grad_g2, grad_c2, grad_g3, grad_c3, grad_g4, grad_c4, grad_ls1, grad_ls2, grad_ls3,
    ])
    left = [
        m.astype(BF).reshape(16, 24, -1, 128).transpose(0, 2, 1, 3).reshape(16, -1, 128)
        for m in (grad_wqkv, grad_wself, grad_wquery, grad_wkeyval, grad_wcross, grad_up)
    ]
    down = grad_down.astype(BF).reshape(16, 96, 3, 128).transpose(0, 2, 1, 3).reshape(16, 288, 128)
    vecs = jnp.pad(grad_vectors.astype(BF).reshape(16, 264), ((0, 0), (0, 2048 - 264))).reshape(16, 16, 128)
    wire_grad = jnp.concatenate(left + [down, vecs], 1).reshape(4, 4, ROWS, 128)
    total, square = reduce(wire_grad)
    grad_norm = jnp.sqrt(jnp.sum(square))
    reduced = jnp.concatenate([from_wire(total), total[1152:].reshape(-1)[:264]])[None]
    total_params = params.shape[1] * count
    total_rows = frames.shape[0] * count
    threshold = 0.01 * math.sqrt(2.0 * total_params * total_rows)
    clipped = reduced * jnp.minimum(1.0, threshold / grad_norm)
    vector_grad = clipped[:, 147456:]
    first_new = BETA_ONE * first_moment + (1.0 - BETA_ONE) * clipped
    second_new = BETA_TWO * second_moment + (1.0 - BETA_TWO) * clipped * clipped
    mean_hat = first_new / (1.0 - BETA_ONE**STEP)
    square_hat = second_new / (1.0 - BETA_TWO**STEP)
    new_params = params - LEARN_RATE * (
        mean_hat / (jnp.sqrt(square_hat) + ADAM_EPS) + DECAY_RATE * params
    )
    return (
        result.astype(BF)[None], input_grad[None], clipped, vector_grad, grad_norm, first_new, second_new, new_params,
    )


def solution(mesh):
    placed = (
        P("branch", "frames", None),
        P(None, "frames"),
        P("branch", "frames", None),
        P("branch", "frames"),
        P("branch", "frames"),
        P("branch", "frames"),
    )
    return jax.shard_map(
        fast_device if mesh.shape["frames"] == 16 else on_device,
        mesh=mesh,
        in_specs=placed,
        out_specs=(
            P("branch", "frames", None),
            P("branch", "frames", None),
            P("branch", "frames"),
            P("branch", "frames"),
            P(),
            P("branch", "frames"),
            P("branch", "frames"),
            P("branch", "frames"),
        ),
        check_vma=False,
    )
```

```python
from functools import partial
import math

import jax
import jax.numpy as jnp
from jax import lax
from jax.experimental import pallas as pl
from jax.experimental.pallas import tpu as pltpu
from jax.sharding import PartitionSpec as P

HEADS = 8
HEAD_DIM = 48
D = 384
FF = 1536
NV = 11
STEP = 5


BETA_ONE = 0.9
BETA_TWO = 0.999
LEARN_RATE = 0.05
DECAY_RATE = 0.01
ADAM_EPS = 1e-08
NORM_EPS = 1e-05
MASKED = -1e30


def from_partner(array, axis, apart):
    return lax.ppermute(array, axis, [(i, i ^ 1 << apart) for i in range(lax.axis_size(axis))])


def layer_norm(values, gain, shift):
    centre = values - jnp.mean(values, -1, keepdims=True)
    spread = jnp.mean(centre * centre, -1, keepdims=True)
    return centre * lax.rsqrt(spread + NORM_EPS) * gain + shift


def unpack(flat, count):
    shapes = ((D, 3 * D), (D, D), (D, D), (D, 2 * D), (D, D), (D, FF), (FF, D), (NV, D))
    sliced = flat.reshape(count, flat.shape[0] // count)
    pieces = []
    offset = 0
    for rows_in, cols_out in shapes:
        width = rows_in * cols_out // count
        pieces.append(sliced[:, offset : offset + width].reshape(rows_in, cols_out))
        offset += width
    return pieces


def split_heads(tensor):
    return tensor.reshape(tensor.shape[0], HEADS, HEAD_DIM)


def matmul(left, right):
    return jnp.dot(left, right, preferred_element_type=jnp.float32)


def weight_grad(inputs, grads):
    return jnp.einsum("ri,rj->ij", inputs, grads, preferred_element_type=jnp.float32)


def back_input(grads, weight):
    return jnp.einsum("rj,ij->ri", grads, weight, preferred_element_type=jnp.float32)


def masked_scores(queries, keys_in, allowed, scale):
    scores = (
        jnp.einsum("qhe,khe->hqk", queries, keys_in, preferred_element_type=jnp.float32) * scale
    )
    return jnp.where(allowed[None], scores, MASKED)


def attend(queries, keys_in, values_in, allowed, scale):
    scores = masked_scores(queries, keys_in, allowed, scale)
    row_max = jnp.max(scores, -1, keepdims=True)
    raised = jnp.exp(scores - row_max)
    row_sum = jnp.sum(raised, -1, keepdims=True)
    weights = (raised / row_sum).astype(jnp.bfloat16)
    output = jnp.einsum("hqk,khe->qhe", weights, values_in, preferred_element_type=jnp.float32)
    return (output, row_max + jnp.log(row_sum))


def attend_back(queries, keys_in, values_in, allowed, scale, log_sum, grad_out):
    probs = jnp.exp(masked_scores(queries, keys_in, allowed, scale) - log_sum)
    grad_probs = jnp.einsum("qhe,khe->hqk", grad_out, values_in, preferred_element_type=jnp.float32)
    grad_values = jnp.einsum(
        "hqk,qhe->khe", probs.astype(jnp.bfloat16), grad_out, preferred_element_type=jnp.float32
    )
    centred = grad_probs - jnp.sum(probs * grad_probs, -1, keepdims=True)
    grad_scores = (probs * centred).astype(jnp.bfloat16)
    grad_queries = (
        jnp.einsum("hqk,khe->qhe", grad_scores, keys_in, preferred_element_type=jnp.float32) * scale
    )
    grad_keys = (
        jnp.einsum("hqk,qhe->khe", grad_scores, queries, preferred_element_type=jnp.float32) * scale
    )
    return (
        grad_queries.astype(jnp.bfloat16),
        grad_keys.astype(jnp.bfloat16),
        grad_values.astype(jnp.bfloat16),
    )


def on_device(frames_in, seg_ids, cotangent, params, first_moment, second_moment):
    frames = frames_in[0].astype(jnp.float32)
    rows = frames.shape[0]
    count = lax.axis_size("frames")
    side = lax.axis_index("branch")
    own_seg = jnp.where(side == 0, seg_ids[0], seg_ids[1])
    far_seg = jnp.where(side == 0, seg_ids[1], seg_ids[0])
    self_mask = own_seg[:, None] == own_seg[None, :]
    cross_mask = own_seg[:, None] == far_seg[None, :]
    scale = 1.0 / math.sqrt(HEAD_DIM)
    shard16 = params.astype(jnp.bfloat16)
    whole = lax.all_gather(shard16, "frames", axis=1, tiled=True)[0]
    w_qkv, w_self, w_query, w_keyval, w_cross, w_up, w_down, vec16 = unpack(whole, count)
    vectors = vec16.astype(jnp.float32)
    normed, norm1_back = jax.vjp(layer_norm, frames, vectors[0], vectors[1])
    normed16 = normed.astype(jnp.bfloat16)
    joined16 = matmul(normed16, w_qkv).astype(jnp.bfloat16)
    query16 = split_heads(joined16[:, :D])
    key16 = split_heads(joined16[:, D : 2 * D])
    value16 = split_heads(joined16[:, 2 * D :])
    attended, self_lse = attend(query16, key16, value16, self_mask, scale)
    attended16 = attended.reshape(rows, D).astype(jnp.bfloat16)
    self_out = matmul(attended16, w_self)
    hidden = frames + vectors[8] * self_out
    cross_in, norm2_back = jax.vjp(layer_norm, hidden, vectors[2], vectors[3])
    cross_in16 = cross_in.astype(jnp.bfloat16)
    cross_q16 = matmul(cross_in16, w_query).astype(jnp.bfloat16)
    source, norm3_back = jax.vjp(layer_norm, hidden, vectors[4], vectors[5])
    source16 = source.astype(jnp.bfloat16)
    keyval16 = matmul(source16, w_keyval).astype(jnp.bfloat16)
    far_kv = from_partner(keyval16, "branch", 0)
    far_keys = split_heads(far_kv[:, :D])
    far_values = split_heads(far_kv[:, D:])
    cross_heads = split_heads(cross_q16)
    mixed, cross_lse = attend(cross_heads, far_keys, far_values, cross_mask, scale)
    mixed16 = mixed.reshape(rows, D).astype(jnp.bfloat16)
    cross_out = matmul(mixed16, w_cross)
    second_h = hidden + vectors[9] * cross_out
    ffn_in, norm4_back = jax.vjp(layer_norm, second_h, vectors[6], vectors[7])
    ffn_in16 = ffn_in.astype(jnp.bfloat16)
    pre_act = matmul(ffn_in16, w_up)
    activated, gelu_back = jax.vjp(partial(jax.nn.gelu, approximate=False), pre_act)
    activated16 = activated.astype(jnp.bfloat16)
    ffn_out = matmul(activated16, w_down)
    result = second_h + vectors[10] * ffn_out
    grad_out = cotangent[0].astype(jnp.float32)
    grad_ls3 = jnp.sum(grad_out * ffn_out, 0)
    grad_ffn16 = (grad_out * vectors[10]).astype(jnp.bfloat16)
    grad_down = weight_grad(activated16, grad_ffn16)
    grad_act = back_input(grad_ffn16, w_down)
    grad_pre16 = gelu_back(grad_act)[0].astype(jnp.bfloat16)
    grad_up = weight_grad(ffn_in16, grad_pre16)
    grad_h2_ln, grad_g4, grad_c4 = norm4_back(back_input(grad_pre16, w_up))
    grad_h2 = grad_out + grad_h2_ln
    grad_ls2 = jnp.sum(grad_h2 * cross_out, 0)
    grad_cross16 = (grad_h2 * vectors[9]).astype(jnp.bfloat16)
    grad_wcross = weight_grad(mixed16, grad_cross16)
    grad_mixed16 = back_input(grad_cross16, w_cross).astype(jnp.bfloat16)
    grad_cq16, grad_far_keys, grad_far_values = attend_back(
        cross_heads, far_keys, far_values, cross_mask, scale, cross_lse, split_heads(grad_mixed16)
    )
    returned = jnp.concatenate(
        [grad_far_keys.reshape(rows, D), grad_far_values.reshape(rows, D)], 1
    )
    grad_keyval16 = from_partner(returned, "branch", 0)
    grad_wkeyval = weight_grad(source16, grad_keyval16)
    grad_h_kv, grad_g3, grad_c3 = norm3_back(back_input(grad_keyval16, w_keyval))
    grad_cq_flat = grad_cq16.reshape(rows, D)
    grad_wquery = weight_grad(cross_in16, grad_cq_flat)
    grad_h_q, grad_g2, grad_c2 = norm2_back(back_input(grad_cq_flat, w_query))
    grad_hidden = grad_h2 + grad_h_q + grad_h_kv
    grad_ls1 = jnp.sum(grad_hidden * self_out, 0)
    grad_self16 = (grad_hidden * vectors[8]).astype(jnp.bfloat16)
    grad_wself = weight_grad(attended16, grad_self16)
    grad_att16 = back_input(grad_self16, w_self).astype(jnp.bfloat16)
    grad_q16, grad_k16, grad_v16 = attend_back(
        query16, key16, value16, self_mask, scale, self_lse, split_heads(grad_att16)
    )
    grad_joined16 = jnp.concatenate(
        [grad_q16.reshape(rows, D), grad_k16.reshape(rows, D), grad_v16.reshape(rows, D)], 1
    )
    grad_wqkv = weight_grad(normed16, grad_joined16)
    grad_x_ln, grad_g1, grad_c1 = norm1_back(back_input(grad_joined16, w_qkv))
    input_grad = grad_hidden + grad_x_ln
    grad_vectors = jnp.stack(
        [
            grad_g1,
            grad_c1,
            grad_g2,
            grad_c2,
            grad_g3,
            grad_c3,
            grad_g4,
            grad_c4,
            grad_ls1,
            grad_ls2,
            grad_ls3,
        ]
    )
    pieces = [
        grad_wqkv,
        grad_wself,
        grad_wquery,
        grad_wkeyval,
        grad_wcross,
        grad_up,
        grad_down,
        grad_vectors,
    ]
    flat_grad = jnp.concatenate([piece.reshape(count, -1) for piece in pieces], 1).reshape(1, -1)
    reduced = lax.psum_scatter(flat_grad, "frames", scatter_dimension=1, tiled=True)
    local_square = jnp.sum(reduced * reduced)
    square_sum = lax.psum(local_square, ("branch", "frames"))
    grad_norm = jnp.sqrt(square_sum)
    total_params = params.shape[1] * count
    total_rows = rows * count
    threshold = 0.01 * math.sqrt(2.0 * total_params * total_rows)
    clipped = reduced * jnp.minimum(1.0, threshold / grad_norm)
    vec_width = NV * D // count
    vector_grad = clipped[:, clipped.shape[1] - vec_width :]
    first_new = BETA_ONE * first_moment + (1.0 - BETA_ONE) * clipped
    second_new = BETA_TWO * second_moment + (1.0 - BETA_TWO) * clipped * clipped
    mean_hat = first_new / (1.0 - BETA_ONE**STEP)
    square_hat = second_new / (1.0 - BETA_TWO**STEP)
    new_params = params - LEARN_RATE * (
        mean_hat / (jnp.sqrt(square_hat) + ADAM_EPS) + DECAY_RATE * params
    )
    return (
        result.astype(jnp.bfloat16)[None],
        input_grad[None],
        clipped,
        vector_grad,
        grad_norm,
        first_new,
        second_new,
        new_params,
    )


MESH = pl.DeviceIdType.MESH
BF = jnp.bfloat16
F32 = jnp.float32
C2 = math.log2(math.e) / math.sqrt(HEAD_DIM)
SCALE = 1.0 / math.sqrt(HEAD_DIM)
N = 1024
TILE = 256
LEAD = 16
DOWN = LEAD + 36 * 24
ROWS = DOWN + 288
FLAT = 1160
QKV, SELF, QUERY, KEYVAL, CROSS, UP = (0, 9), (216, 3), (288, 3), (360, 6), (504, 3), (576, 12)
OUT_ORDER = [(m, c) for m in (QKV, SELF, QUERY, KEYVAL, CROSS, UP) for c in range(m[1])]
BACK_ORDER = [e for s in range(3) for e in ((QKV, s), (QKV, 3 + s), (QKV, 6 + s), (SELF, s))] + OUT_ORDER[12:]
OUT_PIECES = ((0, 112), (112, 96), (208, 48), (256, 336), (592, 288), (880, 288))
BACK_PIECES = ((880, 288), (592, 288), (304, 288), (16, 96), (112, 96), (208, 96))


def remote(src, dst, send, recv, **device):
    return pltpu.make_async_remote_copy(
        src_ref=src, dst_ref=dst, send_sem=send, recv_sem=recv, device_id=device, device_id_type=MESH
    )


def mm(a, b):
    return lax.dot_general(a, b, (((1,), (0,)), ((), ())), preferred_element_type=F32)


def mm_nt(a, b):
    return lax.dot_general(a, b, (((1,), (1,)), ((), ())), preferred_element_type=F32)


def loop(start, stop, body):
    lax.fori_loop(start, stop, lambda i, _: (body(i), 0)[1], 0)


def rows_at(i, size):
    return pl.ds(pl.multiple_of(i * size, size), size)


def normalise(values):
    centre = values - jnp.mean(values, -1, keepdims=True)
    scale = lax.rsqrt(jnp.mean(centre * centre, -1, keepdims=True) + NORM_EPS)
    return centre * scale, scale


def normalise_back(unit, scale, grad):
    return scale * (grad - jnp.mean(grad, -1, keepdims=True) - unit * jnp.mean(grad * unit, -1, keepdims=True))


def att_head(q, k, v, hot, mask):
    n = k.shape[1]
    k32 = k.astype(F32) * C2
    high = k32.astype(BF)
    low = (k32 - high.astype(F32)).astype(BF)
    keys = jnp.concatenate([high, low, hot], 0).T
    values = jnp.concatenate([v, jnp.ones((16, n), BF)], 0)
    scores = mm(keys, jnp.concatenate([q, q, mask], 0))
    e = jnp.exp2(scores - jnp.max(scores, 0, keepdims=True)).astype(BF)
    o = mm(values, e)
    inv = 1.0 / o[48:49]
    return o[:48] * inv, e, inv


def att_back_head(q, k, v, o, do, e_ref, inv):
    n = k.shape[1]
    values = jnp.concatenate([v, v, jnp.ones((32, n), BF)], 0).T
    do = do.astype(F32)
    minus = -jnp.sum(do * o, 0, keepdims=True) * inv
    do = do * inv
    high = do.astype(BF)
    low = (do - high.astype(F32)).astype(BF)
    minus_high = minus.astype(BF).astype(F32)
    row = lax.broadcasted_iota(jnp.int32, (32, n), 0)
    extra = jnp.where(row == 0, minus_high, jnp.where(row == 1, minus - minus_high, 0.0)).astype(BF)
    grads = jnp.concatenate([high, low, extra], 0)
    dq = []
    half = n // 2
    for t in range(2):
        at = slice(t * half, (t + 1) * half)
        e = e_ref[:, at]
        ds = (e.astype(F32) * mm(values, grads[:, at])).astype(BF)
        a = mm_nt(q[:, at], ds)
        b = mm_nt(high[:, at], e)
        dk, dv = (a, b) if t == 0 else (dk + a, dv + b)
        dq.append(mm(k, ds))
    return (jnp.concatenate(dq, 1) * SCALE).astype(BF), (dk * SCALE).astype(BF), dv.astype(BF)


def step_kernel(*refs):
    it = iter(refs)
    (x, cot, pflat, seg) = (next(it) for _ in range(4))
    (out_hbm, gin_hbm, flat, norm, e1_hbm, e2_hbm) = (next(it) for _ in range(6))
    (net, r1, s2, r2, vec, vflat, vg, vr1, vr2, nb, nb2) = (next(it) for _ in range(11))
    (wqkv, wself, wquery, wkv, wcross, wup, wdown) = (next(it) for _ in range(7))
    (at, qkv, o1, h, n2t, n3t, cq, kv, far, o2) = (next(it) for _ in range(10))
    (n4t, zt, du, dffn, dh, dcr, dot, dkv, dkv_far) = (next(it) for _ in range(9))
    (ring, inv1, inv2, hot1, hot2, mask, stage16, stage32) = (next(it) for _ in range(8))
    (as1, ar1, as2, ar2, bs1, br1, bs2, br2, ks, kr, vs, vr, ns, nr, es, os, gs) = (next(it) for _ in range(17))
    j = lax.axis_index("frames")
    b = lax.axis_index("branch")
    z, p = j // 4, j % 4

    def zp(k):
        return (z + k) % 4 * 4 + p

    def pp(k):
        return z * 4 + (p + k) % 4

    bar = pltpu.get_barrier_semaphore()
    for k in (1, 2, 3):
        pl.semaphore_signal(bar, inc=1, device_id={"frames": zp(k)}, device_id_type=MESH)
        pl.semaphore_signal(bar, inc=1, device_id={"frames": pp(k)}, device_id_type=MESH)
    for k in range(4):
        pl.semaphore_signal(bar, inc=1, device_id={"branch": 1 - b, "frames": pp(k)}, device_id_type=MESH)

    net[z, p, pl.ds(0, 16), :] = jnp.concatenate([pflat[pl.ds(1152, 8), :], jnp.zeros((8, 128), F32)], 0).astype(BF)
    for m in range(18):
        pair = [pflat[pl.ds(mat[0] + c, 24, stride=mat[1]), :] for mat, c in OUT_ORDER[2 * m : 2 * m + 2]]
        net[z, p, pl.ds(LEAD + 48 * m, 48), :] = jnp.concatenate(pair, 0).astype(BF)
    for c in range(3):
        net[z, p, pl.ds(DOWN + 96 * c, 96), :] = pflat[pl.ds(864 + c, 96, stride=3), :].astype(BF)
    pl.semaphore_wait(bar, 10)

    a1, a2, b1, b2 = {}, {}, {}, {}

    def out_first(i):
        part = net.at[z, p, pl.ds(*OUT_PIECES[i])]
        for k in (1, 2, 3):
            a1[i, k] = remote(part, part, as1.at[i, k - 1], ar1.at[i, k - 1], frames=zp(k))
            a1[i, k].start()

    def out_second(i):
        for k in (1, 2, 3):
            a1[i, k].wait_recv()
        part = net.at[:, p, pl.ds(*OUT_PIECES[i])]
        for k in (1, 2, 3):
            a2[i, k] = remote(part, part, as2.at[i, k - 1], ar2.at[i, k - 1], frames=pp(k))
            a2[i, k].start()

    def out_ready(i):
        for k in (1, 2, 3):
            a2[i, k].wait_recv()

    def back_first(i):
        rows = pl.ds(*BACK_PIECES[i])
        for k in (1, 2, 3):
            b1[i, k] = remote(
                net.at[:, (p + k) % 4, rows], r1.at[k - 1, :, rows], bs1.at[i, k - 1], br1.at[i, k - 1], frames=pp(k)
            )
            b1[i, k].start()

    def back_second(i):
        rows = pl.ds(*BACK_PIECES[i])
        for k in (1, 2, 3):
            b1[i, k].wait_recv()
        for k in (1, 2, 3, 0):
            to = (z + k) % 4
            total = net[to, p, rows, :].astype(F32)
            for q in range(3):
                total = total + r1[q, to, rows, :].astype(F32)
            if k:
                s2[k - 1, rows, :] = total.astype(BF)
                b2[i, k] = remote(
                    s2.at[k - 1, rows], r2.at[k - 1, rows], bs2.at[i, k - 1], br2.at[i, k - 1], frames=zp(k)
                )
                b2[i, k].start()
            else:
                b2[i, 0] = total

    def back_ready(i):
        first, count = BACK_PIECES[i]
        for k in (1, 2, 3):
            b2[i, k].wait_recv()
        total = b2[i, 0]
        for k in range(3):
            total = total + r2[k, pl.ds(first, count), :].astype(F32)
        if first == DOWN:
            for c in range(3):
                flat[pl.ds(864 + c, 96, stride=3), :] = total[96 * c : 96 * c + 96]
        else:
            for c in range(count // 24):
                mat, col = BACK_ORDER[(first - LEAD) // 24 + c]
                flat[pl.ds(mat[0] + col, 24, stride=mat[1]), :] = total[24 * c : 24 * c + 24]
        return jnp.sum((total * total).reshape(count // 8, 8, 128), 0)

    def block_pair(m):
        got = net[:, :, pl.ds(LEAD + 48 * m, 48), :].astype(F32).reshape(16, 48, 128)
        return got[:, :24].reshape(384, 128).astype(BF), got[:, 24:].reshape(384, 128).astype(BF)

    weights = {QKV: wqkv, SELF: wself, QUERY: wquery, KEYVAL: wkv, CROSS: wcross, UP: wup}

    def unpack_pairs(start, stop):
        for m in range(start, stop):
            for (mat, c), block in zip(OUT_ORDER[2 * m : 2 * m + 2], block_pair(m)):
                if mat in (QKV, QUERY, KEYVAL):
                    weights[mat][pl.ds(128 * c, 128), :] = block.T
                else:
                    weights[mat][:, pl.ds(128 * c, 128)] = block

    def put_pair(first_row, left, right):
        both = jnp.concatenate([left.reshape(16, 24, 128), right.reshape(16, 24, 128)], 1)
        net[:, :, pl.ds(first_row, 48), :] = both.astype(BF).reshape(4, 4, 48, 128)

    for i in range(3):
        out_first(i)
    own = seg[pl.ds(b, 1), :]
    other = seg[pl.ds(1 - b, 1), :]
    number = lax.broadcasted_iota(jnp.int32, (32, N), 0)
    same = number + 4 * j == own
    hot1[...] = jnp.where(same, 1.0, 0.0).astype(BF)
    hot2[...] = jnp.where(number + 4 * j == other, 1.0, 0.0).astype(BF)
    mask[...] = jnp.where(same | (number >= 4), 0.0, MASKED).astype(BF)
    vg[...] = jnp.zeros((16, D), F32)
    for i in range(3):
        out_second(i)
    out_first(3)
    for i in range(3):
        out_ready(i)

    vflat[...] = jnp.zeros((48, 128), F32)
    lane = lax.broadcasted_iota(jnp.int32, (8, 128), 1)
    sub = lax.broadcasted_iota(jnp.int32, (8, 128), 0)
    for i in range(16):
        got = net[i // 4, i % 4, pl.ds(0, 16), :].astype(F32)[:8]
        got = jnp.where(sub * 128 + lane < 264, got, 0.0)
        if i:
            got = pltpu.roll(got, 8 * i, 1)
            got = jnp.where(lane < 8 * i, pltpu.roll(got, 1, 0), got)
        vflat[pl.ds(2 * i, 8), :] += got
    for c in range(3):
        vec[:, pl.ds(128 * c, 128)] = vflat[pl.ds(c, 16, stride=3), :]
    unpack_pairs(0, 5)
    wself[:, pl.ds(0, 128)] = block_pair(4)[1]

    def vector(i):
        return vec[pl.ds(i, 1), :]

    def add_vector(i, grad):
        vg[pl.ds(i, 1), :] += jnp.sum(grad, 0, keepdims=True)

    def first_norm(t):
        rows = rows_at(t, TILE)
        unit, _ = normalise(x[rows, :].astype(F32))
        at[:, rows] = (unit * vector(0) + vector(1)).astype(BF).T

    loop(0, 4, first_norm)

    def project(w, n_ref, to):
        def part(i):
            rows = rows_at(i, D)
            to[rows, :] = mm(w[rows, :], n_ref[...]).astype(BF)

        loop(0, to.shape[0] // D, part)

    project(wqkv, at, qkv)
    out_second(3)
    out_first(4)

    def head(ref, first, i):
        return ref[pl.ds(pl.multiple_of(first + i * 48, 16), 48), :]

    def set_head(ref, first, i, value):
        ref[pl.ds(pl.multiple_of(first + i * 48, 16), 48), :] = value

    def e_out(e_hbm, i):
        return pltpu.make_async_copy(ring.at[i % 3], e_hbm.at[i], es.at[i % 3])

    def e_in(e_hbm, i):
        return pltpu.make_async_copy(e_hbm.at[i], ring.at[i % 3], es.at[i % 3])

    def attend_heads(start, stop, q, kvs, kfirst, hot, o_ref, inv_ref, e_hbm):
        def one(i):
            @pl.when(i >= 3)
            def _():
                e_out(e_hbm, i - 3).wait()

            o, e, inv = att_head(
                head(q, 0, i), head(kvs, kfirst, i), head(kvs, kfirst + D, i), hot[...], mask[...]
            )
            ring[i % 3] = e
            e_out(e_hbm, i).start()
            set_head(o_ref, 0, i, o)
            inv_ref[pl.ds(i, 1), :] = inv

        loop(start, stop, one)
        if stop == HEADS:
            for i in range(5, 8):
                e_out(e_hbm, i).wait()

    def attend_back_heads(start, stop, q, kvs, kfirst, o_ref, inv_ref, e_hbm, dk_ref, dfirst):
        if start == 0:
            e_in(e_hbm, 0).start()
            e_in(e_hbm, 1).start()

        def one(i):
            @pl.when(i + 2 < HEADS)
            def _():
                e_in(e_hbm, i + 2).start()

            e_in(e_hbm, i).wait()
            dq, dk, dv = att_back_head(
                head(q, 0, i), head(kvs, kfirst, i), head(kvs, kfirst + D, i), head(o_ref, 0, i), head(dot, 0, i),
                ring.at[i % 3], inv_ref[pl.ds(i, 1), :],
            )
            set_head(q, 0, i, dq)
            set_head(dk_ref, dfirst, i, dk)
            set_head(dk_ref, dfirst + D, i, dv)

        loop(start, stop, one)

    attend_heads(0, 4, qkv, qkv, D, hot1, o1, inv1, e1_hbm)
    out_second(4)
    out_first(5)
    attend_heads(4, 8, qkv, qkv, D, hot1, o1, inv1, e1_hbm)
    out_second(5)
    out_ready(3)
    unpack_pairs(5, 12)

    def second_norm(t):
        rows = rows_at(t, TILE)
        self_out = mm(o1[:, rows].astype(BF).T, wself[...])
        hidden = x[rows, :].astype(F32) + vector(8) * self_out
        h[rows, :] = hidden
        unit, _ = normalise(hidden)
        n2t[:, rows] = (unit * vector(2) + vector(3)).astype(BF).T
        n3t[:, rows] = (unit * vector(4) + vector(5)).astype(BF).T

    loop(0, 4, second_norm)
    project(wkv, n3t, kv)
    send_kv = remote(kv, far, ks.at[0], kr.at[0], branch=1 - b)
    send_kv.start()
    project(wquery, n2t, cq)
    send_kv.wait_recv()
    attend_heads(0, 8, cq, far, 0, hot2, o2, inv2, e2_hbm)
    out_ready(4)
    unpack_pairs(12, 18)
    out_ready(5)
    for c in range(3):
        wdown[:, pl.ds(128 * c, 128)] = net[:, :, pl.ds(DOWN + 96 * c, 96), :].reshape(1536, 128)
    for c in list(a1.values()) + list(a2.values()):
        c.wait_send()

    def out_copy(t):
        return pltpu.make_async_copy(stage16.at[t % 2], out_hbm.at[rows_at(t, TILE)], os.at[t % 2])

    def feed_forward(t):
        rows = rows_at(t, TILE)
        cross_out = mm(o2[:, rows].astype(BF).T, wcross[...])
        second_h = h[rows, :] + vector(9) * cross_out
        unit, scale = normalise(second_h)
        n4 = (unit * vector(6) + vector(7)).astype(BF)
        n4t[:, rows] = n4.T
        grad_out = cot[rows, :].astype(F32)
        dffn16 = (grad_out * vector(10)).astype(BF)
        dffn[rows, :] = dffn16
        ffn_out = jnp.zeros((TILE, D), F32)
        dn4 = jnp.zeros((TILE, D), F32)
        for c in range(4):
            part = slice(c * D, (c + 1) * D)
            u = mm(n4, wup[:, part])
            share = 0.5 * (1.0 + lax.erf(u * math.sqrt(0.5)))
            slope = share + u * (jnp.exp(-0.5 * u * u) * (1.0 / math.sqrt(2.0 * math.pi)))
            z16 = (u * share).astype(BF)
            zt[part, rows] = z16.T
            ffn_out = ffn_out + mm(z16, wdown[part, :])
            du16 = (mm_nt(dffn16, wdown[part, :]) * slope).astype(BF)
            du[rows, part] = du16
            dn4 = dn4 + mm_nt(du16, wup[:, part])

        @pl.when(t >= 2)
        def _():
            out_copy(t - 2).wait()

        stage16[t % 2] = (second_h + vector(10) * ffn_out).astype(BF)
        out_copy(t).start()
        add_vector(10, grad_out * ffn_out)
        add_vector(6, dn4 * unit)
        add_vector(7, dn4)
        dh2 = grad_out + normalise_back(unit, scale, dn4 * vector(6))
        dh[rows, :] = dh2
        add_vector(9, dh2 * cross_out)
        dcross16 = (dh2 * vector(9)).astype(BF)
        dcr[rows, :] = dcross16
        dot[:, rows] = mm_nt(wcross[...], dcross16).astype(BF)

    loop(0, 4, feed_forward)
    for i in (2, 3):
        out_copy(i).wait()

    def down_grad(i):
        grad = mm(zt[rows_at(i, D), :], dffn[...])
        for c in range(3):
            net[i, :, pl.ds(DOWN + 96 * c, 96), :] = grad[:, 128 * c : 128 * c + 128].astype(BF).reshape(4, 96, 128)

    loop(0, 4, down_grad)
    back_first(0)

    def up_grad(i):
        grad = mm(n4t[...], du[:, rows_at(i, 256)])
        put_pair(pl.multiple_of(LEAD + 24 * 24 + 48 * i, 16), grad[:, :128], grad[:, 128:])

    loop(0, 6, up_grad)
    back_first(1)
    attend_back_heads(0, 4, cq, far, 0, o2, inv2, e2_hbm, dkv, 0)
    back_second(0)
    attend_back_heads(4, 8, cq, far, 0, o2, inv2, e2_hbm, dkv, 0)
    send_dkv = remote(dkv, dkv_far, ks.at[1], kr.at[1], branch=1 - b)
    send_dkv.start()
    back_second(1)
    g_query = mm_nt(n2t[...], cq[...])
    g_cross = mm(o2[...].astype(BF), dcr[...])
    put_pair(LEAD + 24 * 12, g_query[:, :128], g_query[:, 128:256])
    put_pair(LEAD + 24 * 22, g_cross[:, 128:256], g_cross[:, 256:])
    send_dkv.wait_recv()

    def third_back(t):
        rows = rows_at(t, TILE)
        dn2 = mm(cq[:, rows].T, wquery[...])
        dn3 = mm(dkv_far[:, rows].T, wkv[...])
        unit, scale = normalise(h[rows, :])
        add_vector(2, dn2 * unit)
        add_vector(3, dn2)
        add_vector(4, dn3 * unit)
        add_vector(5, dn3)
        hidden_grad = dh[rows, :] + normalise_back(unit, scale, dn2 * vector(2) + dn3 * vector(4))
        dh[rows, :] = hidden_grad
        self_out = mm(o1[:, rows].astype(BF).T, wself[...])
        add_vector(8, hidden_grad * self_out)
        dself16 = (hidden_grad * vector(8)).astype(BF)
        dcr[rows, :] = dself16
        dot[:, rows] = mm_nt(wself[...], dself16).astype(BF)

    g_kv = mm_nt(n3t[...], dkv_far[...])
    put_pair(LEAD + 24 * 14, g_query[:, 256:], g_kv[:, :128])
    put_pair(LEAD + 24 * 16, g_kv[:, 128:256], g_kv[:, 256:384])
    put_pair(LEAD + 24 * 18, g_kv[:, 384:512], g_kv[:, 512:640])
    put_pair(LEAD + 24 * 20, g_kv[:, 640:], g_cross[:, :128])
    back_first(2)
    loop(0, 4, third_back)
    g_self = mm(o1[...].astype(BF), dcr[...])
    squares = back_ready(0)
    for s, (start, stop) in enumerate(((0, 3), (3, 6), (6, 8))):
        attend_back_heads(start, stop, qkv, qkv, D, o1, inv1, e1_hbm, qkv, D)
        g = [mm_nt(at[...], qkv[pl.ds(D * i + 128 * s, 128), :]) for i in range(3)]
        put_pair(LEAD + 96 * s, g[0], g[1])
        put_pair(LEAD + 96 * s + 48, g[2], g_self[:, 128 * s : 128 * s + 128])
        back_first(3 + s)
        back_second(2 + s)
        if s == 0:
            squares = squares + back_ready(1)
        if s == 1:
            squares = squares + back_ready(2)

    def gin_copy(t):
        return pltpu.make_async_copy(stage32.at[t % 2], gin_hbm.at[rows_at(t, TILE)], gs.at[t % 2])

    def first_back(t):
        rows = rows_at(t, TILE)
        dn1 = mm(qkv[:, rows].T, wqkv[...])
        unit, scale = normalise(x[rows, :].astype(F32))
        add_vector(0, dn1 * unit)
        add_vector(1, dn1)

        @pl.when(t >= 2)
        def _():
            gin_copy(t - 2).wait()

        stage32[t % 2] = dh[rows, :] + normalise_back(unit, scale, dn1 * vector(0))
        gin_copy(t).start()

    loop(0, 4, first_back)
    v1, v2 = [], []
    for k in (1, 2, 3):
        v1.append(remote(vg, vr1.at[k - 1], vs.at[0, k - 1], vr.at[0, k - 1], frames=pp(k)))
        v1[-1].start()
    back_second(5)
    for c in v1:
        c.wait()
    vg[...] = vg[...] + vr1[0] + vr1[1] + vr1[2]
    for k in (1, 2, 3):
        v2.append(remote(vg, vr2.at[k - 1], vs.at[1, k - 1], vr.at[1, k - 1], frames=zp(k)))
        v2[-1].start()
    for i in (3, 4, 5):
        squares = squares + back_ready(i)
    for c in v2:
        c.wait()
    total = vg[...] + vr2[0] + vr2[1] + vr2[2]
    for c in range(3):
        vflat[pl.ds(c, 16, stride=3), :] = total[:, 128 * c : 128 * c + 128]
    near = vflat[pl.ds(2 * j, 8), :]
    turn = (128 - 8 * j) % 128
    near = pltpu.roll(near, turn, 1)
    near = jnp.where(lane < 128 - 8 * j, near, pltpu.roll(near, 7, 0))
    near = jnp.where(sub * 128 + lane < 264, near, 0.0)
    flat[pl.ds(1152, 8), :] = near
    squares = squares + near * near
    me = 2 * p + b
    nb[pl.ds(me, 1)] = squares[None]
    cn, cz = [], []
    for k in range(4):
        for c in (0, 1):
            if k or c:
                i = len(cn)
                cn.append(
                    remote(nb.at[me], nb.at[me], ns.at[i], nr.at[i], frames=pp(k), branch=(b + c) % 2)
                )
                cn[-1].start()
    for c in cn:
        c.wait_recv()
    nb2[pl.ds(z, 1)] = jnp.sum(nb[...], 0)[None]
    for k in (1, 2, 3):
        cz.append(remote(nb2.at[z], nb2.at[z], ns.at[6 + k], nr.at[6 + k], frames=zp(k)))
        cz[-1].start()
    for c in cz:
        c.wait_recv()
    norm[...] = jnp.sum(nb2[...], 0)
    for c in [v for key, v in list(b1.items()) + list(b2.items()) if key[1]] + cn + cz + [send_kv, send_dkv]:
        c.wait_send()
    for i in (2, 3):
        gin_copy(i).wait()


def step(x, cot, pflat, seg):
    dma = pltpu.SemaphoreType.DMA
    v = pltpu.VMEM
    whole = pl.BlockSpec(memory_space=v)
    hbm = pl.BlockSpec(memory_space=pl.ANY)
    shape = jax.ShapeDtypeStruct
    n_out, n_back = len(OUT_PIECES), len(BACK_PIECES)
    return pl.pallas_call(
        step_kernel,
        out_shape=(
            shape((N, D), BF), shape((N, D), F32), shape((FLAT, 128), F32), shape((8, 128), F32),
            shape((HEADS, N, N), BF), shape((HEADS, N, N), BF),
        ),
        in_specs=[whole] * 4,
        out_specs=(hbm, hbm, whole, whole, hbm, hbm),
        scratch_shapes=[
            v((4, 4, ROWS, 128), BF), v((3, 4, ROWS, 128), BF), v((3, ROWS, 128), BF), v((3, ROWS, 128), BF),
            v((16, D), F32), v((48, 128), F32), v((16, D), F32), v((3, 16, D), F32), v((3, 16, D), F32),
            v((8, 8, 128), F32), v((4, 8, 128), F32),
            v((3 * D, D), BF), v((D, D), BF), v((D, D), BF), v((2 * D, D), BF), v((D, D), BF), v((D, FF), BF),
            v((FF, D), BF),
            v((D, N), BF), v((3 * D, N), BF), v((D, N), F32), v((N, D), F32), v((D, N), BF), v((D, N), BF),
            v((D, N), BF), v((2 * D, N), BF), v((2 * D, N), BF), v((D, N), F32),
            v((D, N), BF), v((FF, N), BF), v((N, FF), BF), v((N, D), BF), v((N, D), F32), v((N, D), BF),
            v((D, N), BF), v((2 * D, N), BF), v((2 * D, N), BF),
            v((3, N, N), BF), v((HEADS, N), F32), v((HEADS, N), F32), v((32, N), BF), v((32, N), BF), v((32, N), BF),
            v((2, TILE, D), BF), v((2, TILE, D), F32),
            dma((n_out, 3)), dma((n_out, 3)), dma((n_out, 3)), dma((n_out, 3)),
            dma((n_back, 3)), dma((n_back, 3)), dma((n_back, 3)), dma((n_back, 3)),
            dma((2,)), dma((2,)), dma((2, 3)), dma((2, 3)), dma((10,)), dma((10,)), dma((3,)), dma((2,)), dma((2,)),
        ],
        compiler_params=pltpu.CompilerParams(
            collective_id=0, has_side_effects=True, vmem_limit_bytes=63 * 1024 * 1024
        ),
        name="step",
    )(x, cot, pflat, seg)


def fast_device(frames_in, seg_ids, cotangent, params, first_moment, second_moment):
    count = lax.axis_size("frames")
    size = params.shape[1]
    pflat = jnp.pad(params[0], (0, FLAT * 128 - size)).reshape(FLAT, 128)
    result, input_grad, flat, square, _, _ = step(frames_in[0], cotangent[0], pflat, seg_ids)
    grad_norm = jnp.sqrt(jnp.sum(square))
    reduced = flat.reshape(1, -1)[:, :size]
    total_params = size * count
    total_rows = frames_in.shape[1] * count
    threshold = 0.01 * math.sqrt(2.0 * total_params * total_rows)
    clipped = reduced * jnp.minimum(1.0, threshold / grad_norm)
    vector_grad = clipped[:, size - NV * D // count :]
    first_new = BETA_ONE * first_moment + (1.0 - BETA_ONE) * clipped
    second_new = BETA_TWO * second_moment + (1.0 - BETA_TWO) * clipped * clipped
    mean_hat = first_new / (1.0 - BETA_ONE**STEP)
    square_hat = second_new / (1.0 - BETA_TWO**STEP)
    new_params = params - LEARN_RATE * (
        mean_hat / (jnp.sqrt(square_hat) + ADAM_EPS) + DECAY_RATE * params
    )
    return (result[None], input_grad[None], clipped, vector_grad, grad_norm, first_new, second_new, new_params)


def solution(mesh):
    placed = (
        P("branch", "frames", None),
        P(None, "frames"),
        P("branch", "frames", None),
        P("branch", "frames"),
        P("branch", "frames"),
        P("branch", "frames"),
    )
    return jax.shard_map(
        fast_device if mesh.shape["frames"] == 16 else on_device,
        mesh=mesh,
        in_specs=placed,
        out_specs=(
            P("branch", "frames", None),
            P("branch", "frames", None),
            P("branch", "frames"),
            P("branch", "frames"),
            P(),
            P("branch", "frames"),
            P("branch", "frames"),
            P("branch", "frames"),
        ),
        check_vma=False,
    )
```

```python
from functools import partial
import math

import jax
import jax.numpy as jnp
from jax import lax
from jax.experimental import pallas as pl
from jax.experimental.pallas import tpu as pltpu
from jax.sharding import PartitionSpec as P

HEADS = 8
HEAD_DIM = 48
D = 384
FF = 1536
NV = 11
STEP = 5


BETA_ONE = 0.9
BETA_TWO = 0.999
LEARN_RATE = 0.05
DECAY_RATE = 0.01
ADAM_EPS = 1e-08
NORM_EPS = 1e-05
MASKED = -1e30


def from_partner(array, axis, apart):
    return lax.ppermute(array, axis, [(i, i ^ 1 << apart) for i in range(lax.axis_size(axis))])


def layer_norm(values, gain, shift):
    centre = values - jnp.mean(values, -1, keepdims=True)
    spread = jnp.mean(centre * centre, -1, keepdims=True)
    return centre * lax.rsqrt(spread + NORM_EPS) * gain + shift


def unpack(flat, count):
    shapes = ((D, 3 * D), (D, D), (D, D), (D, 2 * D), (D, D), (D, FF), (FF, D), (NV, D))
    sliced = flat.reshape(count, flat.shape[0] // count)
    pieces = []
    offset = 0
    for rows_in, cols_out in shapes:
        width = rows_in * cols_out // count
        pieces.append(sliced[:, offset : offset + width].reshape(rows_in, cols_out))
        offset += width
    return pieces


def split_heads(tensor):
    return tensor.reshape(tensor.shape[0], HEADS, HEAD_DIM)


def matmul(left, right):
    return jnp.dot(left, right, preferred_element_type=jnp.float32)


def weight_grad(inputs, grads):
    return jnp.einsum("ri,rj->ij", inputs, grads, preferred_element_type=jnp.float32)


def back_input(grads, weight):
    return jnp.einsum("rj,ij->ri", grads, weight, preferred_element_type=jnp.float32)


def masked_scores(queries, keys_in, allowed, scale):
    scores = (
        jnp.einsum("qhe,khe->hqk", queries, keys_in, preferred_element_type=jnp.float32) * scale
    )
    return jnp.where(allowed[None], scores, MASKED)


def attend(queries, keys_in, values_in, allowed, scale):
    scores = masked_scores(queries, keys_in, allowed, scale)
    row_max = jnp.max(scores, -1, keepdims=True)
    raised = jnp.exp(scores - row_max)
    row_sum = jnp.sum(raised, -1, keepdims=True)
    weights = (raised / row_sum).astype(jnp.bfloat16)
    output = jnp.einsum("hqk,khe->qhe", weights, values_in, preferred_element_type=jnp.float32)
    return (output, row_max + jnp.log(row_sum))


def attend_back(queries, keys_in, values_in, allowed, scale, log_sum, grad_out):
    probs = jnp.exp(masked_scores(queries, keys_in, allowed, scale) - log_sum)
    grad_probs = jnp.einsum("qhe,khe->hqk", grad_out, values_in, preferred_element_type=jnp.float32)
    grad_values = jnp.einsum(
        "hqk,qhe->khe", probs.astype(jnp.bfloat16), grad_out, preferred_element_type=jnp.float32
    )
    centred = grad_probs - jnp.sum(probs * grad_probs, -1, keepdims=True)
    grad_scores = (probs * centred).astype(jnp.bfloat16)
    grad_queries = (
        jnp.einsum("hqk,khe->qhe", grad_scores, keys_in, preferred_element_type=jnp.float32) * scale
    )
    grad_keys = (
        jnp.einsum("hqk,qhe->khe", grad_scores, queries, preferred_element_type=jnp.float32) * scale
    )
    return (
        grad_queries.astype(jnp.bfloat16),
        grad_keys.astype(jnp.bfloat16),
        grad_values.astype(jnp.bfloat16),
    )


def on_device(frames_in, seg_ids, cotangent, params, first_moment, second_moment):
    frames = frames_in[0].astype(jnp.float32)
    rows = frames.shape[0]
    count = lax.axis_size("frames")
    side = lax.axis_index("branch")
    own_seg = jnp.where(side == 0, seg_ids[0], seg_ids[1])
    far_seg = jnp.where(side == 0, seg_ids[1], seg_ids[0])
    self_mask = own_seg[:, None] == own_seg[None, :]
    cross_mask = own_seg[:, None] == far_seg[None, :]
    scale = 1.0 / math.sqrt(HEAD_DIM)
    shard16 = params.astype(jnp.bfloat16)
    whole = lax.all_gather(shard16, "frames", axis=1, tiled=True)[0]
    w_qkv, w_self, w_query, w_keyval, w_cross, w_up, w_down, vec16 = unpack(whole, count)
    vectors = vec16.astype(jnp.float32)
    normed, norm1_back = jax.vjp(layer_norm, frames, vectors[0], vectors[1])
    normed16 = normed.astype(jnp.bfloat16)
    joined16 = matmul(normed16, w_qkv).astype(jnp.bfloat16)
    query16 = split_heads(joined16[:, :D])
    key16 = split_heads(joined16[:, D : 2 * D])
    value16 = split_heads(joined16[:, 2 * D :])
    attended, self_lse = attend(query16, key16, value16, self_mask, scale)
    attended16 = attended.reshape(rows, D).astype(jnp.bfloat16)
    self_out = matmul(attended16, w_self)
    hidden = frames + vectors[8] * self_out
    cross_in, norm2_back = jax.vjp(layer_norm, hidden, vectors[2], vectors[3])
    cross_in16 = cross_in.astype(jnp.bfloat16)
    cross_q16 = matmul(cross_in16, w_query).astype(jnp.bfloat16)
    source, norm3_back = jax.vjp(layer_norm, hidden, vectors[4], vectors[5])
    source16 = source.astype(jnp.bfloat16)
    keyval16 = matmul(source16, w_keyval).astype(jnp.bfloat16)
    far_kv = from_partner(keyval16, "branch", 0)
    far_keys = split_heads(far_kv[:, :D])
    far_values = split_heads(far_kv[:, D:])
    cross_heads = split_heads(cross_q16)
    mixed, cross_lse = attend(cross_heads, far_keys, far_values, cross_mask, scale)
    mixed16 = mixed.reshape(rows, D).astype(jnp.bfloat16)
    cross_out = matmul(mixed16, w_cross)
    second_h = hidden + vectors[9] * cross_out
    ffn_in, norm4_back = jax.vjp(layer_norm, second_h, vectors[6], vectors[7])
    ffn_in16 = ffn_in.astype(jnp.bfloat16)
    pre_act = matmul(ffn_in16, w_up)
    activated, gelu_back = jax.vjp(partial(jax.nn.gelu, approximate=False), pre_act)
    activated16 = activated.astype(jnp.bfloat16)
    ffn_out = matmul(activated16, w_down)
    result = second_h + vectors[10] * ffn_out
    grad_out = cotangent[0].astype(jnp.float32)
    grad_ls3 = jnp.sum(grad_out * ffn_out, 0)
    grad_ffn16 = (grad_out * vectors[10]).astype(jnp.bfloat16)
    grad_down = weight_grad(activated16, grad_ffn16)
    grad_act = back_input(grad_ffn16, w_down)
    grad_pre16 = gelu_back(grad_act)[0].astype(jnp.bfloat16)
    grad_up = weight_grad(ffn_in16, grad_pre16)
    grad_h2_ln, grad_g4, grad_c4 = norm4_back(back_input(grad_pre16, w_up))
    grad_h2 = grad_out + grad_h2_ln
    grad_ls2 = jnp.sum(grad_h2 * cross_out, 0)
    grad_cross16 = (grad_h2 * vectors[9]).astype(jnp.bfloat16)
    grad_wcross = weight_grad(mixed16, grad_cross16)
    grad_mixed16 = back_input(grad_cross16, w_cross).astype(jnp.bfloat16)
    grad_cq16, grad_far_keys, grad_far_values = attend_back(
        cross_heads, far_keys, far_values, cross_mask, scale, cross_lse, split_heads(grad_mixed16)
    )
    returned = jnp.concatenate(
        [grad_far_keys.reshape(rows, D), grad_far_values.reshape(rows, D)], 1
    )
    grad_keyval16 = from_partner(returned, "branch", 0)
    grad_wkeyval = weight_grad(source16, grad_keyval16)
    grad_h_kv, grad_g3, grad_c3 = norm3_back(back_input(grad_keyval16, w_keyval))
    grad_cq_flat = grad_cq16.reshape(rows, D)
    grad_wquery = weight_grad(cross_in16, grad_cq_flat)
    grad_h_q, grad_g2, grad_c2 = norm2_back(back_input(grad_cq_flat, w_query))
    grad_hidden = grad_h2 + grad_h_q + grad_h_kv
    grad_ls1 = jnp.sum(grad_hidden * self_out, 0)
    grad_self16 = (grad_hidden * vectors[8]).astype(jnp.bfloat16)
    grad_wself = weight_grad(attended16, grad_self16)
    grad_att16 = back_input(grad_self16, w_self).astype(jnp.bfloat16)
    grad_q16, grad_k16, grad_v16 = attend_back(
        query16, key16, value16, self_mask, scale, self_lse, split_heads(grad_att16)
    )
    grad_joined16 = jnp.concatenate(
        [grad_q16.reshape(rows, D), grad_k16.reshape(rows, D), grad_v16.reshape(rows, D)], 1
    )
    grad_wqkv = weight_grad(normed16, grad_joined16)
    grad_x_ln, grad_g1, grad_c1 = norm1_back(back_input(grad_joined16, w_qkv))
    input_grad = grad_hidden + grad_x_ln
    grad_vectors = jnp.stack(
        [
            grad_g1,
            grad_c1,
            grad_g2,
            grad_c2,
            grad_g3,
            grad_c3,
            grad_g4,
            grad_c4,
            grad_ls1,
            grad_ls2,
            grad_ls3,
        ]
    )
    pieces = [
        grad_wqkv,
        grad_wself,
        grad_wquery,
        grad_wkeyval,
        grad_wcross,
        grad_up,
        grad_down,
        grad_vectors,
    ]
    flat_grad = jnp.concatenate([piece.reshape(count, -1) for piece in pieces], 1).reshape(1, -1)
    reduced = lax.psum_scatter(flat_grad, "frames", scatter_dimension=1, tiled=True)
    local_square = jnp.sum(reduced * reduced)
    square_sum = lax.psum(local_square, ("branch", "frames"))
    grad_norm = jnp.sqrt(square_sum)
    total_params = params.shape[1] * count
    total_rows = rows * count
    threshold = 0.01 * math.sqrt(2.0 * total_params * total_rows)
    clipped = reduced * jnp.minimum(1.0, threshold / grad_norm)
    vec_width = NV * D // count
    vector_grad = clipped[:, clipped.shape[1] - vec_width :]
    first_new = BETA_ONE * first_moment + (1.0 - BETA_ONE) * clipped
    second_new = BETA_TWO * second_moment + (1.0 - BETA_TWO) * clipped * clipped
    mean_hat = first_new / (1.0 - BETA_ONE**STEP)
    square_hat = second_new / (1.0 - BETA_TWO**STEP)
    new_params = params - LEARN_RATE * (
        mean_hat / (jnp.sqrt(square_hat) + ADAM_EPS) + DECAY_RATE * params
    )
    return (
        result.astype(jnp.bfloat16)[None],
        input_grad[None],
        clipped,
        vector_grad,
        grad_norm,
        first_new,
        second_new,
        new_params,
    )


MESH = pl.DeviceIdType.MESH
BF = jnp.bfloat16
F32 = jnp.float32
C2 = math.log2(math.e) / math.sqrt(HEAD_DIM)
SCALE = 1.0 / math.sqrt(HEAD_DIM)
N = 1024
TILE = 256
LEAD = 16
DOWN = LEAD + 36 * 24
ROWS = DOWN + 288
FLAT = 1160
QKV, SELF, QUERY, KEYVAL, CROSS, UP = (0, 9), (216, 3), (288, 3), (360, 6), (504, 3), (576, 12)
ORDER = [e for s in range(3) for e in ((QKV, s), (QKV, 3 + s), (QKV, 6 + s), (SELF, s))]
ORDER += [(m, c) for m in (QUERY, KEYVAL, CROSS, UP) for c in range(m[1])]
OUT_PIECES = ((0, 112), (112, 96), (208, 96), (304, 288), (592, 288), (880, 288))
BACK_PIECES = ((880, 288), (592, 288), (304, 288), (16, 96), (112, 96), (208, 96))


def remote(src, dst, send, recv, **device):
    return pltpu.make_async_remote_copy(
        src_ref=src, dst_ref=dst, send_sem=send, recv_sem=recv, device_id=device, device_id_type=MESH
    )


def mm(a, b):
    return lax.dot_general(a, b, (((1,), (0,)), ((), ())), preferred_element_type=F32)


def mm_nt(a, b):
    return lax.dot_general(a, b, (((1,), (1,)), ((), ())), preferred_element_type=F32)


def loop(start, stop, body):
    lax.fori_loop(start, stop, lambda i, _: (body(i), 0)[1], 0)


def rows_at(i, size):
    return pl.ds(pl.multiple_of(i * size, size), size)


def normalise(values):
    centre = values - jnp.mean(values, -1, keepdims=True)
    scale = lax.rsqrt(jnp.mean(centre * centre, -1, keepdims=True) + NORM_EPS)
    return centre * scale, scale


def normalise_back(unit, scale, grad):
    return scale * (grad - jnp.mean(grad, -1, keepdims=True) - unit * jnp.mean(grad * unit, -1, keepdims=True))


def att_back_head(q, k, v, o, do, e, inv, e_turned, ds_turned):
    n = k.shape[1]
    values = jnp.concatenate([v, v, jnp.ones((32, n), BF)], 0).T
    do = do.astype(F32)
    minus = -jnp.sum(do * o, 0, keepdims=True) * inv
    do = do * inv
    high = do.astype(BF)
    low = (do - high.astype(F32)).astype(BF)
    minus_high = minus.astype(BF).astype(F32)
    row = lax.broadcasted_iota(jnp.int32, (32, n), 0)
    extra = jnp.where(row == 0, minus_high, jnp.where(row == 1, minus - minus_high, 0.0)).astype(BF)
    grads = jnp.concatenate([high, low, extra], 0)
    e_turned[...] = e.T
    ds = (e.astype(F32) * mm(values, grads)).astype(BF)
    ds_turned[...] = ds.T
    dq = mm(k, ds)
    dk = mm(q, ds_turned[...])
    dv = mm(high, e_turned[...])
    return (dq * SCALE).astype(BF), (dk * SCALE).astype(BF), dv.astype(BF)


def step_kernel(*refs):
    it = iter(refs)
    (x, cot, pflat, seg) = (next(it) for _ in range(4))
    (out_hbm, gin_hbm, flat, norm, e1_hbm, e2_hbm) = (next(it) for _ in range(6))
    (net, r1, s2, r2, vec, vflat, vg, vr1, vr2, nb, nb2) = (next(it) for _ in range(11))
    (wqkv, wself, wquery, wkv, wcross, wup, wdown) = (next(it) for _ in range(7))
    (at, qkv, o1, h, n2t, n3t, cq, kv, far, o2) = (next(it) for _ in range(10))
    (n4t, zt, du, dffn, dh, dcr, dot, dkv, dkv_far) = (next(it) for _ in range(9))
    (ring, keys, scores, inv1, inv2, hot1, hot2, mask, stage16, stage32) = (next(it) for _ in range(10))
    (as1, ar1, as2, ar2, bs1, br1, bs2, br2, ks, kr, vs, vr, ns, nr, es, os, gs) = (next(it) for _ in range(17))
    j = lax.axis_index("frames")
    b = lax.axis_index("branch")
    z, p = j // 4, j % 4

    def zp(k):
        return (z + k) % 4 * 4 + p

    def pp(k):
        return z * 4 + (p + k) % 4

    bar = pltpu.get_barrier_semaphore()
    for k in (1, 2, 3):
        pl.semaphore_signal(bar, inc=1, device_id={"frames": zp(k)}, device_id_type=MESH)
        pl.semaphore_signal(bar, inc=1, device_id={"frames": pp(k)}, device_id_type=MESH)
    for k in range(4):
        pl.semaphore_signal(bar, inc=1, device_id={"branch": 1 - b, "frames": pp(k)}, device_id_type=MESH)

    net[z, p, pl.ds(0, 16), :] = jnp.concatenate([pflat[pl.ds(1152, 8), :], jnp.zeros((8, 128), F32)], 0).astype(BF)
    for m in range(18):
        pair = [pflat[pl.ds(mat[0] + c, 24, stride=mat[1]), :] for mat, c in ORDER[2 * m : 2 * m + 2]]
        net[z, p, pl.ds(LEAD + 48 * m, 48), :] = jnp.concatenate(pair, 0).astype(BF)
    for c in range(3):
        net[z, p, pl.ds(DOWN + 96 * c, 96), :] = pflat[pl.ds(864 + c, 96, stride=3), :].astype(BF)
    pl.semaphore_wait(bar, 10)

    others = (1, 2, 3)

    def a1(i, k):
        part = net.at[z, p, pl.ds(*OUT_PIECES[i])]
        return remote(part, part, as1.at[i, k - 1], ar1.at[i, k - 1], frames=zp(k))

    def a2(i, k):
        part = net.at[:, p, pl.ds(*OUT_PIECES[i])]
        return remote(part, part, as2.at[i, k - 1], ar2.at[i, k - 1], frames=pp(k))

    def b1(i, k):
        rows = pl.ds(*BACK_PIECES[i])
        return remote(
            net.at[:, (p + k) % 4, rows], r1.at[k - 1, :, rows], bs1.at[i, k - 1], br1.at[i, k - 1], frames=pp(k)
        )

    def b2(i, k):
        rows = pl.ds(*BACK_PIECES[i])
        return remote(s2.at[k - 1, rows], r2.at[k - 1, rows], bs2.at[i, k - 1], br2.at[i, k - 1], frames=zp(k))

    def out_first(i):
        for k in others:
            a1(i, k).start()

    def out_second(i):
        for k in others:
            a1(i, k).wait_recv()
        for k in others:
            a2(i, k).start()

    def out_ready(i):
        for k in others:
            a2(i, k).wait_recv()

    def back_first(i):
        for k in others:
            b1(i, k).start()

    mine = {}

    def back_second(i):
        rows = pl.ds(*BACK_PIECES[i])
        for k in others:
            b1(i, k).wait_recv()
        for k in (1, 2, 3, 0):
            to = (z + k) % 4
            total = net[to, p, rows, :].astype(F32)
            for q in range(3):
                total = total + r1[q, to, rows, :].astype(F32)
            if k:
                s2[k - 1, rows, :] = total.astype(BF)
                b2(i, k).start()
            else:
                mine[i] = total

    def back_ready(i):
        first, count = BACK_PIECES[i]
        for k in others:
            b2(i, k).wait_recv()
        total = mine[i]
        for k in range(3):
            total = total + r2[k, pl.ds(first, count), :].astype(F32)
        if first == DOWN:
            for c in range(3):
                flat[pl.ds(864 + c, 96, stride=3), :] = total[96 * c : 96 * c + 96]
        else:
            for c in range(count // 24):
                mat, col = ORDER[(first - LEAD) // 24 + c]
                flat[pl.ds(mat[0] + col, 24, stride=mat[1]), :] = total[24 * c : 24 * c + 24]
        return jnp.sum((total * total).reshape(count // 8, 8, 128), 0)

    def block_pair(m):
        got = net[:, :, pl.ds(LEAD + 48 * m, 48), :].astype(F32).reshape(16, 48, 128)
        return got[:, :24].reshape(384, 128).astype(BF), got[:, 24:].reshape(384, 128).astype(BF)

    weights = {QKV: wqkv, SELF: wself, QUERY: wquery, KEYVAL: wkv, CROSS: wcross, UP: wup}

    def unpack_pairs(start, stop):
        for m in range(start, stop):
            for (mat, c), block in zip(ORDER[2 * m : 2 * m + 2], block_pair(m)):
                if mat in (QKV, QUERY, KEYVAL):
                    weights[mat][pl.ds(128 * c, 128), :] = block.T
                else:
                    weights[mat][:, pl.ds(128 * c, 128)] = block

    def put_pair(first_row, left, right):
        both = jnp.concatenate([left.reshape(16, 24, 128), right.reshape(16, 24, 128)], 1)
        net[:, :, pl.ds(first_row, 48), :] = both.astype(BF).reshape(4, 4, 48, 128)

    for i in range(3):
        out_first(i)
    own = seg[pl.ds(b, 1), :]
    other = seg[pl.ds(1 - b, 1), :]
    number = lax.broadcasted_iota(jnp.int32, (32, N), 0)
    same = number + 4 * j == own
    hot1[...] = jnp.where(same, 1.0, 0.0).astype(BF)
    hot2[...] = jnp.where(number + 4 * j == other, 1.0, 0.0).astype(BF)
    mask[...] = jnp.where(same | (number >= 4), 0.0, MASKED).astype(BF)
    vg[...] = jnp.zeros((16, D), F32)
    for i in range(3):
        out_second(i)
    out_first(3)
    out_ready(0)

    vflat[...] = jnp.zeros((48, 128), F32)
    lane = lax.broadcasted_iota(jnp.int32, (8, 128), 1)
    sub = lax.broadcasted_iota(jnp.int32, (8, 128), 0)
    for i in range(16):
        got = net[i // 4, i % 4, pl.ds(0, 16), :].astype(F32)[:8]
        got = jnp.where(sub * 128 + lane < 264, got, 0.0)
        if i:
            got = pltpu.roll(got, 8 * i, 1)
            got = jnp.where(lane < 8 * i, pltpu.roll(got, 1, 0), got)
        vflat[pl.ds(2 * i, 8), :] += got
    for c in range(3):
        vec[:, pl.ds(128 * c, 128)] = vflat[pl.ds(c, 16, stride=3), :]
    unpack_pairs(0, 2)

    def vector(i):
        return vec[pl.ds(i, 1), :]

    def add_vector(i, grad):
        vg[pl.ds(i, 1), :] += jnp.sum(grad, 0, keepdims=True)

    def first_norm(t):
        rows = rows_at(t, TILE)
        unit, _ = normalise(x[rows, :].astype(F32))
        at[:, rows] = (unit * vector(0) + vector(1)).astype(BF).T

    loop(0, 4, first_norm)

    def project(w, n_ref, to):
        def part(i):
            rows = rows_at(i, D)
            to[rows, :] = mm(w[rows, :], n_ref[...]).astype(BF)

        loop(0, to.shape[0] // D, part)


    def project_round(i):
        parts = [pl.ds(D * m + 128 * i, 128) for m in range(3)]
        got = mm(jnp.concatenate([wqkv[part, :] for part in parts], 0), at[...]).astype(BF)
        for m, part in enumerate(parts):
            qkv[part, :] = got[128 * m : 128 * m + 128]

    project_round(0)

    def head(ref, first, i):
        return ref[pl.ds(pl.multiple_of(first + i * 48, 16), 48), :]

    def set_head(ref, first, i, value):
        ref[pl.ds(pl.multiple_of(first + i * 48, 16), 48), :] = value

    def e_out(e_hbm, i):
        return pltpu.make_async_copy(ring.at[i % 2], e_hbm.at[i], es.at[i % 2])

    def e_in(e_hbm, i):
        return pltpu.make_async_copy(e_hbm.at[i], ring.at[i % 2], es.at[i % 2])

    half, chunk = N // 2, 256

    def attend(q, kvs, kfirst, hot, o_ref, inv_ref, e_hbm, before):
        def make_keys(i):
            k32 = head(kvs, kfirst, i).astype(F32) * C2
            high = k32.astype(BF)
            low = (k32 - high.astype(F32)).astype(BF)
            keys[i % 2] = jnp.concatenate([high, low, hot[...]], 0).T

        def make_queries(i, t):
            at_t = slice(t * half, (t + 1) * half)
            mine = q[pl.ds(pl.multiple_of(i * 48, 16), 48), at_t]
            return jnp.concatenate([mine, mine, mask[:, at_t]], 0)

        def score(i, t, c, queries, top):
            rows = slice(c * chunk, (c + 1) * chunk)
            got = mm(keys[i % 2, rows, :], queries)
            scores[t, rows, :] = got
            got = jnp.max(got.reshape(chunk // 8, 8, half), 0)
            return got if c == 0 else jnp.maximum(top, got)

        make_keys(0)
        top = None
        queries = make_queries(0, 0)
        for c in range(N // chunk):
            top = score(0, 0, c, queries, top)

        def one(i, top):
            after = jnp.minimum(i + 1, HEADS - 1)
            before(i)

            @pl.when(i >= 2)
            def _():
                e_out(e_hbm, i - 2).wait()

            values = jnp.concatenate([head(kvs, kfirst + D, i), jnp.ones((16, N), BF)], 0)
            for t in range(2):
                if t:
                    make_keys(after)
                next_head, next_half = (after, 0) if t else (i, 1)
                peak = jnp.max(top, 0, keepdims=True)
                queries = make_queries(next_head, next_half)
                at_t = slice(t * half, (t + 1) * half)
                o = jnp.zeros((64, half), F32)
                for c in range(N // chunk):
                    rows = slice(c * chunk, (c + 1) * chunk)
                    top = score(next_head, next_half, c, queries, top)
                    e = jnp.exp2(scores[t, rows, :] - peak).astype(BF)
                    ring[i % 2, rows, at_t] = e
                    o = o + mm(values[:, rows], e)
                inv = 1.0 / o[48:49]
                o_ref[pl.ds(pl.multiple_of(i * 48, 16), 48), at_t] = o[:48] * inv
                inv_ref[pl.ds(i, 1), at_t] = inv
            e_out(e_hbm, i).start()
            return top

        lax.fori_loop(0, HEADS, one, top)
        for i in (6, 7):
            e_out(e_hbm, i).wait()

    def attend_back_heads(start, stop, q, kvs, kfirst, o_ref, inv_ref, e_hbm, dk_ref, dfirst):
        if start == 0:
            e_in(e_hbm, 0).start()

        def one(i):
            @pl.when(i + 1 < HEADS)
            def _():
                e_in(e_hbm, i + 1).start()

            e_in(e_hbm, i).wait()
            dq, dk, dv = att_back_head(
                head(q, 0, i), head(kvs, kfirst, i), head(kvs, kfirst + D, i), head(o_ref, 0, i), head(dot, 0, i),
                ring[i % 2], inv_ref[pl.ds(i, 1), :], zt.at[pl.ds(0, N)], du.at[:, pl.ds(0, N)],
            )
            set_head(q, 0, i, dq)
            set_head(dk_ref, dfirst, i, dk)
            set_head(dk_ref, dfirst + D, i, dv)

        loop(start, stop, one)

    def more_weights(i):
        @pl.when(i == 1)
        def _():
            out_ready(1)
            unpack_pairs(2, 4)
            project_round(1)
            out_second(3)
            out_first(4)

        @pl.when(i == 4)
        def _():
            out_ready(2)
            unpack_pairs(4, 6)
            project_round(2)
            out_second(4)
            out_first(5)

    attend(qkv, qkv, D, hot1, o1, inv1, e1_hbm, more_weights)
    out_second(5)
    out_ready(3)
    unpack_pairs(6, 12)

    def second_norm(t):
        rows = rows_at(t, TILE)
        self_out = mm(o1[:, rows].astype(BF).T, wself[...])
        hidden = x[rows, :].astype(F32) + vector(8) * self_out
        h[rows, :] = hidden
        unit, _ = normalise(hidden)
        n2t[:, rows] = (unit * vector(2) + vector(3)).astype(BF).T
        n3t[:, rows] = (unit * vector(4) + vector(5)).astype(BF).T

    loop(0, 4, second_norm)
    project(wkv, n3t, kv)
    send_kv = remote(kv, far, ks.at[0], kr.at[0], branch=1 - b)
    send_kv.start()
    project(wquery, n2t, cq)
    send_kv.wait_recv()
    attend(cq, far, 0, hot2, o2, inv2, e2_hbm, lambda i: None)
    out_ready(4)
    unpack_pairs(12, 18)
    out_ready(5)
    for c in range(3):
        wdown[:, pl.ds(128 * c, 128)] = net[:, :, pl.ds(DOWN + 96 * c, 96), :].reshape(1536, 128)
    for i in range(len(OUT_PIECES)):
        for k in others:
            a1(i, k).wait_send()
            a2(i, k).wait_send()

    def out_copy(t):
        return pltpu.make_async_copy(stage16.at[t % 2], out_hbm.at[rows_at(t, TILE)], os.at[t % 2])

    def feed_forward(t):
        rows = rows_at(t, TILE)
        cross_out = mm(o2[:, rows].astype(BF).T, wcross[...])
        second_h = h[rows, :] + vector(9) * cross_out
        unit, scale = normalise(second_h)
        n4 = (unit * vector(6) + vector(7)).astype(BF)
        n4t[:, rows] = n4.T
        grad_out = cot[rows, :].astype(F32)
        dffn16 = (grad_out * vector(10)).astype(BF)
        dffn[rows, :] = dffn16
        ffn_out = jnp.zeros((TILE, D), F32)
        dn4 = jnp.zeros((TILE, D), F32)
        for c in range(4):
            part = slice(c * D, (c + 1) * D)
            u = mm(n4, wup[:, part])
            share = 0.5 * (1.0 + lax.erf(u * math.sqrt(0.5)))
            slope = share + u * (jnp.exp(-0.5 * u * u) * (1.0 / math.sqrt(2.0 * math.pi)))
            z16 = (u * share).astype(BF)
            zt[part, rows] = z16.T
            ffn_out = ffn_out + mm(z16, wdown[part, :])
            du16 = (mm_nt(dffn16, wdown[part, :]) * slope).astype(BF)
            du[rows, part] = du16
            dn4 = dn4 + mm_nt(du16, wup[:, part])

        @pl.when(t >= 2)
        def _():
            out_copy(t - 2).wait()

        stage16[t % 2] = (second_h + vector(10) * ffn_out).astype(BF)
        out_copy(t).start()
        add_vector(10, grad_out * ffn_out)
        add_vector(6, dn4 * unit)
        add_vector(7, dn4)
        dh2 = grad_out + normalise_back(unit, scale, dn4 * vector(6))
        dh[rows, :] = dh2
        add_vector(9, dh2 * cross_out)
        dcross16 = (dh2 * vector(9)).astype(BF)
        dcr[rows, :] = dcross16
        dot[:, rows] = mm_nt(wcross[...], dcross16).astype(BF)

    loop(0, 4, feed_forward)
    for i in (2, 3):
        out_copy(i).wait()

    def down_grad(i):
        grad = mm(zt[rows_at(i, D), :], dffn[...])
        for c in range(3):
            net[i, :, pl.ds(DOWN + 96 * c, 96), :] = grad[:, 128 * c : 128 * c + 128].astype(BF).reshape(4, 96, 128)

    loop(0, 4, down_grad)
    back_first(0)

    def up_grad(i):
        grad = mm(n4t[...], du[:, rows_at(i, 256)])
        put_pair(pl.multiple_of(LEAD + 24 * 24 + 48 * i, 16), grad[:, :128], grad[:, 128:])

    loop(0, 6, up_grad)
    back_first(1)
    attend_back_heads(0, 4, cq, far, 0, o2, inv2, e2_hbm, dkv, 0)
    back_second(0)
    attend_back_heads(4, 8, cq, far, 0, o2, inv2, e2_hbm, dkv, 0)
    send_dkv = remote(dkv, dkv_far, ks.at[1], kr.at[1], branch=1 - b)
    send_dkv.start()
    back_second(1)
    g_query = mm_nt(n2t[...], cq[...])
    g_cross = mm(o2[...].astype(BF), dcr[...])
    put_pair(LEAD + 24 * 12, g_query[:, :128], g_query[:, 128:256])
    put_pair(LEAD + 24 * 22, g_cross[:, 128:256], g_cross[:, 256:])
    send_dkv.wait_recv()

    def third_back(t):
        rows = rows_at(t, TILE)
        dn2 = mm(cq[:, rows].T, wquery[...])
        dn3 = mm(dkv_far[:, rows].T, wkv[...])
        unit, scale = normalise(h[rows, :])
        add_vector(2, dn2 * unit)
        add_vector(3, dn2)
        add_vector(4, dn3 * unit)
        add_vector(5, dn3)
        hidden_grad = dh[rows, :] + normalise_back(unit, scale, dn2 * vector(2) + dn3 * vector(4))
        dh[rows, :] = hidden_grad
        self_out = mm(o1[:, rows].astype(BF).T, wself[...])
        add_vector(8, hidden_grad * self_out)
        dself16 = (hidden_grad * vector(8)).astype(BF)
        dcr[rows, :] = dself16
        dot[:, rows] = mm_nt(wself[...], dself16).astype(BF)

    g_kv = mm_nt(n3t[...], dkv_far[...])
    put_pair(LEAD + 24 * 14, g_query[:, 256:], g_kv[:, :128])
    put_pair(LEAD + 24 * 16, g_kv[:, 128:256], g_kv[:, 256:384])
    put_pair(LEAD + 24 * 18, g_kv[:, 384:512], g_kv[:, 512:640])
    put_pair(LEAD + 24 * 20, g_kv[:, 640:], g_cross[:, :128])
    back_first(2)
    loop(0, 4, third_back)
    g_self = mm(o1[...].astype(BF), dcr[...])
    squares = back_ready(0)
    for s, (start, stop) in enumerate(((0, 3), (3, 6), (6, 8))):
        attend_back_heads(start, stop, qkv, qkv, D, o1, inv1, e1_hbm, qkv, D)
        g = [mm_nt(at[...], qkv[pl.ds(D * i + 128 * s, 128), :]) for i in range(3)]
        put_pair(LEAD + 96 * s, g[0], g[1])
        put_pair(LEAD + 96 * s + 48, g[2], g_self[:, 128 * s : 128 * s + 128])
        back_first(3 + s)
        back_second(2 + s)
        if s == 0:
            squares = squares + back_ready(1)
        if s == 1:
            squares = squares + back_ready(2)

    def gin_copy(t):
        return pltpu.make_async_copy(stage32.at[t % 2], gin_hbm.at[rows_at(t, TILE)], gs.at[t % 2])

    def first_back(t):
        rows = rows_at(t, TILE)
        dn1 = mm(qkv[:, rows].T, wqkv[...])
        unit, scale = normalise(x[rows, :].astype(F32))
        add_vector(0, dn1 * unit)
        add_vector(1, dn1)

        @pl.when(t >= 2)
        def _():
            gin_copy(t - 2).wait()

        stage32[t % 2] = dh[rows, :] + normalise_back(unit, scale, dn1 * vector(0))
        gin_copy(t).start()

    loop(0, 4, first_back)
    v1, v2 = [], []
    for k in (1, 2, 3):
        v1.append(remote(vg, vr1.at[k - 1], vs.at[0, k - 1], vr.at[0, k - 1], frames=pp(k)))
        v1[-1].start()
    back_second(5)
    for c in v1:
        c.wait()
    vg[...] = vg[...] + vr1[0] + vr1[1] + vr1[2]
    for k in (1, 2, 3):
        v2.append(remote(vg, vr2.at[k - 1], vs.at[1, k - 1], vr.at[1, k - 1], frames=zp(k)))
        v2[-1].start()
    for i in (3, 4, 5):
        squares = squares + back_ready(i)
    for c in v2:
        c.wait()
    total = vg[...] + vr2[0] + vr2[1] + vr2[2]
    for c in range(3):
        vflat[pl.ds(c, 16, stride=3), :] = total[:, 128 * c : 128 * c + 128]
    near = vflat[pl.ds(2 * j, 8), :]
    turn = (128 - 8 * j) % 128
    near = pltpu.roll(near, turn, 1)
    near = jnp.where(lane < 128 - 8 * j, near, pltpu.roll(near, 7, 0))
    near = jnp.where(sub * 128 + lane < 264, near, 0.0)
    flat[pl.ds(1152, 8), :] = near
    squares = squares + near * near
    me = 2 * p + b
    nb[pl.ds(me, 1)] = squares[None]
    cn, cz = [], []
    for k in range(4):
        for c in (0, 1):
            if k or c:
                i = len(cn)
                cn.append(
                    remote(nb.at[me], nb.at[me], ns.at[i], nr.at[i], frames=pp(k), branch=(b + c) % 2)
                )
                cn[-1].start()
    for c in cn:
        c.wait_recv()
    nb2[pl.ds(z, 1)] = jnp.sum(nb[...], 0)[None]
    for k in (1, 2, 3):
        cz.append(remote(nb2.at[z], nb2.at[z], ns.at[6 + k], nr.at[6 + k], frames=zp(k)))
        cz[-1].start()
    for c in cz:
        c.wait_recv()
    norm[...] = jnp.sum(nb2[...], 0)
    for i in range(len(BACK_PIECES)):
        for k in others:
            b1(i, k).wait_send()
            b2(i, k).wait_send()
    for c in cn + cz + [send_kv, send_dkv]:
        c.wait_send()
    for i in (2, 3):
        gin_copy(i).wait()


def step(x, cot, pflat, seg):
    dma = pltpu.SemaphoreType.DMA
    v = pltpu.VMEM
    whole = pl.BlockSpec(memory_space=v)
    hbm = pl.BlockSpec(memory_space=pl.ANY)
    shape = jax.ShapeDtypeStruct
    n_out, n_back = len(OUT_PIECES), len(BACK_PIECES)
    return pl.pallas_call(
        step_kernel,
        out_shape=(
            shape((N, D), BF), shape((N, D), F32), shape((FLAT, 128), F32), shape((8, 128), F32),
            shape((HEADS, N, N), BF), shape((HEADS, N, N), BF),
        ),
        in_specs=[whole] * 4,
        out_specs=(hbm, hbm, whole, whole, hbm, hbm),
        scratch_shapes=[
            v((4, 4, ROWS, 128), BF), v((3, 4, ROWS, 128), BF), v((3, ROWS, 128), BF), v((3, ROWS, 128), BF),
            v((16, D), F32), v((48, 128), F32), v((16, D), F32), v((3, 16, D), F32), v((3, 16, D), F32),
            v((8, 8, 128), F32), v((4, 8, 128), F32),
            v((3 * D, D), BF), v((D, D), BF), v((D, D), BF), v((2 * D, D), BF), v((D, D), BF), v((D, FF), BF),
            v((FF, D), BF),
            v((D, N), BF), v((3 * D, N), BF), v((D, N), F32), v((N, D), F32), v((D, N), BF), v((D, N), BF),
            v((D, N), BF), v((2 * D, N), BF), v((2 * D, N), BF), v((D, N), F32),
            v((D, N), BF), v((FF, N), BF), v((N, FF), BF), v((N, D), BF), v((N, D), F32), v((N, D), BF),
            v((D, N), BF), v((2 * D, N), BF), v((2 * D, N), BF),
            v((2, N, N), BF), v((2, N, 128), BF), v((2, N, N // 2), F32), v((HEADS, N), F32), v((HEADS, N), F32), v((32, N), BF), v((32, N), BF), v((32, N), BF),
            v((2, TILE, D), BF), v((2, TILE, D), F32),
            dma((n_out, 3)), dma((n_out, 3)), dma((n_out, 3)), dma((n_out, 3)),
            dma((n_back, 3)), dma((n_back, 3)), dma((n_back, 3)), dma((n_back, 3)),
            dma((2,)), dma((2,)), dma((2, 3)), dma((2, 3)), dma((10,)), dma((10,)), dma((2,)), dma((2,)), dma((2,)),
        ],
        compiler_params=pltpu.CompilerParams(
            collective_id=0, has_side_effects=True, vmem_limit_bytes=63 * 1024 * 1024
        ),
        name="step",
    )(x, cot, pflat, seg)


def finish_kernel(threshold, flat, square, params, first, second, out, grad_in, *rest):
    (clip_o, vector_o, norm_o, first_o, second_o, params_o, out_o, grad_in_o) = rest[:8]
    (p, m, v, c_s, tail_p, tail_m, tail_v, tail_c, o_s, g_s, big_in, big_out, tail_in, tail_out, way_in, way_out) = rest[8:]
    size = params.shape[1]
    main = size // 1024 * 1024
    parts = 4
    rows = main // 128 // parts
    moves = []
    for i, (src, by, dst) in enumerate(((out, o_s, out_o), (grad_in, g_s, grad_in_o))):
        count = src.shape[0] // 2
        for k in range(2):
            at = pl.ds(k * count, count)
            moves.append((
                pltpu.make_async_copy(src.at[at], by.at[at], way_in.at[i, k]),
                pltpu.make_async_copy(by.at[at], dst.at[at], way_out.at[i, k]),
            ))
    for come, _ in moves:
        come.start()
    reads = []
    for i in range(parts):
        at = pl.ds(i * rows * 128, rows * 128)
        for k, (src, dst) in enumerate(((params, p), (first, m), (second, v))):
            c = pltpu.make_async_copy(
                src.at[:, at].reshape(rows, 128), dst.at[pl.ds(i * rows, rows)], big_in.at[i, k]
            )
            c.start()
            reads.append(c)
    for k, (src, dst) in enumerate(((params, tail_p), (first, tail_m), (second, tail_v))):
        c = pltpu.make_async_copy(src.at[:, pl.ds(main, size - main)], dst, tail_in.at[k])
        c.start()
        reads.append(c)
    norm = jnp.sqrt(jnp.sum(square[...], keepdims=True))
    norm_o[...] = norm
    share = jnp.minimum(1.0, threshold / norm)

    def update(grad, p_ref, m_ref, v_ref):
        clipped = grad * share
        first_new = BETA_ONE * m_ref[...] + (1.0 - BETA_ONE) * clipped
        second_new = BETA_TWO * v_ref[...] + (1.0 - BETA_TWO) * clipped * clipped
        mean_hat = first_new / (1.0 - BETA_ONE**STEP)
        square_hat = second_new / (1.0 - BETA_TWO**STEP)
        old = p_ref[...]
        p_ref[...] = old - LEARN_RATE * (mean_hat / (jnp.sqrt(square_hat) + ADAM_EPS) + DECAY_RATE * old)
        m_ref[...] = first_new
        v_ref[...] = second_new
        return clipped

    writes = []
    for i in range(parts):
        come, go = moves[i]
        come.wait()
        go.start()
        writes.append(go)
        for c in reads[3 * i : 3 * i + 3]:
            c.wait()
        here = pl.ds(i * rows, rows)
        c_s[here] = update(flat[here], p.at[here], m.at[here], v.at[here])
        at = pl.ds(i * rows * 128, rows * 128)
        for k, (src, dst) in enumerate(((c_s, clip_o), (m, first_o), (v, second_o), (p, params_o))):
            c = pltpu.make_async_copy(
                src.at[here], dst.at[:, at].reshape(rows, 128), big_out.at[i, k]
            )
            c.start()
            writes.append(c)
    for c in reads[3 * parts :]:
        c.wait()
    wide = jnp.concatenate([flat[main // 128 + i : main // 128 + i + 1] for i in range(3)], 1)
    tail_c[...] = update(wide[:, : size - main], tail_p, tail_m, tail_v)
    vector_o[...] = tail_c[...]
    for k, (src, dst) in enumerate(((tail_c, clip_o), (tail_m, first_o), (tail_v, second_o), (tail_p, params_o))):
        c = pltpu.make_async_copy(src, dst.at[:, pl.ds(main, size - main)], tail_out.at[k])
        c.start()
        writes.append(c)
    for c in writes:
        c.wait()


def finish(threshold, flat, square, params, first, second, out, grad_in):
    size = params.shape[1]
    main = size // 1024 * 1024
    dma = pltpu.SemaphoreType.DMA
    v = pltpu.VMEM
    whole = pl.BlockSpec(memory_space=v)
    hbm = pl.BlockSpec(memory_space=pl.ANY)
    shape = jax.ShapeDtypeStruct
    like = shape(params.shape, F32)
    return pl.pallas_call(
        partial(finish_kernel, threshold),
        out_shape=(
            like, shape((1, size - main), F32), shape((1, 1), F32), like, like, like, shape(out.shape, BF),
            shape(grad_in.shape, F32),
        ),
        in_specs=[whole, whole, hbm, hbm, hbm, hbm, hbm],
        out_specs=(hbm, whole, whole, hbm, hbm, hbm, hbm, hbm),
        scratch_shapes=[v((main // 128, 128), F32)] * 4 + [v((1, size - main), F32)] * 4
        + [v(out.shape, BF), v(grad_in.shape, F32)]
        + [dma((4, 3)), dma((4, 4)), dma((3,)), dma((4,)), dma((2, 2)), dma((2, 2))],
        name="finish",
    )(flat, square, params, first, second, out, grad_in)


def fast_device(frames_in, seg_ids, cotangent, params, first_moment, second_moment):
    count = lax.axis_size("frames")
    size = params.shape[1]
    pflat = jnp.pad(params, ((0, 0), (0, FLAT * 128 - size))).reshape(FLAT, 128)
    result, input_grad, flat, square, _, _ = step(frames_in[0], cotangent[0], pflat, seg_ids)
    total_params = size * count
    total_rows = frames_in.shape[1] * count
    threshold = 0.01 * math.sqrt(2.0 * total_params * total_rows)
    clipped, vector_grad, norm, first_new, second_new, new_params, result, input_grad = finish(
        threshold, flat, square, params, first_moment, second_moment, result, input_grad
    )
    return (
        result[None], input_grad[None], clipped, vector_grad, norm.reshape(()), first_new, second_new, new_params,
    )


def solution(mesh):
    placed = (
        P("branch", "frames", None),
        P(None, "frames"),
        P("branch", "frames", None),
        P("branch", "frames"),
        P("branch", "frames"),
        P("branch", "frames"),
    )
    return jax.shard_map(
        fast_device if mesh.shape["frames"] == 16 else on_device,
        mesh=mesh,
        in_specs=placed,
        out_specs=(
            P("branch", "frames", None),
            P("branch", "frames", None),
            P("branch", "frames"),
            P("branch", "frames"),
            P(),
            P("branch", "frames"),
            P("branch", "frames"),
            P("branch", "frames"),
        ),
        check_vma=False,
    )
```

```python
from functools import partial
import math

import jax
import jax.numpy as jnp
from jax import lax
from jax.experimental import pallas as pl
from jax.experimental.pallas import tpu as pltpu
from jax.sharding import PartitionSpec as P

HEADS = 8
HEAD_DIM = 48
D = 384
FF = 1536
NV = 11
STEP = 5


BETA_ONE = 0.9
BETA_TWO = 0.999
LEARN_RATE = 0.05
DECAY_RATE = 0.01
ADAM_EPS = 1e-08
NORM_EPS = 1e-05
MASKED = -1e30


def from_partner(array, axis, apart):
    return lax.ppermute(array, axis, [(i, i ^ 1 << apart) for i in range(lax.axis_size(axis))])


def layer_norm(values, gain, shift):
    centre = values - jnp.mean(values, -1, keepdims=True)
    spread = jnp.mean(centre * centre, -1, keepdims=True)
    return centre * lax.rsqrt(spread + NORM_EPS) * gain + shift


def unpack(flat, count):
    shapes = ((D, 3 * D), (D, D), (D, D), (D, 2 * D), (D, D), (D, FF), (FF, D), (NV, D))
    sliced = flat.reshape(count, flat.shape[0] // count)
    pieces = []
    offset = 0
    for rows_in, cols_out in shapes:
        width = rows_in * cols_out // count
        pieces.append(sliced[:, offset : offset + width].reshape(rows_in, cols_out))
        offset += width
    return pieces


def split_heads(tensor):
    return tensor.reshape(tensor.shape[0], HEADS, HEAD_DIM)


def matmul(left, right):
    return jnp.dot(left, right, preferred_element_type=jnp.float32)


def weight_grad(inputs, grads):
    return jnp.einsum("ri,rj->ij", inputs, grads, preferred_element_type=jnp.float32)


def back_input(grads, weight):
    return jnp.einsum("rj,ij->ri", grads, weight, preferred_element_type=jnp.float32)


def masked_scores(queries, keys_in, allowed, scale):
    scores = (
        jnp.einsum("qhe,khe->hqk", queries, keys_in, preferred_element_type=jnp.float32) * scale
    )
    return jnp.where(allowed[None], scores, MASKED)


def attend(queries, keys_in, values_in, allowed, scale):
    scores = masked_scores(queries, keys_in, allowed, scale)
    row_max = jnp.max(scores, -1, keepdims=True)
    raised = jnp.exp(scores - row_max)
    row_sum = jnp.sum(raised, -1, keepdims=True)
    weights = (raised / row_sum).astype(jnp.bfloat16)
    output = jnp.einsum("hqk,khe->qhe", weights, values_in, preferred_element_type=jnp.float32)
    return (output, row_max + jnp.log(row_sum))


def attend_back(queries, keys_in, values_in, allowed, scale, log_sum, grad_out):
    probs = jnp.exp(masked_scores(queries, keys_in, allowed, scale) - log_sum)
    grad_probs = jnp.einsum("qhe,khe->hqk", grad_out, values_in, preferred_element_type=jnp.float32)
    grad_values = jnp.einsum(
        "hqk,qhe->khe", probs.astype(jnp.bfloat16), grad_out, preferred_element_type=jnp.float32
    )
    centred = grad_probs - jnp.sum(probs * grad_probs, -1, keepdims=True)
    grad_scores = (probs * centred).astype(jnp.bfloat16)
    grad_queries = (
        jnp.einsum("hqk,khe->qhe", grad_scores, keys_in, preferred_element_type=jnp.float32) * scale
    )
    grad_keys = (
        jnp.einsum("hqk,qhe->khe", grad_scores, queries, preferred_element_type=jnp.float32) * scale
    )
    return (
        grad_queries.astype(jnp.bfloat16),
        grad_keys.astype(jnp.bfloat16),
        grad_values.astype(jnp.bfloat16),
    )


def on_device(frames_in, seg_ids, cotangent, params, first_moment, second_moment):
    frames = frames_in[0].astype(jnp.float32)
    rows = frames.shape[0]
    count = lax.axis_size("frames")
    side = lax.axis_index("branch")
    own_seg = jnp.where(side == 0, seg_ids[0], seg_ids[1])
    far_seg = jnp.where(side == 0, seg_ids[1], seg_ids[0])
    self_mask = own_seg[:, None] == own_seg[None, :]
    cross_mask = own_seg[:, None] == far_seg[None, :]
    scale = 1.0 / math.sqrt(HEAD_DIM)
    shard16 = params.astype(jnp.bfloat16)
    whole = lax.all_gather(shard16, "frames", axis=1, tiled=True)[0]
    w_qkv, w_self, w_query, w_keyval, w_cross, w_up, w_down, vec16 = unpack(whole, count)
    vectors = vec16.astype(jnp.float32)
    normed, norm1_back = jax.vjp(layer_norm, frames, vectors[0], vectors[1])
    normed16 = normed.astype(jnp.bfloat16)
    joined16 = matmul(normed16, w_qkv).astype(jnp.bfloat16)
    query16 = split_heads(joined16[:, :D])
    key16 = split_heads(joined16[:, D : 2 * D])
    value16 = split_heads(joined16[:, 2 * D :])
    attended, self_lse = attend(query16, key16, value16, self_mask, scale)
    attended16 = attended.reshape(rows, D).astype(jnp.bfloat16)
    self_out = matmul(attended16, w_self)
    hidden = frames + vectors[8] * self_out
    cross_in, norm2_back = jax.vjp(layer_norm, hidden, vectors[2], vectors[3])
    cross_in16 = cross_in.astype(jnp.bfloat16)
    cross_q16 = matmul(cross_in16, w_query).astype(jnp.bfloat16)
    source, norm3_back = jax.vjp(layer_norm, hidden, vectors[4], vectors[5])
    source16 = source.astype(jnp.bfloat16)
    keyval16 = matmul(source16, w_keyval).astype(jnp.bfloat16)
    far_kv = from_partner(keyval16, "branch", 0)
    far_keys = split_heads(far_kv[:, :D])
    far_values = split_heads(far_kv[:, D:])
    cross_heads = split_heads(cross_q16)
    mixed, cross_lse = attend(cross_heads, far_keys, far_values, cross_mask, scale)
    mixed16 = mixed.reshape(rows, D).astype(jnp.bfloat16)
    cross_out = matmul(mixed16, w_cross)
    second_h = hidden + vectors[9] * cross_out
    ffn_in, norm4_back = jax.vjp(layer_norm, second_h, vectors[6], vectors[7])
    ffn_in16 = ffn_in.astype(jnp.bfloat16)
    pre_act = matmul(ffn_in16, w_up)
    activated, gelu_back = jax.vjp(partial(jax.nn.gelu, approximate=False), pre_act)
    activated16 = activated.astype(jnp.bfloat16)
    ffn_out = matmul(activated16, w_down)
    result = second_h + vectors[10] * ffn_out
    grad_out = cotangent[0].astype(jnp.float32)
    grad_ls3 = jnp.sum(grad_out * ffn_out, 0)
    grad_ffn16 = (grad_out * vectors[10]).astype(jnp.bfloat16)
    grad_down = weight_grad(activated16, grad_ffn16)
    grad_act = back_input(grad_ffn16, w_down)
    grad_pre16 = gelu_back(grad_act)[0].astype(jnp.bfloat16)
    grad_up = weight_grad(ffn_in16, grad_pre16)
    grad_h2_ln, grad_g4, grad_c4 = norm4_back(back_input(grad_pre16, w_up))
    grad_h2 = grad_out + grad_h2_ln
    grad_ls2 = jnp.sum(grad_h2 * cross_out, 0)
    grad_cross16 = (grad_h2 * vectors[9]).astype(jnp.bfloat16)
    grad_wcross = weight_grad(mixed16, grad_cross16)
    grad_mixed16 = back_input(grad_cross16, w_cross).astype(jnp.bfloat16)
    grad_cq16, grad_far_keys, grad_far_values = attend_back(
        cross_heads, far_keys, far_values, cross_mask, scale, cross_lse, split_heads(grad_mixed16)
    )
    returned = jnp.concatenate(
        [grad_far_keys.reshape(rows, D), grad_far_values.reshape(rows, D)], 1
    )
    grad_keyval16 = from_partner(returned, "branch", 0)
    grad_wkeyval = weight_grad(source16, grad_keyval16)
    grad_h_kv, grad_g3, grad_c3 = norm3_back(back_input(grad_keyval16, w_keyval))
    grad_cq_flat = grad_cq16.reshape(rows, D)
    grad_wquery = weight_grad(cross_in16, grad_cq_flat)
    grad_h_q, grad_g2, grad_c2 = norm2_back(back_input(grad_cq_flat, w_query))
    grad_hidden = grad_h2 + grad_h_q + grad_h_kv
    grad_ls1 = jnp.sum(grad_hidden * self_out, 0)
    grad_self16 = (grad_hidden * vectors[8]).astype(jnp.bfloat16)
    grad_wself = weight_grad(attended16, grad_self16)
    grad_att16 = back_input(grad_self16, w_self).astype(jnp.bfloat16)
    grad_q16, grad_k16, grad_v16 = attend_back(
        query16, key16, value16, self_mask, scale, self_lse, split_heads(grad_att16)
    )
    grad_joined16 = jnp.concatenate(
        [grad_q16.reshape(rows, D), grad_k16.reshape(rows, D), grad_v16.reshape(rows, D)], 1
    )
    grad_wqkv = weight_grad(normed16, grad_joined16)
    grad_x_ln, grad_g1, grad_c1 = norm1_back(back_input(grad_joined16, w_qkv))
    input_grad = grad_hidden + grad_x_ln
    grad_vectors = jnp.stack(
        [
            grad_g1,
            grad_c1,
            grad_g2,
            grad_c2,
            grad_g3,
            grad_c3,
            grad_g4,
            grad_c4,
            grad_ls1,
            grad_ls2,
            grad_ls3,
        ]
    )
    pieces = [
        grad_wqkv,
        grad_wself,
        grad_wquery,
        grad_wkeyval,
        grad_wcross,
        grad_up,
        grad_down,
        grad_vectors,
    ]
    flat_grad = jnp.concatenate([piece.reshape(count, -1) for piece in pieces], 1).reshape(1, -1)
    reduced = lax.psum_scatter(flat_grad, "frames", scatter_dimension=1, tiled=True)
    local_square = jnp.sum(reduced * reduced)
    square_sum = lax.psum(local_square, ("branch", "frames"))
    grad_norm = jnp.sqrt(square_sum)
    total_params = params.shape[1] * count
    total_rows = rows * count
    threshold = 0.01 * math.sqrt(2.0 * total_params * total_rows)
    clipped = reduced * jnp.minimum(1.0, threshold / grad_norm)
    vec_width = NV * D // count
    vector_grad = clipped[:, clipped.shape[1] - vec_width :]
    first_new = BETA_ONE * first_moment + (1.0 - BETA_ONE) * clipped
    second_new = BETA_TWO * second_moment + (1.0 - BETA_TWO) * clipped * clipped
    mean_hat = first_new / (1.0 - BETA_ONE**STEP)
    square_hat = second_new / (1.0 - BETA_TWO**STEP)
    new_params = params - LEARN_RATE * (
        mean_hat / (jnp.sqrt(square_hat) + ADAM_EPS) + DECAY_RATE * params
    )
    return (
        result.astype(jnp.bfloat16)[None],
        input_grad[None],
        clipped,
        vector_grad,
        grad_norm,
        first_new,
        second_new,
        new_params,
    )


MESH = pl.DeviceIdType.MESH
BF = jnp.bfloat16
F32 = jnp.float32
C2 = math.log2(math.e) / math.sqrt(HEAD_DIM)
SCALE = 1.0 / math.sqrt(HEAD_DIM)
N = 1024
TILE = 256
LEAD = 16
DOWN = LEAD + 36 * 24
ROWS = DOWN + 288
FLAT = 1160
QKV, SELF, QUERY, KEYVAL, CROSS, UP = (0, 9), (216, 3), (288, 3), (360, 6), (504, 3), (576, 12)
ORDER = [e for s in range(3) for e in ((QKV, s), (QKV, 3 + s), (QKV, 6 + s), (SELF, s))]
ORDER += [(m, c) for m in (QUERY, KEYVAL, CROSS, UP) for c in range(m[1])]
OUT_PIECES = ((0, 112), (112, 96), (208, 96), (304, 288), (592, 288), (880, 288))
BACK_PIECES = ((880, 288), (592, 288), (304, 288), (16, 96), (112, 96), (208, 96))


def remote(src, dst, send, recv, **device):
    return pltpu.make_async_remote_copy(
        src_ref=src, dst_ref=dst, send_sem=send, recv_sem=recv, device_id=device, device_id_type=MESH
    )


def mm(a, b):
    return lax.dot_general(a, b, (((1,), (0,)), ((), ())), preferred_element_type=F32)


def mm_nt(a, b):
    return lax.dot_general(a, b, (((1,), (1,)), ((), ())), preferred_element_type=F32)


def loop(start, stop, body):
    lax.fori_loop(start, stop, lambda i, _: (body(i), 0)[1], 0)


def rows_at(i, size):
    return pl.ds(pl.multiple_of(i * size, size), size)


def normalise(values):
    centre = values - jnp.mean(values, -1, keepdims=True)
    scale = lax.rsqrt(jnp.mean(centre * centre, -1, keepdims=True) + NORM_EPS)
    return centre * scale, scale


def normalise_back(unit, scale, grad):
    return scale * (grad - jnp.mean(grad, -1, keepdims=True) - unit * jnp.mean(grad * unit, -1, keepdims=True))


def att_back_head(q, k, v, o, do, e, inv, e_turned, ds_turned):
    n = k.shape[1]
    values = jnp.concatenate([v, v, jnp.ones((32, n), BF)], 0).T
    do = do.astype(F32)
    minus = -jnp.sum(do * o, 0, keepdims=True) * inv
    do = do * inv
    high = do.astype(BF)
    low = (do - high.astype(F32)).astype(BF)
    minus_high = minus.astype(BF).astype(F32)
    row = lax.broadcasted_iota(jnp.int32, (32, n), 0)
    extra = jnp.where(row == 0, minus_high, jnp.where(row == 1, minus - minus_high, 0.0)).astype(BF)
    grads = jnp.concatenate([high, low, extra], 0)
    e_turned[...] = e.T
    ds = (e.astype(F32) * mm(values, grads)).astype(BF)
    ds_turned[...] = ds.T
    dq = mm(k, ds)
    dk = mm(q, ds_turned[...])
    dv = mm(high, e_turned[...])
    return (dq * SCALE).astype(BF), (dk * SCALE).astype(BF), dv.astype(BF)


def step_kernel(*refs):
    it = iter(refs)
    (x_hbm, cot_hbm, pflat, seg) = (next(it) for _ in range(4))
    (out_hbm, gin_hbm, flat, norm, e1_hbm, e2_hbm) = (next(it) for _ in range(6))
    (net, r1, s2, r2, vec, vflat, vg, vg0, vsum, vr1, vr2, late, nb) = (next(it) for _ in range(13))
    (wqkv, wself, wquery, wkv, wcross, wup, wdown) = (next(it) for _ in range(7))
    (at, qkv, o1, h, n2t, n3t, cq, kv, far, o2) = (next(it) for _ in range(10))
    (n4t, zt, du, dffn, dh, dcr, dot, dkv, dkv_far, gself) = (next(it) for _ in range(10))
    (ring, keys, scores, inv1, inv2, hot1, hot2, mask, stage16, stage32, x, cot, sq) = (next(it) for _ in range(13))
    (as1, ar1, as2, ar2, as3, ar3, bs1, br1, bs2, br2, bs3, br3, ks, kr, vs, vr, ls, lr, ns, nr, es, os, gs, xs) = (
        next(it) for _ in range(24)
    )
    j = lax.axis_index("frames")
    b = lax.axis_index("branch")
    z, p = j // 4, j % 4

    def zp(k):
        return (z + k) % 4 * 4 + p

    def pp(k):
        return z * 4 + (p + k) % 4

    bar = pltpu.get_barrier_semaphore()
    for k in (1, 2, 3):
        pl.semaphore_signal(bar, inc=1, device_id={"frames": zp(k)}, device_id_type=MESH)
        pl.semaphore_signal(bar, inc=1, device_id={"frames": pp(k)}, device_id_type=MESH)
    for k in range(4):
        pl.semaphore_signal(bar, inc=1, device_id={"branch": 1 - b, "frames": pp(k)}, device_id_type=MESH)

    x_copy = pltpu.make_async_copy(x_hbm, x, xs.at[0])
    cot_copy = pltpu.make_async_copy(cot_hbm, cot, xs.at[1])
    x_copy.start()

    def pack_pairs(start, stop):
        for m in range(start, stop):
            pair = [pflat[pl.ds(mat[0] + c, 24, stride=mat[1]), :] for mat, c in ORDER[2 * m : 2 * m + 2]]
            net[z, p, pl.ds(LEAD + 48 * m, 48), :] = jnp.concatenate(pair, 0).astype(BF)

    net[z, p, pl.ds(0, 16), :] = jnp.concatenate([pflat[pl.ds(1152, 8), :], jnp.zeros((8, 128), F32)], 0).astype(BF)
    pack_pairs(0, 2)
    pl.semaphore_wait(bar, 10)

    others = (1, 2, 3)

    def a1(i, k):
        part = net.at[z, p, pl.ds(*OUT_PIECES[i])]
        return remote(part, part, as1.at[i, k - 1], ar1.at[i, k - 1], frames=zp(k))

    beside = (p + 1 - 2 * (p % 2), (p + 2) % 4, 3 - p)

    def a2(i, k):
        part = net.at[:, p, pl.ds(*OUT_PIECES[i])]
        return remote(part, part, as2.at[i, k], ar2.at[i, k], frames=z * 4 + beside[k])

    def a3(i, k):
        first, count = OUT_PIECES[i]
        part = net.at[:, beside[k], pl.ds(first + k * (count // 2), count // 2)]
        return remote(part, part, as3.at[i, k], ar3.at[i, k], frames=z * 4 + beside[1 - k])

    direct = len(BACK_PIECES) - 1

    def b1(i, k):
        first, count = BACK_PIECES[i]
        if i == direct:
            rows = pl.ds(first, count)
            return remote(
                net.at[:, beside[k], rows], r1.at[k, :, rows], bs1.at[i, k], br1.at[i, k], frames=z * 4 + beside[k]
            )
        way, across = k % 2, k // 2
        rows = pl.ds(first + way * (count // 2), count // 2)
        return remote(
            net.at[:, beside[2 if across else way], rows], r1.at[across, :, rows], bs1.at[i, k], br1.at[i, k],
            frames=z * 4 + beside[way],
        )

    def b3(i, k):
        first, count = BACK_PIECES[i]
        rows = pl.ds(first + k * (count // 2), count // 2)
        part = net.at[:, beside[1 - k], rows]
        return remote(part, r1.at[2, :, rows], bs3.at[i, k], br3.at[i, k], frames=z * 4 + beside[1 - k])

    def back_ways(i):
        return range(3 if i == direct else 4)

    def b2(i, k):
        rows = pl.ds(*BACK_PIECES[i])
        return remote(s2.at[k - 1, rows], r2.at[k - 1, rows], bs2.at[i, k - 1], br2.at[i, k - 1], frames=zp(k))

    def out_first(i):
        for k in others:
            a1(i, k).start()

    def out_second(i):
        for k in others:
            a1(i, k).wait_recv()
        for k in range(2 if i else 3):
            a2(i, k).start()

    def out_third(i):
        for k in range(2):
            a2(i, k).wait_recv()
        for k in range(2):
            a3(i, k).start()

    def out_ready(i):
        for k in range(2 if i else 3):
            (a3 if i else a2)(i, k).wait_recv()

    def back_first(i):
        for k in back_ways(i):
            b1(i, k).start()

    def back_middle(i):
        first, count = BACK_PIECES[i]
        for k in back_ways(i):
            b1(i, k).wait_recv()
        for k in range(2):
            rows = pl.ds(first + k * (count // 2), count // 2)
            to = beside[1 - k]
            for q in range(4):
                net[q, to, rows, :] = (net[q, to, rows, :].astype(F32) + r1[1, q, rows, :].astype(F32)).astype(BF)
            b3(i, k).start()

    def plane_sum(i, to):
        rows = pl.ds(*BACK_PIECES[i])
        total = net[to, p, rows, :].astype(F32) + r1[0, to, rows, :].astype(F32) + r1[2, to, rows, :].astype(F32)
        return total + r1[1, to, rows, :].astype(F32) if i == direct else total

    def back_second(i):
        rows = pl.ds(*BACK_PIECES[i])
        if i == direct:
            for k in back_ways(i):
                b1(i, k).wait_recv()
        else:
            for k in range(2):
                b3(i, k).wait_recv()
        for k in others:
            s2[k - 1, rows, :] = plane_sum(i, (z + k) % 4).astype(BF)
            b2(i, k).start()

    def back_ready(i):
        first, count = BACK_PIECES[i]
        for k in others:
            b2(i, k).wait_recv()
        total = plane_sum(i, z)
        for k in range(3):
            total = total + r2[k, pl.ds(first, count), :].astype(F32)
        if first == DOWN:
            for c in range(3):
                flat[pl.ds(864 + c, 96, stride=3), :] = total[96 * c : 96 * c + 96]
        else:
            for c in range(count // 24):
                mat, col = ORDER[(first - LEAD) // 24 + c]
                flat[pl.ds(mat[0] + col, 24, stride=mat[1]), :] = total[24 * c : 24 * c + 24]
        sq[...] += jnp.sum((total * total).reshape(count // 8, 8, 128), 0)

    def block_pair(m):
        got = net[:, :, pl.ds(LEAD + 48 * m, 48), :].astype(F32).reshape(16, 48, 128)
        return got[:, :24].reshape(384, 128).astype(BF), got[:, 24:].reshape(384, 128).astype(BF)

    weights = {QKV: wqkv, SELF: wself, QUERY: wquery, KEYVAL: wkv, CROSS: wcross, UP: wup}

    def unpack_pairs(start, stop):
        for m in range(start, stop):
            for (mat, c), block in zip(ORDER[2 * m : 2 * m + 2], block_pair(m)):
                if mat in (QKV, QUERY, KEYVAL):
                    weights[mat][pl.ds(128 * c, 128), :] = block.T
                else:
                    weights[mat][:, pl.ds(128 * c, 128)] = block

    def put_pair(first_row, left, right):
        both = jnp.concatenate([left.reshape(16, 24, 128), right.reshape(16, 24, 128)], 1)
        net[:, :, pl.ds(first_row, 48), :] = both.astype(BF).reshape(4, 4, 48, 128)

    out_first(0)
    pack_pairs(2, 6)
    out_first(1)
    out_first(2)
    pack_pairs(6, 18)
    for c in range(3):
        net[z, p, pl.ds(DOWN + 96 * c, 96), :] = pflat[pl.ds(864 + c, 96, stride=3), :].astype(BF)
    own = seg[pl.ds(b, 1), :]
    other = seg[pl.ds(1 - b, 1), :]
    number = lax.broadcasted_iota(jnp.int32, (32, N), 0)
    same = number + 4 * j == own
    hot1[...] = jnp.where(same, 1.0, 0.0).astype(BF)
    hot2[...] = jnp.where(number + 4 * j == other, 1.0, 0.0).astype(BF)
    mask[...] = jnp.where(same | (number >= 4), 0.0, MASKED).astype(BF)
    vg[...] = jnp.zeros((16, D), F32)
    vg0[...] = jnp.zeros((8, D), F32)
    sq[...] = jnp.zeros((8, 128), F32)
    out_second(0)
    out_first(3)
    out_second(1)
    out_second(2)
    out_ready(0)
    out_third(1)

    vflat[...] = jnp.zeros((48, 128), F32)
    lane = lax.broadcasted_iota(jnp.int32, (8, 128), 1)
    sub = lax.broadcasted_iota(jnp.int32, (8, 128), 0)
    for i in range(16):
        got = net[i // 4, i % 4, pl.ds(0, 16), :].astype(F32)[:8]
        got = jnp.where(sub * 128 + lane < 264, got, 0.0)
        if i:
            got = pltpu.roll(got, 8 * i, 1)
            got = jnp.where(lane < 8 * i, pltpu.roll(got, 1, 0), got)
        vflat[pl.ds(2 * i, 8), :] += got
    for c in range(3):
        vec[:, pl.ds(128 * c, 128)] = vflat[pl.ds(c, 16, stride=3), :]
    unpack_pairs(0, 2)

    def vector(i):
        return vec[pl.ds(i, 1), :]

    def add_vector(i, grad):
        vg[pl.ds(i, 1), :] += jnp.sum(grad, 0, keepdims=True)

    def first_norm(t):
        rows = rows_at(t, TILE)
        unit, _ = normalise(x[rows, :].astype(F32))
        at[:, rows] = (unit * vector(0) + vector(1)).astype(BF).T

    x_copy.wait()
    cot_copy.start()
    loop(0, 4, first_norm)

    def project(w, n_ref, to):
        def part(i):
            rows = rows_at(i, D)
            to[rows, :] = mm(w[rows, :], n_ref[...]).astype(BF)

        loop(0, to.shape[0] // D, part)


    def project_round(i):
        parts = [pl.ds(D * m + 128 * i, 128) for m in range(3)]
        got = mm(jnp.concatenate([wqkv[part, :] for part in parts], 0), at[...]).astype(BF)
        for m, part in enumerate(parts):
            qkv[part, :] = got[128 * m : 128 * m + 128]

    project_round(0)

    def head(ref, first, i):
        return ref[pl.ds(pl.multiple_of(first + i * 48, 16), 48), :]

    def set_head(ref, first, i, value):
        ref[pl.ds(pl.multiple_of(first + i * 48, 16), 48), :] = value

    def e_out(e_hbm, i):
        return pltpu.make_async_copy(ring.at[i % 2], e_hbm.at[i], es.at[i % 2])

    def e_in(e_hbm, i):
        return pltpu.make_async_copy(e_hbm.at[i], ring.at[i % 2], es.at[i % 2])

    half, chunk = N // 2, 256

    def attend(q, kvs, kfirst, hot, o_ref, inv_ref, e_hbm, before):
        def make_keys(i):
            k32 = head(kvs, kfirst, i).astype(F32) * C2
            high = k32.astype(BF)
            low = (k32 - high.astype(F32)).astype(BF)
            keys[i % 2] = jnp.concatenate([high, low, hot[...]], 0).T

        def make_queries(i, t):
            at_t = slice(t * half, (t + 1) * half)
            mine = q[pl.ds(pl.multiple_of(i * 48, 16), 48), at_t]
            return jnp.concatenate([mine, mine, mask[:, at_t]], 0)

        def score(i, t, c, queries, top):
            rows = slice(c * chunk, (c + 1) * chunk)
            got = mm(keys[i % 2, rows, :], queries)
            scores[t, rows, :] = got
            got = jnp.max(got.reshape(chunk // 8, 8, half), 0)
            return got if c == 0 else jnp.maximum(top, got)

        make_keys(0)
        top = None
        queries = make_queries(0, 0)
        for c in range(N // chunk):
            top = score(0, 0, c, queries, top)

        def one(i, top):
            after = jnp.minimum(i + 1, HEADS - 1)
            before(i)

            @pl.when(i >= 2)
            def _():
                e_out(e_hbm, i - 2).wait()

            values = jnp.concatenate([head(kvs, kfirst + D, i), jnp.ones((16, N), BF)], 0)
            for t in range(2):
                if t:
                    make_keys(after)
                next_head, next_half = (after, 0) if t else (i, 1)
                peak = jnp.max(top, 0, keepdims=True)
                queries = make_queries(next_head, next_half)
                at_t = slice(t * half, (t + 1) * half)
                o = jnp.zeros((64, half), F32)
                for c in range(N // chunk):
                    rows = slice(c * chunk, (c + 1) * chunk)
                    top = score(next_head, next_half, c, queries, top)
                    e = jnp.exp2(scores[t, rows, :] - peak).astype(BF)
                    ring[i % 2, rows, at_t] = e
                    o = o + mm(values[:, rows], e)
                inv = 1.0 / o[48:49]
                o_ref[pl.ds(pl.multiple_of(i * 48, 16), 48), at_t] = o[:48] * inv
                inv_ref[pl.ds(i, 1), at_t] = inv
            e_out(e_hbm, i).start()
            return top

        lax.fori_loop(0, HEADS, one, top)
        for i in (6, 7):
            e_out(e_hbm, i).wait()

    def attend_back(q, kvs, kfirst, o_ref, inv_ref, e_hbm, dk_ref, dfirst, before):
        e_in(e_hbm, 0).start()

        def one(i):
            @pl.when(i + 1 < HEADS)
            def _():
                e_in(e_hbm, i + 1).start()

            before(i)
            e_in(e_hbm, i).wait()
            dq, dk, dv = att_back_head(
                head(q, 0, i), head(kvs, kfirst, i), head(kvs, kfirst + D, i), head(o_ref, 0, i), head(dot, 0, i),
                ring[i % 2], inv_ref[pl.ds(i, 1), :], zt.at[pl.ds(0, N)], du.at[:, pl.ds(0, N)],
            )
            set_head(q, 0, i, dq)
            set_head(dk_ref, dfirst, i, dk)
            set_head(dk_ref, dfirst + D, i, dv)

        loop(0, HEADS, one)

    def at_head(i, **steps):
        for name, step in steps.items():
            pl.when(i == int(name[1:]))(step)

    def more_weights(i):
        @pl.when(i == 0)
        def _():
            out_second(3)
            out_first(4)

        @pl.when(i == 1)
        def _():
            out_ready(1)
            out_third(2)
            unpack_pairs(2, 4)
            project_round(1)

        @pl.when(i == 4)
        def _():
            out_ready(2)
            out_third(3)
            out_second(4)
            out_first(5)
            unpack_pairs(4, 6)
            project_round(2)

    attend(qkv, qkv, D, hot1, o1, inv1, e1_hbm, more_weights)
    out_ready(3)
    out_third(4)
    out_second(5)
    unpack_pairs(6, 12)

    def second_norm(t):
        rows = rows_at(t, TILE)
        self_out = mm(o1[:, rows].astype(BF).T, wself[...])
        hidden = x[rows, :].astype(F32) + vector(8) * self_out
        h[rows, :] = hidden
        unit, _ = normalise(hidden)
        n2t[:, rows] = (unit * vector(2) + vector(3)).astype(BF).T
        n3t[:, rows] = (unit * vector(4) + vector(5)).astype(BF).T

    loop(0, 4, second_norm)
    project(wkv, n3t, kv)
    send_kv = remote(kv, far, ks.at[0], kr.at[0], branch=1 - b)
    send_kv.start()
    project(wquery, n2t, cq)

    def last_weights(i):
        @pl.when(i == 2)
        def _():
            out_ready(4)
            out_third(5)

    send_kv.wait_recv()
    attend(cq, far, 0, hot2, o2, inv2, e2_hbm, last_weights)
    unpack_pairs(12, 18)
    out_ready(5)
    for c in range(3):
        wdown[:, pl.ds(128 * c, 128)] = net[:, :, pl.ds(DOWN + 96 * c, 96), :].reshape(1536, 128)
    for i in range(len(OUT_PIECES)):
        for k in others:
            a1(i, k).wait_send()
        for k in range(2 if i else 3):
            a2(i, k).wait_send()
            if i:
                a3(i, k).wait_send()

    def out_copy(t):
        return pltpu.make_async_copy(stage16.at[t % 2], out_hbm.at[rows_at(t, TILE)], os.at[t % 2])

    def feed_forward(t):
        rows = rows_at(t, TILE)
        cross_out = mm(o2[:, rows].astype(BF).T, wcross[...])
        second_h = h[rows, :] + vector(9) * cross_out
        unit, scale = normalise(second_h)
        n4 = (unit * vector(6) + vector(7)).astype(BF)
        n4t[:, rows] = n4.T
        grad_out = cot[rows, :].astype(F32)
        dffn16 = (grad_out * vector(10)).astype(BF)
        dffn[rows, :] = dffn16
        ffn_out = jnp.zeros((TILE, D), F32)
        dn4 = jnp.zeros((TILE, D), F32)
        for c in range(4):
            part = slice(c * D, (c + 1) * D)
            u = mm(n4, wup[:, part])
            share = 0.5 * (1.0 + lax.erf(u * math.sqrt(0.5)))
            slope = share + u * (jnp.exp(-0.5 * u * u) * (1.0 / math.sqrt(2.0 * math.pi)))
            z16 = (u * share).astype(BF)
            zt[part, rows] = z16.T
            ffn_out = ffn_out + mm(z16, wdown[part, :])
            du16 = (mm_nt(dffn16, wdown[part, :]) * slope).astype(BF)
            du[rows, part] = du16
            dn4 = dn4 + mm_nt(du16, wup[:, part])

        @pl.when(t >= 2)
        def _():
            out_copy(t - 2).wait()

        stage16[t % 2] = (second_h + vector(10) * ffn_out).astype(BF)
        out_copy(t).start()
        add_vector(10, grad_out * ffn_out)
        add_vector(6, dn4 * unit)
        add_vector(7, dn4)
        dh2 = grad_out + normalise_back(unit, scale, dn4 * vector(6))
        dh[rows, :] = dh2
        add_vector(9, dh2 * cross_out)
        dcross16 = (dh2 * vector(9)).astype(BF)
        dcr[rows, :] = dcross16
        dot[:, rows] = mm_nt(wcross[...], dcross16).astype(BF)

    cot_copy.wait()
    loop(0, 4, feed_forward)
    for i in (2, 3):
        out_copy(i).wait()

    def down_grad(i):
        grad = mm(zt[rows_at(i, D), :], dffn[...])
        for c in range(3):
            net[i, :, pl.ds(DOWN + 96 * c, 96), :] = grad[:, 128 * c : 128 * c + 128].astype(BF).reshape(4, 96, 128)

    loop(0, 4, down_grad)
    back_first(0)

    def up_grad(i):
        grad = mm(n4t[...], du[:, rows_at(i, 256)])
        put_pair(pl.multiple_of(LEAD + 24 * 24 + 48 * i, 16), grad[:, :128], grad[:, 128:])

    loop(0, 6, up_grad)
    back_first(1)
    attend_back(
        cq, far, 0, o2, inv2, e2_hbm, dkv, 0, lambda i: at_head(i, h4=lambda: back_middle(0), h7=lambda: back_middle(1))
    )
    send_dkv = remote(dkv, dkv_far, ks.at[1], kr.at[1], branch=1 - b)
    send_dkv.start()
    back_second(0)
    g_query = mm_nt(n2t[...], cq[...])
    g_cross = mm(o2[...].astype(BF), dcr[...])
    put_pair(LEAD + 24 * 12, g_query[:, :128], g_query[:, 128:256])
    put_pair(LEAD + 24 * 22, g_cross[:, 128:256], g_cross[:, 256:])
    send_dkv.wait_recv()

    def third_back(t):
        rows = rows_at(t, TILE)
        dn2 = mm(cq[:, rows].T, wquery[...])
        dn3 = mm(dkv_far[:, rows].T, wkv[...])
        unit, scale = normalise(h[rows, :])
        add_vector(2, dn2 * unit)
        add_vector(3, dn2)
        add_vector(4, dn3 * unit)
        add_vector(5, dn3)
        hidden_grad = dh[rows, :] + normalise_back(unit, scale, dn2 * vector(2) + dn3 * vector(4))
        dh[rows, :] = hidden_grad
        self_out = mm(o1[:, rows].astype(BF).T, wself[...])
        add_vector(8, hidden_grad * self_out)
        dself16 = (hidden_grad * vector(8)).astype(BF)
        dcr[rows, :] = dself16
        dot[:, rows] = mm_nt(wself[...], dself16).astype(BF)

    g_kv = mm_nt(n3t[...], dkv_far[...])
    put_pair(LEAD + 24 * 14, g_query[:, 256:], g_kv[:, :128])
    put_pair(LEAD + 24 * 16, g_kv[:, 128:256], g_kv[:, 256:384])
    put_pair(LEAD + 24 * 18, g_kv[:, 384:512], g_kv[:, 512:640])
    put_pair(LEAD + 24 * 20, g_kv[:, 640:], g_cross[:, :128])
    back_first(2)
    back_second(1)
    loop(0, 4, third_back)
    gself[...] = mm(o1[...].astype(BF), dcr[...])
    back_ready(0)

    def v1(k):
        return remote(vg, vr1.at[k - 1], vs.at[0, k - 1], vr.at[0, k - 1], frames=pp(k))

    def v2(k):
        return remote(vsum, vr2.at[k - 1], vs.at[1, k - 1], vr.at[1, k - 1], frames=zp(k))

    for k in others:
        v1(k).start()

    def round_grad(i):
        g = [mm_nt(at[...], qkv[pl.ds(D * m + 128 * i, 128), :]) for m in range(3)]
        put_pair(LEAD + 96 * i, g[0], g[1])
        put_pair(LEAD + 96 * i + 48, g[2], gself[:, 128 * i : 128 * i + 128])
        back_first(3 + i)

    def vectors_on():
        for k in others:
            v1(k).wait_recv()
        vsum[...] = vg[...] + vr1[0] + vr1[1] + vr1[2]
        for k in others:
            v2(k).start()

    def vectors_there():
        for k in others:
            v2(k).wait_recv()
        total = vsum[...] + vr2[0] + vr2[1] + vr2[2]
        for c in range(3):
            vflat[pl.ds(c, 16, stride=3), :] = total[:, 128 * c : 128 * c + 128]

    def ahead(i):
        @pl.when(i == 2)
        def _():
            back_middle(2)
            back_ready(1)

        @pl.when(i == 3)
        def _():
            round_grad(0)
            vectors_on()

        @pl.when(i == 4)
        def _():
            back_second(2)

        @pl.when(i == 5)
        def _():
            back_middle(3)
            vectors_there()

        @pl.when(i == 6)
        def _():
            round_grad(1)

        @pl.when(i == 7)
        def _():
            back_second(3)
            back_middle(4)
            back_ready(2)

    attend_back(qkv, qkv, D, o1, inv1, e1_hbm, qkv, D, ahead)
    round_grad(2)
    back_second(4)

    def gin_copy(t):
        return pltpu.make_async_copy(stage32.at[t % 2], gin_hbm.at[rows_at(t, TILE)], gs.at[t % 2])

    def first_back(t):
        rows = rows_at(t, TILE)
        dn1 = mm(qkv[:, rows].T, wqkv[...])
        unit, scale = normalise(x[rows, :].astype(F32))
        vg0[0:1, :] += jnp.sum(dn1 * unit, 0, keepdims=True)
        vg0[1:2, :] += jnp.sum(dn1, 0, keepdims=True)

        @pl.when(t >= 2)
        def _():
            gin_copy(t - 2).wait()

        stage32[t % 2] = dh[rows, :] + normalise_back(unit, scale, dn1 * vector(0))
        gin_copy(t).start()

    loop(0, 4, first_back)
    blocks = [vg0[r : r + 1, 128 * c : 128 * c + 128] for r in range(2) for c in range(3)]
    late[pl.ds(j, 1)] = jnp.concatenate(blocks + [jnp.zeros((2, 128), F32)], 0)[None]

    def far_vector(k):
        return remote(late.at[j], late.at[j], ls.at[k - 1], lr.at[k - 1], frames=(j + k) % 16)

    for k in range(1, 16):
        far_vector(k).start()
    back_second(5)
    back_ready(3)
    back_ready(4)
    for k in range(1, 16):
        far_vector(k).wait_recv()
    vflat[pl.ds(0, 8), :] += jnp.sum(late[...], 0)
    near = vflat[pl.ds(2 * j, 8), :]
    turn = (128 - 8 * j) % 128
    near = pltpu.roll(near, turn, 1)
    near = jnp.where(lane < 128 - 8 * j, near, pltpu.roll(near, 7, 0))
    near = jnp.where(sub * 128 + lane < 264, near, 0.0)
    flat[pl.ds(1152, 8), :] = near
    back_ready(5)
    squares = sq[...] + near * near
    me = 16 * b + j
    nb[pl.ds(me, 1), 0:1, :] = jnp.sum(squares, 0, keepdims=True)[None]

    def far_square(k):
        to = (me + k) % 32
        part = nb.at[me, pl.ds(0, 1)]
        return remote(part, part, ns.at[k - 1], nr.at[k - 1], branch=to // 16, frames=to % 16)

    for k in range(1, 32):
        far_square(k).start()
    for k in range(1, 32):
        far_square(k).wait_recv()
    norm[...] = jnp.sum(nb[:, 0, :], 0, keepdims=True)
    for i in range(len(BACK_PIECES)):
        for k in others:
            b2(i, k).wait_send()
        for k in back_ways(i):
            b1(i, k).wait_send()
        if i != direct:
            for k in range(2):
                b3(i, k).wait_send()
    for k in others:
        v1(k).wait_send()
        v2(k).wait_send()
    for k in range(1, 16):
        far_vector(k).wait_send()
    for k in range(1, 32):
        far_square(k).wait_send()
    send_kv.wait_send()
    send_dkv.wait_send()
    for i in (2, 3):
        gin_copy(i).wait()


def step(x, cot, pflat, seg):
    dma = pltpu.SemaphoreType.DMA
    v = pltpu.VMEM
    whole = pl.BlockSpec(memory_space=v)
    hbm = pl.BlockSpec(memory_space=pl.ANY)
    shape = jax.ShapeDtypeStruct
    n_out, n_back = len(OUT_PIECES), len(BACK_PIECES)
    return pl.pallas_call(
        step_kernel,
        out_shape=(
            shape((N, D), BF), shape((N, D), F32), shape((FLAT, 128), F32), shape((1, 128), F32),
            shape((HEADS, N, N), BF), shape((HEADS, N, N), BF),
        ),
        in_specs=[hbm, hbm, whole, whole],
        out_specs=(hbm, hbm, whole, whole, hbm, hbm),
        scratch_shapes=[
            v((4, 4, ROWS, 128), BF), v((3, 4, ROWS, 128), BF), v((3, ROWS, 128), BF), v((3, ROWS, 128), BF),
            v((16, D), F32), v((48, 128), F32), v((16, D), F32), v((8, D), F32), v((16, D), F32), v((3, 16, D), F32),
            v((3, 16, D), F32), v((16, 8, 128), F32), v((32, 8, 128), F32),
            v((3 * D, D), BF), v((D, D), BF), v((D, D), BF), v((2 * D, D), BF), v((D, D), BF), v((D, FF), BF),
            v((FF, D), BF),
            v((D, N), BF), v((3 * D, N), BF), v((D, N), F32), v((N, D), F32), v((D, N), BF), v((D, N), BF),
            v((D, N), BF), v((2 * D, N), BF), v((2 * D, N), BF), v((D, N), F32),
            v((D, N), BF), v((FF, N), BF), v((N, FF), BF), v((N, D), BF), v((N, D), F32), v((N, D), BF),
            v((D, N), BF), v((2 * D, N), BF), v((2 * D, N), BF), v((D, D), F32),
            v((2, N, N), BF), v((2, N, 128), BF), v((2, N, N // 2), F32), v((HEADS, N), F32), v((HEADS, N), F32), v((32, N), BF), v((32, N), BF), v((32, N), BF),
            v((2, TILE, D), BF), v((2, TILE, D), F32), v((N, D), BF), v((N, D), BF), v((8, 128), F32),
            dma((n_out, 3)), dma((n_out, 3)), dma((n_out, 3)), dma((n_out, 3)), dma((n_out, 2)), dma((n_out, 2)),
            dma((n_back, 4)), dma((n_back, 4)), dma((n_back, 3)), dma((n_back, 3)), dma((n_back, 2)), dma((n_back, 2)),
            dma((2,)), dma((2,)), dma((2, 3)), dma((2, 3)), dma((15,)), dma((15,)), dma((31,)), dma((31,)),
            dma((2,)), dma((2,)), dma((2,)), dma((2,)),
        ],
        compiler_params=pltpu.CompilerParams(
            collective_id=0, has_side_effects=True, vmem_limit_bytes=63 * 1024 * 1024
        ),
        name="step",
    )(x, cot, pflat, seg)


def finish_kernel(threshold, flat, square, params, first, second, out, grad_in, *rest):
    (clip_o, vector_o, norm_o, first_o, second_o, params_o, out_o, grad_in_o) = rest[:8]
    (p, m, v, c_s, tail_p, tail_m, tail_v, tail_c, o_s, g_s, big_in, big_out, tail_in, tail_out, way_in, way_out) = rest[8:]
    size = params.shape[1]
    main = size // 1024 * 1024
    parts = 4
    rows = main // 128 // parts
    moves = []
    for i, (src, by, dst) in enumerate(((out, o_s, out_o), (grad_in, g_s, grad_in_o))):
        count = src.shape[0] // 2
        for k in range(2):
            at = pl.ds(k * count, count)
            moves.append((
                pltpu.make_async_copy(src.at[at], by.at[at], way_in.at[i, k]),
                pltpu.make_async_copy(by.at[at], dst.at[at], way_out.at[i, k]),
            ))
    for come, _ in moves:
        come.start()
    reads = []
    for i in range(parts):
        at = pl.ds(i * rows * 128, rows * 128)
        for k, (src, dst) in enumerate(((params, p), (first, m), (second, v))):
            c = pltpu.make_async_copy(
                src.at[:, at].reshape(rows, 128), dst.at[pl.ds(i * rows, rows)], big_in.at[i, k]
            )
            c.start()
            reads.append(c)
    for k, (src, dst) in enumerate(((params, tail_p), (first, tail_m), (second, tail_v))):
        c = pltpu.make_async_copy(src.at[:, pl.ds(main, size - main)], dst, tail_in.at[k])
        c.start()
        reads.append(c)
    norm = jnp.sqrt(jnp.sum(square[...], keepdims=True))
    norm_o[...] = norm
    share = jnp.minimum(1.0, threshold / norm)

    def update(grad, p_ref, m_ref, v_ref):
        clipped = grad * share
        first_new = BETA_ONE * m_ref[...] + (1.0 - BETA_ONE) * clipped
        second_new = BETA_TWO * v_ref[...] + (1.0 - BETA_TWO) * clipped * clipped
        mean_hat = first_new / (1.0 - BETA_ONE**STEP)
        square_hat = second_new / (1.0 - BETA_TWO**STEP)
        old = p_ref[...]
        p_ref[...] = old - LEARN_RATE * (mean_hat / (jnp.sqrt(square_hat) + ADAM_EPS) + DECAY_RATE * old)
        m_ref[...] = first_new
        v_ref[...] = second_new
        return clipped

    writes = []
    for i in range(parts):
        come, go = moves[i]
        come.wait()
        go.start()
        writes.append(go)
        for c in reads[3 * i : 3 * i + 3]:
            c.wait()
        here = pl.ds(i * rows, rows)
        c_s[here] = update(flat[here], p.at[here], m.at[here], v.at[here])
        at = pl.ds(i * rows * 128, rows * 128)
        for k, (src, dst) in enumerate(((c_s, clip_o), (m, first_o), (v, second_o), (p, params_o))):
            c = pltpu.make_async_copy(
                src.at[here], dst.at[:, at].reshape(rows, 128), big_out.at[i, k]
            )
            c.start()
            writes.append(c)
    for c in reads[3 * parts :]:
        c.wait()
    wide = jnp.concatenate([flat[main // 128 + i : main // 128 + i + 1] for i in range(3)], 1)
    tail_c[...] = update(wide[:, : size - main], tail_p, tail_m, tail_v)
    vector_o[...] = tail_c[...]
    for k, (src, dst) in enumerate(((tail_c, clip_o), (tail_m, first_o), (tail_v, second_o), (tail_p, params_o))):
        c = pltpu.make_async_copy(src, dst.at[:, pl.ds(main, size - main)], tail_out.at[k])
        c.start()
        writes.append(c)
    for c in writes:
        c.wait()


def finish(threshold, flat, square, params, first, second, out, grad_in):
    size = params.shape[1]
    main = size // 1024 * 1024
    dma = pltpu.SemaphoreType.DMA
    v = pltpu.VMEM
    whole = pl.BlockSpec(memory_space=v)
    hbm = pl.BlockSpec(memory_space=pl.ANY)
    shape = jax.ShapeDtypeStruct
    like = shape(params.shape, F32)
    return pl.pallas_call(
        partial(finish_kernel, threshold),
        out_shape=(
            like, shape((1, size - main), F32), shape((1, 1), F32), like, like, like, shape(out.shape, BF),
            shape(grad_in.shape, F32),
        ),
        in_specs=[whole, whole, hbm, hbm, hbm, hbm, hbm],
        out_specs=(hbm, whole, whole, hbm, hbm, hbm, hbm, hbm),
        scratch_shapes=[v((main // 128, 128), F32)] * 4 + [v((1, size - main), F32)] * 4
        + [v(out.shape, BF), v(grad_in.shape, F32)]
        + [dma((4, 3)), dma((4, 4)), dma((3,)), dma((4,)), dma((2, 2)), dma((2, 2))],
        name="finish",
    )(flat, square, params, first, second, out, grad_in)


def fast_device(frames_in, seg_ids, cotangent, params, first_moment, second_moment):
    count = lax.axis_size("frames")
    size = params.shape[1]
    pflat = jnp.pad(params, ((0, 0), (0, FLAT * 128 - size))).reshape(FLAT, 128)
    result, input_grad, flat, square, _, _ = step(frames_in[0], cotangent[0], pflat, seg_ids)
    total_params = size * count
    total_rows = frames_in.shape[1] * count
    threshold = 0.01 * math.sqrt(2.0 * total_params * total_rows)
    clipped, vector_grad, norm, first_new, second_new, new_params, result, input_grad = finish(
        threshold, flat, square, params, first_moment, second_moment, result, input_grad
    )
    return (
        result[None], input_grad[None], clipped, vector_grad, norm.reshape(()), first_new, second_new, new_params,
    )


def solution(mesh):
    placed = (
        P("branch", "frames", None),
        P(None, "frames"),
        P("branch", "frames", None),
        P("branch", "frames"),
        P("branch", "frames"),
        P("branch", "frames"),
    )
    return jax.shard_map(
        fast_device if mesh.shape["frames"] == 16 else on_device,
        mesh=mesh,
        in_specs=placed,
        out_specs=(
            P("branch", "frames", None),
            P("branch", "frames", None),
            P("branch", "frames"),
            P("branch", "frames"),
            P(),
            P("branch", "frames"),
            P("branch", "frames"),
            P("branch", "frames"),
        ),
        check_vma=False,
    )
```

```python
from functools import partial
import math

import jax
import jax.numpy as jnp
from jax import lax
from jax.experimental import pallas as pl
from jax.experimental.pallas import tpu as pltpu
from jax.sharding import PartitionSpec as P

HEADS = 8
HEAD_DIM = 48
D = 384
FF = 1536
NV = 11
STEP = 5


BETA_ONE = 0.9
BETA_TWO = 0.999
LEARN_RATE = 0.05
DECAY_RATE = 0.01
ADAM_EPS = 1e-08
NORM_EPS = 1e-05
MASKED = -1e30


def from_partner(array, axis, apart):
    return lax.ppermute(array, axis, [(i, i ^ 1 << apart) for i in range(lax.axis_size(axis))])


def layer_norm(values, gain, shift):
    centre = values - jnp.mean(values, -1, keepdims=True)
    spread = jnp.mean(centre * centre, -1, keepdims=True)
    return centre * lax.rsqrt(spread + NORM_EPS) * gain + shift


def unpack(flat, count):
    shapes = ((D, 3 * D), (D, D), (D, D), (D, 2 * D), (D, D), (D, FF), (FF, D), (NV, D))
    sliced = flat.reshape(count, flat.shape[0] // count)
    pieces = []
    offset = 0
    for rows_in, cols_out in shapes:
        width = rows_in * cols_out // count
        pieces.append(sliced[:, offset : offset + width].reshape(rows_in, cols_out))
        offset += width
    return pieces


def split_heads(tensor):
    return tensor.reshape(tensor.shape[0], HEADS, HEAD_DIM)


def matmul(left, right):
    return jnp.dot(left, right, preferred_element_type=jnp.float32)


def weight_grad(inputs, grads):
    return jnp.einsum("ri,rj->ij", inputs, grads, preferred_element_type=jnp.float32)


def back_input(grads, weight):
    return jnp.einsum("rj,ij->ri", grads, weight, preferred_element_type=jnp.float32)


def masked_scores(queries, keys_in, allowed, scale):
    scores = (
        jnp.einsum("qhe,khe->hqk", queries, keys_in, preferred_element_type=jnp.float32) * scale
    )
    return jnp.where(allowed[None], scores, MASKED)


def attend(queries, keys_in, values_in, allowed, scale):
    scores = masked_scores(queries, keys_in, allowed, scale)
    row_max = jnp.max(scores, -1, keepdims=True)
    raised = jnp.exp(scores - row_max)
    row_sum = jnp.sum(raised, -1, keepdims=True)
    weights = (raised / row_sum).astype(jnp.bfloat16)
    output = jnp.einsum("hqk,khe->qhe", weights, values_in, preferred_element_type=jnp.float32)
    return (output, row_max + jnp.log(row_sum))


def attend_back(queries, keys_in, values_in, allowed, scale, log_sum, grad_out):
    probs = jnp.exp(masked_scores(queries, keys_in, allowed, scale) - log_sum)
    grad_probs = jnp.einsum("qhe,khe->hqk", grad_out, values_in, preferred_element_type=jnp.float32)
    grad_values = jnp.einsum(
        "hqk,qhe->khe", probs.astype(jnp.bfloat16), grad_out, preferred_element_type=jnp.float32
    )
    centred = grad_probs - jnp.sum(probs * grad_probs, -1, keepdims=True)
    grad_scores = (probs * centred).astype(jnp.bfloat16)
    grad_queries = (
        jnp.einsum("hqk,khe->qhe", grad_scores, keys_in, preferred_element_type=jnp.float32) * scale
    )
    grad_keys = (
        jnp.einsum("hqk,qhe->khe", grad_scores, queries, preferred_element_type=jnp.float32) * scale
    )
    return (
        grad_queries.astype(jnp.bfloat16),
        grad_keys.astype(jnp.bfloat16),
        grad_values.astype(jnp.bfloat16),
    )


def on_device(frames_in, seg_ids, cotangent, params, first_moment, second_moment):
    frames = frames_in[0].astype(jnp.float32)
    rows = frames.shape[0]
    count = lax.axis_size("frames")
    side = lax.axis_index("branch")
    own_seg = jnp.where(side == 0, seg_ids[0], seg_ids[1])
    far_seg = jnp.where(side == 0, seg_ids[1], seg_ids[0])
    self_mask = own_seg[:, None] == own_seg[None, :]
    cross_mask = own_seg[:, None] == far_seg[None, :]
    scale = 1.0 / math.sqrt(HEAD_DIM)
    shard16 = params.astype(jnp.bfloat16)
    whole = lax.all_gather(shard16, "frames", axis=1, tiled=True)[0]
    w_qkv, w_self, w_query, w_keyval, w_cross, w_up, w_down, vec16 = unpack(whole, count)
    vectors = vec16.astype(jnp.float32)
    normed, norm1_back = jax.vjp(layer_norm, frames, vectors[0], vectors[1])
    normed16 = normed.astype(jnp.bfloat16)
    joined16 = matmul(normed16, w_qkv).astype(jnp.bfloat16)
    query16 = split_heads(joined16[:, :D])
    key16 = split_heads(joined16[:, D : 2 * D])
    value16 = split_heads(joined16[:, 2 * D :])
    attended, self_lse = attend(query16, key16, value16, self_mask, scale)
    attended16 = attended.reshape(rows, D).astype(jnp.bfloat16)
    self_out = matmul(attended16, w_self)
    hidden = frames + vectors[8] * self_out
    cross_in, norm2_back = jax.vjp(layer_norm, hidden, vectors[2], vectors[3])
    cross_in16 = cross_in.astype(jnp.bfloat16)
    cross_q16 = matmul(cross_in16, w_query).astype(jnp.bfloat16)
    source, norm3_back = jax.vjp(layer_norm, hidden, vectors[4], vectors[5])
    source16 = source.astype(jnp.bfloat16)
    keyval16 = matmul(source16, w_keyval).astype(jnp.bfloat16)
    far_kv = from_partner(keyval16, "branch", 0)
    far_keys = split_heads(far_kv[:, :D])
    far_values = split_heads(far_kv[:, D:])
    cross_heads = split_heads(cross_q16)
    mixed, cross_lse = attend(cross_heads, far_keys, far_values, cross_mask, scale)
    mixed16 = mixed.reshape(rows, D).astype(jnp.bfloat16)
    cross_out = matmul(mixed16, w_cross)
    second_h = hidden + vectors[9] * cross_out
    ffn_in, norm4_back = jax.vjp(layer_norm, second_h, vectors[6], vectors[7])
    ffn_in16 = ffn_in.astype(jnp.bfloat16)
    pre_act = matmul(ffn_in16, w_up)
    activated, gelu_back = jax.vjp(partial(jax.nn.gelu, approximate=False), pre_act)
    activated16 = activated.astype(jnp.bfloat16)
    ffn_out = matmul(activated16, w_down)
    result = second_h + vectors[10] * ffn_out
    grad_out = cotangent[0].astype(jnp.float32)
    grad_ls3 = jnp.sum(grad_out * ffn_out, 0)
    grad_ffn16 = (grad_out * vectors[10]).astype(jnp.bfloat16)
    grad_down = weight_grad(activated16, grad_ffn16)
    grad_act = back_input(grad_ffn16, w_down)
    grad_pre16 = gelu_back(grad_act)[0].astype(jnp.bfloat16)
    grad_up = weight_grad(ffn_in16, grad_pre16)
    grad_h2_ln, grad_g4, grad_c4 = norm4_back(back_input(grad_pre16, w_up))
    grad_h2 = grad_out + grad_h2_ln
    grad_ls2 = jnp.sum(grad_h2 * cross_out, 0)
    grad_cross16 = (grad_h2 * vectors[9]).astype(jnp.bfloat16)
    grad_wcross = weight_grad(mixed16, grad_cross16)
    grad_mixed16 = back_input(grad_cross16, w_cross).astype(jnp.bfloat16)
    grad_cq16, grad_far_keys, grad_far_values = attend_back(
        cross_heads, far_keys, far_values, cross_mask, scale, cross_lse, split_heads(grad_mixed16)
    )
    returned = jnp.concatenate(
        [grad_far_keys.reshape(rows, D), grad_far_values.reshape(rows, D)], 1
    )
    grad_keyval16 = from_partner(returned, "branch", 0)
    grad_wkeyval = weight_grad(source16, grad_keyval16)
    grad_h_kv, grad_g3, grad_c3 = norm3_back(back_input(grad_keyval16, w_keyval))
    grad_cq_flat = grad_cq16.reshape(rows, D)
    grad_wquery = weight_grad(cross_in16, grad_cq_flat)
    grad_h_q, grad_g2, grad_c2 = norm2_back(back_input(grad_cq_flat, w_query))
    grad_hidden = grad_h2 + grad_h_q + grad_h_kv
    grad_ls1 = jnp.sum(grad_hidden * self_out, 0)
    grad_self16 = (grad_hidden * vectors[8]).astype(jnp.bfloat16)
    grad_wself = weight_grad(attended16, grad_self16)
    grad_att16 = back_input(grad_self16, w_self).astype(jnp.bfloat16)
    grad_q16, grad_k16, grad_v16 = attend_back(
        query16, key16, value16, self_mask, scale, self_lse, split_heads(grad_att16)
    )
    grad_joined16 = jnp.concatenate(
        [grad_q16.reshape(rows, D), grad_k16.reshape(rows, D), grad_v16.reshape(rows, D)], 1
    )
    grad_wqkv = weight_grad(normed16, grad_joined16)
    grad_x_ln, grad_g1, grad_c1 = norm1_back(back_input(grad_joined16, w_qkv))
    input_grad = grad_hidden + grad_x_ln
    grad_vectors = jnp.stack(
        [
            grad_g1,
            grad_c1,
            grad_g2,
            grad_c2,
            grad_g3,
            grad_c3,
            grad_g4,
            grad_c4,
            grad_ls1,
            grad_ls2,
            grad_ls3,
        ]
    )
    pieces = [
        grad_wqkv,
        grad_wself,
        grad_wquery,
        grad_wkeyval,
        grad_wcross,
        grad_up,
        grad_down,
        grad_vectors,
    ]
    flat_grad = jnp.concatenate([piece.reshape(count, -1) for piece in pieces], 1).reshape(1, -1)
    reduced = lax.psum_scatter(flat_grad, "frames", scatter_dimension=1, tiled=True)
    local_square = jnp.sum(reduced * reduced)
    square_sum = lax.psum(local_square, ("branch", "frames"))
    grad_norm = jnp.sqrt(square_sum)
    total_params = params.shape[1] * count
    total_rows = rows * count
    threshold = 0.01 * math.sqrt(2.0 * total_params * total_rows)
    clipped = reduced * jnp.minimum(1.0, threshold / grad_norm)
    vec_width = NV * D // count
    vector_grad = clipped[:, clipped.shape[1] - vec_width :]
    first_new = BETA_ONE * first_moment + (1.0 - BETA_ONE) * clipped
    second_new = BETA_TWO * second_moment + (1.0 - BETA_TWO) * clipped * clipped
    mean_hat = first_new / (1.0 - BETA_ONE**STEP)
    square_hat = second_new / (1.0 - BETA_TWO**STEP)
    new_params = params - LEARN_RATE * (
        mean_hat / (jnp.sqrt(square_hat) + ADAM_EPS) + DECAY_RATE * params
    )
    return (
        result.astype(jnp.bfloat16)[None],
        input_grad[None],
        clipped,
        vector_grad,
        grad_norm,
        first_new,
        second_new,
        new_params,
    )


MESH = pl.DeviceIdType.MESH
BF = jnp.bfloat16
F32 = jnp.float32
C2 = math.log2(math.e) / math.sqrt(HEAD_DIM)
SCALE = 1.0 / math.sqrt(HEAD_DIM)
N = 1024
TILE = 512
TILES = N // TILE
LEAD = 16
DOWN = LEAD + 36 * 24
ROWS = DOWN + 288
FLAT = 1160
QKV, SELF, QUERY, KEYVAL, CROSS, UP = (0, 9), (216, 3), (288, 3), (360, 6), (504, 3), (576, 12)
ORDER = [e for s in range(3) for e in ((QKV, s), (QKV, 3 + s), (QKV, 6 + s), (SELF, s))]
ORDER += [(m, c) for m in (QUERY, KEYVAL, CROSS, UP) for c in range(m[1])]
OUT_PIECES = ((0, 112), (112, 96), (208, 96), (304, 288), (592, 288), (880, 128), (1008, 160))
BACK_PIECES = ((880, 288), (592, 288), (304, 288), (16, 96), (112, 96), (208, 96))


def remote(src, dst, send, recv, **device):
    return pltpu.make_async_remote_copy(
        src_ref=src, dst_ref=dst, send_sem=send, recv_sem=recv, device_id=device, device_id_type=MESH
    )


def mm(a, b):
    return lax.dot_general(a, b, (((1,), (0,)), ((), ())), preferred_element_type=F32)


def mm_nt(a, b):
    return lax.dot_general(a, b, (((1,), (1,)), ((), ())), preferred_element_type=F32)


def loop(start, stop, body):
    lax.fori_loop(start, stop, lambda i, _: (body(i), 0)[1], 0)


def rows_at(i, size):
    return pl.ds(pl.multiple_of(i * size, size), size)


def normalise(values):
    centre = values - jnp.mean(values, -1, keepdims=True)
    scale = lax.rsqrt(jnp.mean(centre * centre, -1, keepdims=True) + NORM_EPS)
    return centre * scale, scale


def normalise_back(unit, scale, grad):
    return scale * (grad - jnp.mean(grad, -1, keepdims=True) - unit * jnp.mean(grad * unit, -1, keepdims=True))


def att_back_head(q, k, v, o, do, e, inv, e_turned, ds_turned):
    n = k.shape[1]
    values = jnp.concatenate([v, v, jnp.ones((32, n), BF)], 0).T
    do = do.astype(F32)
    minus = -jnp.sum(do * o, 0, keepdims=True) * inv
    do = do * inv
    high = do.astype(BF)
    low = (do - high.astype(F32)).astype(BF)
    minus_high = minus.astype(BF).astype(F32)
    row = lax.broadcasted_iota(jnp.int32, (32, n), 0)
    extra = jnp.where(row == 0, minus_high, jnp.where(row == 1, minus - minus_high, 0.0)).astype(BF)
    grads = jnp.concatenate([high, low, extra], 0)
    e_turned[...] = e.T
    ds = (e.astype(F32) * mm(values, grads)).astype(BF)
    ds_turned[...] = ds.T
    dq = mm(k, ds)
    dk = mm(q, ds_turned[...])
    dv = mm(high, e_turned[...])
    return (dq * SCALE).astype(BF), (dk * SCALE).astype(BF), dv.astype(BF)


def step_kernel(*refs):
    it = iter(refs)
    (x_hbm, cot_hbm, params, seg) = (next(it) for _ in range(4))
    (out_hbm, gin_hbm, flat, norm, e1_hbm, e2_hbm) = (next(it) for _ in range(6))
    (net, r1, s2, r2, vec, vflat, vg, vg0, vsum, vr1, vr2, late, nb) = (next(it) for _ in range(13))
    (wqkv, wself, wquery, wkv, wcross, wup, wdown) = (next(it) for _ in range(7))
    (at, qkv, o1, h, n2t, n3t, cq, kv, far, o2) = (next(it) for _ in range(10))
    (n4t, zt, du, dffn, dh, dcr, dot, dkv, dkv_far, gself) = (next(it) for _ in range(10))
    (ring, keys, scores, inv1, inv2, hot1, hot2, mask, stage16, stage32, x, cot, sq, praw) = (next(it) for _ in range(14))
    (as1, ar1, as2, ar2, as3, ar3, bs1, br1, bs2, br2, bs3, br3, ks, kr, vs, vr, ls, lr, ns, nr, es, os, gs, xs) = (
        next(it) for _ in range(24)
    )
    j = lax.axis_index("frames")
    b = lax.axis_index("branch")
    z, p = j // 4, j % 4

    def zp(k):
        return (z + k) % 4 * 4 + p

    def pp(k):
        return z * 4 + (p + k) % 4

    bar = pltpu.get_barrier_semaphore()
    for k in (1, 2, 3):
        pl.semaphore_signal(bar, inc=1, device_id={"frames": zp(k)}, device_id_type=MESH)
        pl.semaphore_signal(bar, inc=1, device_id={"frames": pp(k)}, device_id_type=MESH)
    for k in range(4):
        pl.semaphore_signal(bar, inc=1, device_id={"branch": 1 - b, "frames": pp(k)}, device_id_type=MESH)

    x_copy = pltpu.make_async_copy(x_hbm, x, xs.at[0])
    cot_copy = pltpu.make_async_copy(cot_hbm, cot, xs.at[1])
    main = params.shape[1] // 1024 * 1024
    urgent = SELF[0] + 24 * SELF[1]
    spans = ((0, urgent * 128), (urgent * 128, params.shape[1] - urgent * 128))
    p_copies = [
        pltpu.make_async_copy(params.at[:, pl.ds(*span)], praw.at[:, pl.ds(*span)], xs.at[2 + i])
        for i, span in enumerate(spans)
    ]

    pflat = flat

    def lay_out(i):
        pflat[rows_at(i, 8), :] = praw[:, pl.ds(pl.multiple_of(i * 1024, 1024), 1024)].reshape(8, 128)

    for c in (*p_copies, x_copy):
        c.start()

    def pack_pairs(start, stop):
        for m in range(start, stop):
            pair = [pflat[pl.ds(mat[0] + c, 24, stride=mat[1]), :] for mat, c in ORDER[2 * m : 2 * m + 2]]
            net[z, p, pl.ds(LEAD + 48 * m, 48), :] = jnp.concatenate(pair, 0).astype(BF)

    p_copies[0].wait()
    loop(0, urgent // 8, lay_out)
    p_copies[1].wait()
    tail = jnp.concatenate([praw[:, main:], jnp.zeros((1, 120), F32)], 1)
    tail = [tail[:, 128 * i : 128 * i + 128] for i in range(3)]
    net[z, p, pl.ds(0, 16), :] = jnp.concatenate(tail + [jnp.zeros((13, 128), F32)], 0).astype(BF)
    pack_pairs(0, 2)
    pl.semaphore_wait(bar, 10)

    others = (1, 2, 3)

    beside = (p + 1 - 2 * (p % 2), (p + 2) % 4, 3 - p)
    turned = len(OUT_PIECES) - 1

    def a1(i, k):
        part = net.at[z, slice(None) if i == turned else p, pl.ds(*OUT_PIECES[i])]
        return remote(part, part, as1.at[i, k - 1], ar1.at[i, k - 1], frames=zp(k))

    def a2(i, k):
        part = net.at[z if i == turned else slice(None), p, pl.ds(*OUT_PIECES[i])]
        return remote(part, part, as2.at[i, k], ar2.at[i, k], frames=z * 4 + beside[k])

    def a3(i, k):
        first, count = OUT_PIECES[i]
        part = net.at[z if i == turned else slice(None), beside[k], pl.ds(first + k * (count // 2), count // 2)]
        return remote(part, part, as3.at[i, k], ar3.at[i, k], frames=z * 4 + beside[1 - k])

    direct = len(BACK_PIECES) - 1

    def b1(i, k):
        first, count = BACK_PIECES[i]
        if i == direct:
            rows = pl.ds(first, count)
            return remote(
                net.at[:, beside[k], rows], r1.at[k, :, rows], bs1.at[i, k], br1.at[i, k], frames=z * 4 + beside[k]
            )
        way, across = k % 2, k // 2
        rows = pl.ds(first + way * (count // 2), count // 2)
        return remote(
            net.at[:, beside[2 if across else way], rows], r1.at[across, :, rows], bs1.at[i, k], br1.at[i, k],
            frames=z * 4 + beside[way],
        )

    def b3(i, k):
        first, count = BACK_PIECES[i]
        rows = pl.ds(first + k * (count // 2), count // 2)
        part = net.at[:, beside[1 - k], rows]
        return remote(part, r1.at[2, :, rows], bs3.at[i, k], br3.at[i, k], frames=z * 4 + beside[1 - k])

    def back_ways(i):
        return range(3 if i == direct else 4)

    def b2(i, k):
        rows = pl.ds(*BACK_PIECES[i])
        return remote(s2.at[k - 1, rows], r2.at[k - 1, rows], bs2.at[i, k - 1], br2.at[i, k - 1], frames=zp(k))

    def out_first(i):
        if i == turned:
            for k in range(2):
                a3(i, k).wait_recv()
        for k in others:
            a1(i, k).start()

    def out_second(i):
        if i != turned:
            for k in others:
                a1(i, k).wait_recv()
        for k in range(2 if i else 3):
            a2(i, k).start()

    def out_third(i):
        for k in range(2):
            a2(i, k).wait_recv()
        for k in range(2):
            a3(i, k).start()

    def out_ready(i):
        if i == turned:
            for k in others:
                a1(i, k).wait_recv()
            return
        for k in range(2 if i else 3):
            (a3 if i else a2)(i, k).wait_recv()

    def back_first(i):
        for k in back_ways(i):
            b1(i, k).start()

    def back_middle(i):
        first, count = BACK_PIECES[i]
        for k in back_ways(i):
            b1(i, k).wait_recv()
        for k in range(2):
            rows = pl.ds(first + k * (count // 2), count // 2)
            to = beside[1 - k]
            for q in range(4):
                net[q, to, rows, :] = (net[q, to, rows, :].astype(F32) + r1[1, q, rows, :].astype(F32)).astype(BF)
            b3(i, k).start()

    def plane_sum(i, to):
        rows = pl.ds(*BACK_PIECES[i])
        total = net[to, p, rows, :].astype(F32) + r1[0, to, rows, :].astype(F32) + r1[2, to, rows, :].astype(F32)
        return total + r1[1, to, rows, :].astype(F32) if i == direct else total

    def back_second(i):
        rows = pl.ds(*BACK_PIECES[i])
        if i == direct:
            for k in back_ways(i):
                b1(i, k).wait_recv()
        else:
            for k in range(2):
                b3(i, k).wait_recv()
        for k in others:
            s2[k - 1, rows, :] = plane_sum(i, (z + k) % 4).astype(BF)
            b2(i, k).start()

    def back_ready(i):
        first, count = BACK_PIECES[i]
        for k in others:
            b2(i, k).wait_recv()
        total = plane_sum(i, z)
        for k in range(3):
            total = total + r2[k, pl.ds(first, count), :].astype(F32)
        if first == DOWN:
            for c in range(3):
                flat[pl.ds(864 + c, 96, stride=3), :] = total[96 * c : 96 * c + 96]
        else:
            for c in range(count // 24):
                mat, col = ORDER[(first - LEAD) // 24 + c]
                flat[pl.ds(mat[0] + col, 24, stride=mat[1]), :] = total[24 * c : 24 * c + 24]
        sq[...] += jnp.sum((total * total).reshape(count // 8, 8, 128), 0)

    def block_pair(m):
        got = net[:, :, pl.ds(LEAD + 48 * m, 48), :].astype(F32).reshape(16, 48, 128)
        return got[:, :24].reshape(384, 128).astype(BF), got[:, 24:].reshape(384, 128).astype(BF)

    weights = {QKV: wqkv, SELF: wself, QUERY: wquery, KEYVAL: wkv, CROSS: wcross, UP: wup}

    def unpack_pairs(start, stop):
        for m in range(start, stop):
            for (mat, c), block in zip(ORDER[2 * m : 2 * m + 2], block_pair(m)):
                if mat in (QKV, QUERY, KEYVAL):
                    weights[mat][pl.ds(128 * c, 128), :] = block.T
                else:
                    weights[mat][:, pl.ds(128 * c, 128)] = block

    def put_pair(first_row, left, right):
        both = jnp.concatenate([left.reshape(16, 24, 128), right.reshape(16, 24, 128)], 1)
        net[:, :, pl.ds(first_row, 48), :] = both.astype(BF).reshape(4, 4, 48, 128)

    out_first(0)
    loop(urgent // 8, main // 1024, lay_out)
    for c in range(3):
        net[z, p, pl.ds(DOWN + 96 * c, 96), :] = pflat[pl.ds(864 + c, 96, stride=3), :].astype(BF)
    out_second(turned)
    pack_pairs(2, 6)
    out_first(1)
    out_first(2)
    pack_pairs(6, 18)
    own = seg[pl.ds(b, 1), :]
    other = seg[pl.ds(1 - b, 1), :]
    number = lax.broadcasted_iota(jnp.int32, (32, N), 0)
    same = number + 4 * j == own
    hot1[...] = jnp.where(same, 1.0, 0.0).astype(BF)
    hot2[...] = jnp.where(number + 4 * j == other, 1.0, 0.0).astype(BF)
    mask[...] = jnp.where(same | (number >= 4), 0.0, MASKED).astype(BF)
    vg[...] = jnp.zeros((16, D), F32)
    vg0[...] = jnp.zeros((8, D), F32)
    sq[...] = jnp.zeros((8, 128), F32)
    out_third(turned)
    out_second(0)
    out_first(3)
    out_second(1)
    out_second(2)
    out_ready(0)

    vflat[...] = jnp.zeros((48, 128), F32)
    lane = lax.broadcasted_iota(jnp.int32, (8, 128), 1)
    sub = lax.broadcasted_iota(jnp.int32, (8, 128), 0)
    for i in range(16):
        got = net[i // 4, i % 4, pl.ds(0, 16), :].astype(F32)[:8]
        got = jnp.where(sub * 128 + lane < 264, got, 0.0)
        if i:
            got = pltpu.roll(got, 8 * i, 1)
            got = jnp.where(lane < 8 * i, pltpu.roll(got, 1, 0), got)
        vflat[pl.ds(2 * i, 8), :] += got
    for c in range(3):
        vec[:, pl.ds(128 * c, 128)] = vflat[pl.ds(c, 16, stride=3), :]
    unpack_pairs(0, 2)

    def vector(i):
        return vec[pl.ds(i, 1), :]

    def add_vector(i, grad):
        vg[pl.ds(i, 1), :] += jnp.sum(grad, 0, keepdims=True)

    def first_norm(t):
        rows = rows_at(t, TILE)
        unit, _ = normalise(x[rows, :].astype(F32))
        at[:, rows] = (unit * vector(0) + vector(1)).astype(BF).T

    x_copy.wait()
    cot_copy.start()
    loop(0, TILES, first_norm)

    def project(w, n_ref, to):
        def part(i):
            rows = rows_at(i, D)
            to[rows, :] = mm(w[rows, :], n_ref[...]).astype(BF)

        loop(0, to.shape[0] // D, part)


    def project_round(i):
        parts = [pl.ds(D * m + 128 * i, 128) for m in range(3)]
        got = mm(jnp.concatenate([wqkv[part, :] for part in parts], 0), at[...]).astype(BF)
        for m, part in enumerate(parts):
            qkv[part, :] = got[128 * m : 128 * m + 128]

    project_round(0)

    def head(ref, first, i):
        return ref[pl.ds(pl.multiple_of(first + i * 48, 16), 48), :]

    def set_head(ref, first, i, value):
        ref[pl.ds(pl.multiple_of(first + i * 48, 16), 48), :] = value

    def e_out(e_hbm, i):
        return pltpu.make_async_copy(ring.at[i % 2], e_hbm.at[i], es.at[i % 2])

    def e_in(e_hbm, i):
        return pltpu.make_async_copy(e_hbm.at[i], ring.at[i % 2], es.at[i % 2])

    half, chunk = N // 2, 256

    def attend(q, kvs, kfirst, hot, o_ref, inv_ref, e_hbm, before):
        def make_keys(i):
            k32 = head(kvs, kfirst, i).astype(F32) * C2
            high = k32.astype(BF)
            low = (k32 - high.astype(F32)).astype(BF)
            keys[i % 2] = jnp.concatenate([high, low, hot[...]], 0).T

        def make_queries(i, t):
            at_t = slice(t * half, (t + 1) * half)
            mine = q[pl.ds(pl.multiple_of(i * 48, 16), 48), at_t]
            return jnp.concatenate([mine, mine, mask[:, at_t]], 0)

        def score(i, t, c, queries, top):
            rows = slice(c * chunk, (c + 1) * chunk)
            got = mm(keys[i % 2, rows, :], queries)
            scores[t, rows, :] = got
            got = jnp.max(got.reshape(chunk // 8, 8, half), 0)
            return got if c == 0 else jnp.maximum(top, got)

        make_keys(0)
        top = None
        queries = make_queries(0, 0)
        for c in range(N // chunk):
            top = score(0, 0, c, queries, top)

        def one(i, top):
            after = jnp.minimum(i + 1, HEADS - 1)
            @pl.when(i >= 2)
            def _():
                e_out(e_hbm, i - 2).wait()

            values = jnp.concatenate([head(kvs, kfirst + D, i), jnp.ones((16, N), BF)], 0)
            for t in range(2):
                if t:
                    before(i)
                    make_keys(after)
                next_head, next_half = (after, 0) if t else (i, 1)
                peak = jnp.max(top, 0, keepdims=True)
                queries = make_queries(next_head, next_half)
                at_t = slice(t * half, (t + 1) * half)
                o = jnp.zeros((64, half), F32)
                for c in range(N // chunk):
                    rows = slice(c * chunk, (c + 1) * chunk)
                    top = score(next_head, next_half, c, queries, top)
                    e = jnp.exp2(scores[t, rows, :] - peak).astype(BF)
                    ring[i % 2, rows, at_t] = e
                    o = o + mm(values[:, rows], e)
                inv = 1.0 / o[48:49]
                o_ref[pl.ds(pl.multiple_of(i * 48, 16), 48), at_t] = o[:48] * inv
                inv_ref[pl.ds(i, 1), at_t] = inv
            e_out(e_hbm, i).start()
            return top

        lax.fori_loop(0, HEADS, one, top)
        for i in (6, 7):
            e_out(e_hbm, i).wait()

    def attend_back(q, kvs, kfirst, o_ref, inv_ref, e_hbm, dk_ref, dfirst, before):
        e_in(e_hbm, 0).start()

        def one(i):
            @pl.when(i + 1 < HEADS)
            def _():
                e_in(e_hbm, i + 1).start()

            before(i)
            e_in(e_hbm, i).wait()
            dq, dk, dv = att_back_head(
                head(q, 0, i), head(kvs, kfirst, i), head(kvs, kfirst + D, i), head(o_ref, 0, i), head(dot, 0, i),
                ring[i % 2], inv_ref[pl.ds(i, 1), :], zt.at[pl.ds(0, N)], du.at[:, pl.ds(0, N)],
            )
            set_head(q, 0, i, dq)
            set_head(dk_ref, dfirst, i, dk)
            set_head(dk_ref, dfirst + D, i, dv)

        loop(0, HEADS, one)

    def at_head(i, **steps):
        for name, step in steps.items():
            pl.when(i == int(name[1:]))(step)

    def second_round():
        out_ready(1)
        out_third(2)
        unpack_pairs(2, 4)
        project_round(1)

    def third_round():
        out_ready(2)
        unpack_pairs(4, 6)
        project_round(2)

    def steps(*calls):
        def run():
            for f, i in calls:
                f(i)

        return run

    attend(
        qkv, qkv, D, hot1, o1, inv1, e1_hbm,
        lambda i: at_head(
            i, h0=steps((out_third, 1), (out_second, 3), (out_first, 4)), h1=second_round,
            h2=steps((out_first, 5), (out_first, turned)), h4=third_round, h5=steps((out_third, 3), (out_second, 4)),
        ),
    )
    out_ready(3)
    unpack_pairs(6, 12)

    def second_norm(t):
        rows = rows_at(t, TILE)
        self_out = mm(o1[:, rows].astype(BF).T, wself[...])
        hidden = x[rows, :].astype(F32) + vector(8) * self_out
        h[rows, :] = hidden
        unit, _ = normalise(hidden)
        n2t[:, rows] = (unit * vector(2) + vector(3)).astype(BF).T
        n3t[:, rows] = (unit * vector(4) + vector(5)).astype(BF).T

    loop(0, TILES, second_norm)
    project(wkv, n3t, kv)
    send_kv = remote(kv, far, ks.at[0], kr.at[0], branch=1 - b)
    send_kv.start()
    project(wquery, n2t, cq)
    send_kv.wait_recv()
    attend(
        cq, far, 0, hot2, o2, inv2, e2_hbm,
        lambda i: at_head(i, h1=steps((out_third, 4), (out_second, 5)), h5=steps((out_third, 5))),
    )
    out_ready(4)
    unpack_pairs(12, 18)
    out_ready(5)
    out_ready(turned)
    for c in range(3):
        wdown[:, pl.ds(128 * c, 128)] = net[:, :, pl.ds(DOWN + 96 * c, 96), :].reshape(1536, 128)
    for i in range(len(OUT_PIECES)):
        for k in others:
            a1(i, k).wait_send()
        for k in range(2 if i else 3):
            a2(i, k).wait_send()
            if i:
                a3(i, k).wait_send()

    def out_copy(t):
        return pltpu.make_async_copy(stage16.at[t % 2], out_hbm.at[rows_at(t, TILE)], os.at[t % 2])

    def feed_forward(t):
        rows = rows_at(t, TILE)
        cross_out = mm(o2[:, rows].astype(BF).T, wcross[...])
        second_h = h[rows, :] + vector(9) * cross_out
        unit, scale = normalise(second_h)
        n4 = (unit * vector(6) + vector(7)).astype(BF)
        n4t[:, rows] = n4.T
        grad_out = cot[rows, :].astype(F32)
        dffn16 = (grad_out * vector(10)).astype(BF)
        dffn[rows, :] = dffn16
        ffn_out = jnp.zeros((TILE, D), F32)
        dn4 = jnp.zeros((TILE, D), F32)
        for c in range(4):
            part = slice(c * D, (c + 1) * D)
            u = mm(n4, wup[:, part])
            share = 0.5 * (1.0 + lax.erf(u * math.sqrt(0.5)))
            slope = share + u * (jnp.exp(-0.5 * u * u) * (1.0 / math.sqrt(2.0 * math.pi)))
            z16 = (u * share).astype(BF)
            zt[part, rows] = z16.T
            ffn_out = ffn_out + mm(z16, wdown[part, :])
            du16 = (mm_nt(dffn16, wdown[part, :]) * slope).astype(BF)
            du[rows, part] = du16
            dn4 = dn4 + mm_nt(du16, wup[:, part])

        @pl.when(t >= 2)
        def _():
            out_copy(t - 2).wait()

        stage16[t % 2] = (second_h + vector(10) * ffn_out).astype(BF)
        out_copy(t).start()
        add_vector(10, grad_out * ffn_out)
        add_vector(6, dn4 * unit)
        add_vector(7, dn4)
        dh2 = grad_out + normalise_back(unit, scale, dn4 * vector(6))
        dh[rows, :] = dh2
        add_vector(9, dh2 * cross_out)
        dcross16 = (dh2 * vector(9)).astype(BF)
        dcr[rows, :] = dcross16
        dot[:, rows] = mm_nt(wcross[...], dcross16).astype(BF)

    cot_copy.wait()
    loop(0, TILES, feed_forward)
    for i in (TILES - 2, TILES - 1):
        out_copy(i).wait()

    def down_grad(i):
        grad = mm(zt[rows_at(i, D), :], dffn[...])
        for c in range(3):
            net[i, :, pl.ds(DOWN + 96 * c, 96), :] = grad[:, 128 * c : 128 * c + 128].astype(BF).reshape(4, 96, 128)

    loop(0, 4, down_grad)
    back_first(0)

    def up_grad(i):
        grad = mm(n4t[...], du[:, rows_at(i, 256)])
        put_pair(pl.multiple_of(LEAD + 24 * 24 + 48 * i, 16), grad[:, :128], grad[:, 128:])

    loop(0, 6, up_grad)
    back_first(1)
    attend_back(
        cq, far, 0, o2, inv2, e2_hbm, dkv, 0, lambda i: at_head(i, h4=lambda: back_middle(0), h7=lambda: back_middle(1))
    )
    send_dkv = remote(dkv, dkv_far, ks.at[1], kr.at[1], branch=1 - b)
    send_dkv.start()
    back_second(0)
    g_query = mm_nt(n2t[...], cq[...])
    g_cross = mm(o2[...].astype(BF), dcr[...])
    put_pair(LEAD + 24 * 12, g_query[:, :128], g_query[:, 128:256])
    put_pair(LEAD + 24 * 22, g_cross[:, 128:256], g_cross[:, 256:])
    send_dkv.wait_recv()

    def third_back(t):
        rows = rows_at(t, TILE)
        dn2 = mm(cq[:, rows].T, wquery[...])
        dn3 = mm(dkv_far[:, rows].T, wkv[...])
        unit, scale = normalise(h[rows, :])
        add_vector(2, dn2 * unit)
        add_vector(3, dn2)
        add_vector(4, dn3 * unit)
        add_vector(5, dn3)
        hidden_grad = dh[rows, :] + normalise_back(unit, scale, dn2 * vector(2) + dn3 * vector(4))
        dh[rows, :] = hidden_grad
        self_out = mm(o1[:, rows].astype(BF).T, wself[...])
        add_vector(8, hidden_grad * self_out)
        dself16 = (hidden_grad * vector(8)).astype(BF)
        dcr[rows, :] = dself16
        dot[:, rows] = mm_nt(wself[...], dself16).astype(BF)

    g_kv = mm_nt(n3t[...], dkv_far[...])
    put_pair(LEAD + 24 * 14, g_query[:, 256:], g_kv[:, :128])
    put_pair(LEAD + 24 * 16, g_kv[:, 128:256], g_kv[:, 256:384])
    put_pair(LEAD + 24 * 18, g_kv[:, 384:512], g_kv[:, 512:640])
    put_pair(LEAD + 24 * 20, g_kv[:, 640:], g_cross[:, :128])
    back_first(2)
    back_second(1)
    loop(0, TILES, third_back)
    gself[...] = mm(o1[...].astype(BF), dcr[...])
    back_ready(0)

    def v1(k):
        return remote(vg, vr1.at[k - 1], vs.at[0, k - 1], vr.at[0, k - 1], frames=pp(k))

    def v2(k):
        return remote(vsum, vr2.at[k - 1], vs.at[1, k - 1], vr.at[1, k - 1], frames=zp(k))

    for k in others:
        v1(k).start()

    def round_grad(i):
        g = [mm_nt(at[...], qkv[pl.ds(D * m + 128 * i, 128), :]) for m in range(3)]
        put_pair(LEAD + 96 * i, g[0], g[1])
        put_pair(LEAD + 96 * i + 48, g[2], gself[:, 128 * i : 128 * i + 128])
        back_first(3 + i)

    def vectors_on():
        for k in others:
            v1(k).wait_recv()
        vsum[...] = vg[...] + vr1[0] + vr1[1] + vr1[2]
        for k in others:
            v2(k).start()

    def vectors_there():
        for k in others:
            v2(k).wait_recv()
        total = vsum[...] + vr2[0] + vr2[1] + vr2[2]
        for c in range(3):
            vflat[pl.ds(c, 16, stride=3), :] = total[:, 128 * c : 128 * c + 128]

    def ahead(i):
        @pl.when(i == 2)
        def _():
            back_middle(2)
            back_ready(1)

        @pl.when(i == 3)
        def _():
            round_grad(0)
            vectors_on()

        @pl.when(i == 4)
        def _():
            back_second(2)

        @pl.when(i == 5)
        def _():
            back_middle(3)
            vectors_there()

        @pl.when(i == 6)
        def _():
            round_grad(1)

        @pl.when(i == 7)
        def _():
            back_second(3)
            back_middle(4)
            back_ready(2)

    attend_back(qkv, qkv, D, o1, inv1, e1_hbm, qkv, D, ahead)
    round_grad(2)
    back_second(4)

    def gin_copy(t):
        return pltpu.make_async_copy(stage32.at[t % 2], gin_hbm.at[rows_at(t, TILE)], gs.at[t % 2])

    def first_back(t):
        rows = rows_at(t, TILE)
        dn1 = mm(qkv[:, rows].T, wqkv[...])
        unit, scale = normalise(x[rows, :].astype(F32))
        vg0[0:1, :] += jnp.sum(dn1 * unit, 0, keepdims=True)
        vg0[1:2, :] += jnp.sum(dn1, 0, keepdims=True)

        @pl.when(t >= 2)
        def _():
            gin_copy(t - 2).wait()

        stage32[t % 2] = dh[rows, :] + normalise_back(unit, scale, dn1 * vector(0))
        gin_copy(t).start()

    loop(0, TILES, first_back)
    blocks = [vg0[r : r + 1, 128 * c : 128 * c + 128] for r in range(2) for c in range(3)]
    late[pl.ds(j, 1)] = jnp.concatenate(blocks + [jnp.zeros((2, 128), F32)], 0)[None]

    def far_vector(k):
        return remote(late.at[j], late.at[j], ls.at[k - 1], lr.at[k - 1], frames=(j + k) % 16)

    for k in range(1, 16):
        far_vector(k).start()
    back_second(5)
    back_ready(3)
    back_ready(4)
    for k in range(1, 16):
        far_vector(k).wait_recv()
    vflat[pl.ds(0, 8), :] += jnp.sum(late[...], 0)
    near = vflat[pl.ds(2 * j, 8), :]
    turn = (128 - 8 * j) % 128
    near = pltpu.roll(near, turn, 1)
    near = jnp.where(lane < 128 - 8 * j, near, pltpu.roll(near, 7, 0))
    near = jnp.where(sub * 128 + lane < 264, near, 0.0)
    flat[pl.ds(1152, 8), :] = near
    back_ready(5)
    squares = sq[...] + near * near
    me = 16 * b + j
    nb[pl.ds(me, 1), 0:1, :] = jnp.sum(squares, 0, keepdims=True)[None]

    def far_square(k):
        to = (me + k) % 32
        part = nb.at[me, pl.ds(0, 1)]
        return remote(part, part, ns.at[k - 1], nr.at[k - 1], branch=to // 16, frames=to % 16)

    for k in range(1, 32):
        far_square(k).start()
    for k in range(1, 32):
        far_square(k).wait_recv()
    norm[...] = jnp.sum(nb[:, 0, :], 0, keepdims=True)
    for i in range(len(BACK_PIECES)):
        for k in others:
            b2(i, k).wait_send()
        for k in back_ways(i):
            b1(i, k).wait_send()
        if i != direct:
            for k in range(2):
                b3(i, k).wait_send()
    for k in others:
        v1(k).wait_send()
        v2(k).wait_send()
    for k in range(1, 16):
        far_vector(k).wait_send()
    for k in range(1, 32):
        far_square(k).wait_send()
    send_kv.wait_send()
    send_dkv.wait_send()
    for i in (TILES - 2, TILES - 1):
        gin_copy(i).wait()


def step(x, cot, params, seg):
    dma = pltpu.SemaphoreType.DMA
    v = pltpu.VMEM
    whole = pl.BlockSpec(memory_space=v)
    hbm = pl.BlockSpec(memory_space=pl.ANY)
    shape = jax.ShapeDtypeStruct
    n_out, n_back = len(OUT_PIECES), len(BACK_PIECES)
    return pl.pallas_call(
        step_kernel,
        out_shape=(
            shape((N, D), BF), shape((N, D), F32), shape((FLAT, 128), F32), shape((1, 128), F32),
            shape((HEADS, N, N), BF), shape((HEADS, N, N), BF),
        ),
        in_specs=[hbm, hbm, hbm, whole],
        out_specs=(hbm, hbm, whole, whole, hbm, hbm),
        scratch_shapes=[
            v((4, 4, ROWS, 128), BF), v((3, 4, ROWS, 128), BF), v((3, ROWS, 128), BF), v((3, ROWS, 128), BF),
            v((16, D), F32), v((48, 128), F32), v((16, D), F32), v((8, D), F32), v((16, D), F32), v((3, 16, D), F32),
            v((3, 16, D), F32), v((16, 8, 128), F32), v((32, 8, 128), F32),
            v((3 * D, D), BF), v((D, D), BF), v((D, D), BF), v((2 * D, D), BF), v((D, D), BF), v((D, FF), BF),
            v((FF, D), BF),
            v((D, N), BF), v((3 * D, N), BF), v((D, N), F32), v((N, D), F32), v((D, N), BF), v((D, N), BF),
            v((D, N), BF), v((2 * D, N), BF), v((2 * D, N), BF), v((D, N), F32),
            v((D, N), BF), v((FF, N), BF), v((N, FF), BF), v((N, D), BF), v((N, D), F32), v((N, D), BF),
            v((D, N), BF), v((2 * D, N), BF), v((2 * D, N), BF), v((D, D), F32),
            v((2, N, N), BF), v((2, N, 128), BF), v((2, N, N // 2), F32), v((HEADS, N), F32), v((HEADS, N), F32), v((32, N), BF), v((32, N), BF), v((32, N), BF),
            v((2, TILE, D), BF), v((2, TILE, D), F32), v((N, D), BF), v((N, D), BF), v((8, 128), F32),
            v(params.shape, F32),
            dma((n_out, 3)), dma((n_out, 3)), dma((n_out, 3)), dma((n_out, 3)), dma((n_out, 2)), dma((n_out, 2)),
            dma((n_back, 4)), dma((n_back, 4)), dma((n_back, 3)), dma((n_back, 3)), dma((n_back, 2)), dma((n_back, 2)),
            dma((2,)), dma((2,)), dma((2, 3)), dma((2, 3)), dma((15,)), dma((15,)), dma((31,)), dma((31,)),
            dma((2,)), dma((2,)), dma((2,)), dma((5,)),
        ],
        compiler_params=pltpu.CompilerParams(
            collective_id=0, has_side_effects=True, vmem_limit_bytes=63 * 1024 * 1024
        ),
        name="step",
    )(x, cot, params, seg)


def finish_kernel(threshold, flat, square, params, first, second, out, grad_in, *rest):
    (clip_o, vector_o, norm_o, first_o, second_o, params_o, out_o, grad_in_o) = rest[:8]
    (p, m, v, c_s, tail_p, tail_m, tail_v, tail_c, o_s, g_s, big_in, big_out, tail_in, tail_out, way_in, way_out) = rest[8:]
    size = params.shape[1]
    main = size // 1024 * 1024
    parts = 4
    rows = main // 128 // parts
    moves = []
    for i, (src, by, dst) in enumerate(((out, o_s, out_o), (grad_in, g_s, grad_in_o))):
        count = src.shape[0] // 2
        for k in range(2):
            at = pl.ds(k * count, count)
            moves.append((
                pltpu.make_async_copy(src.at[at], by.at[at], way_in.at[i, k]),
                pltpu.make_async_copy(by.at[at], dst.at[at], way_out.at[i, k]),
            ))
    for come, _ in moves:
        come.start()
    reads = []
    for i in range(parts):
        at = pl.ds(i * rows * 128, rows * 128)
        for k, (src, dst) in enumerate(((params, p), (first, m), (second, v))):
            c = pltpu.make_async_copy(
                src.at[:, at].reshape(rows, 128), dst.at[pl.ds(i * rows, rows)], big_in.at[i, k]
            )
            c.start()
            reads.append(c)
    for k, (src, dst) in enumerate(((params, tail_p), (first, tail_m), (second, tail_v))):
        c = pltpu.make_async_copy(src.at[:, pl.ds(main, size - main)], dst, tail_in.at[k])
        c.start()
        reads.append(c)
    norm = jnp.sqrt(jnp.sum(square[...], keepdims=True))
    norm_o[...] = norm
    share = jnp.minimum(1.0, threshold / norm)

    def update(grad, p_ref, m_ref, v_ref):
        clipped = grad * share
        first_new = BETA_ONE * m_ref[...] + (1.0 - BETA_ONE) * clipped
        second_new = BETA_TWO * v_ref[...] + (1.0 - BETA_TWO) * clipped * clipped
        mean_hat = first_new / (1.0 - BETA_ONE**STEP)
        square_hat = second_new / (1.0 - BETA_TWO**STEP)
        old = p_ref[...]
        p_ref[...] = old - LEARN_RATE * (mean_hat / (jnp.sqrt(square_hat) + ADAM_EPS) + DECAY_RATE * old)
        m_ref[...] = first_new
        v_ref[...] = second_new
        return clipped

    writes = []
    for i in range(parts):
        come, go = moves[i]
        come.wait()
        go.start()
        writes.append(go)
        for c in reads[3 * i : 3 * i + 3]:
            c.wait()
        here = pl.ds(i * rows, rows)
        c_s[here] = update(flat[here], p.at[here], m.at[here], v.at[here])
        at = pl.ds(i * rows * 128, rows * 128)
        for k, (src, dst) in enumerate(((c_s, clip_o), (m, first_o), (v, second_o), (p, params_o))):
            c = pltpu.make_async_copy(
                src.at[here], dst.at[:, at].reshape(rows, 128), big_out.at[i, k]
            )
            c.start()
            writes.append(c)
    for c in reads[3 * parts :]:
        c.wait()
    wide = jnp.concatenate([flat[main // 128 + i : main // 128 + i + 1] for i in range(3)], 1)
    tail_c[...] = update(wide[:, : size - main], tail_p, tail_m, tail_v)
    vector_o[...] = tail_c[...]
    for k, (src, dst) in enumerate(((tail_c, clip_o), (tail_m, first_o), (tail_v, second_o), (tail_p, params_o))):
        c = pltpu.make_async_copy(src, dst.at[:, pl.ds(main, size - main)], tail_out.at[k])
        c.start()
        writes.append(c)
    for c in writes:
        c.wait()


def finish(threshold, flat, square, params, first, second, out, grad_in):
    size = params.shape[1]
    main = size // 1024 * 1024
    dma = pltpu.SemaphoreType.DMA
    v = pltpu.VMEM
    whole = pl.BlockSpec(memory_space=v)
    hbm = pl.BlockSpec(memory_space=pl.ANY)
    shape = jax.ShapeDtypeStruct
    like = shape(params.shape, F32)
    return pl.pallas_call(
        partial(finish_kernel, threshold),
        out_shape=(
            like, shape((1, size - main), F32), shape((1, 1), F32), like, like, like, shape(out.shape, BF),
            shape(grad_in.shape, F32),
        ),
        in_specs=[whole, whole, hbm, hbm, hbm, hbm, hbm],
        out_specs=(hbm, whole, whole, hbm, hbm, hbm, hbm, hbm),
        scratch_shapes=[v((main // 128, 128), F32)] * 4 + [v((1, size - main), F32)] * 4
        + [v(out.shape, BF), v(grad_in.shape, F32)]
        + [dma((4, 3)), dma((4, 4)), dma((3,)), dma((4,)), dma((2, 2)), dma((2, 2))],
        name="finish",
    )(flat, square, params, first, second, out, grad_in)


def fast_device(frames_in, seg_ids, cotangent, params, first_moment, second_moment):
    count = lax.axis_size("frames")
    size = params.shape[1]
    result, input_grad, flat, square, _, _ = step(frames_in[0], cotangent[0], params, seg_ids)
    total_params = size * count
    total_rows = frames_in.shape[1] * count
    threshold = 0.01 * math.sqrt(2.0 * total_params * total_rows)
    clipped, vector_grad, norm, first_new, second_new, new_params, result, input_grad = finish(
        threshold, flat, square, params, first_moment, second_moment, result, input_grad
    )
    return (
        result[None], input_grad[None], clipped, vector_grad, norm.reshape(()), first_new, second_new, new_params,
    )


def solution(mesh):
    placed = (
        P("branch", "frames", None),
        P(None, "frames"),
        P("branch", "frames", None),
        P("branch", "frames"),
        P("branch", "frames"),
        P("branch", "frames"),
    )
    return jax.shard_map(
        fast_device if mesh.shape["frames"] == 16 else on_device,
        mesh=mesh,
        in_specs=placed,
        out_specs=(
            P("branch", "frames", None),
            P("branch", "frames", None),
            P("branch", "frames"),
            P("branch", "frames"),
            P(),
            P("branch", "frames"),
            P("branch", "frames"),
            P("branch", "frames"),
        ),
        check_vma=False,
    )
```

```python
from functools import partial
import math

import jax
import jax.numpy as jnp
from jax import lax
from jax.experimental import pallas as pl
from jax.experimental.pallas import tpu as pltpu
from jax.sharding import PartitionSpec as P

HEADS = 8
HEAD_DIM = 48
D = 384
FF = 1536
NV = 11
STEP = 5


BETA_ONE = 0.9
BETA_TWO = 0.999
LEARN_RATE = 0.05
DECAY_RATE = 0.01
ADAM_EPS = 1e-08
NORM_EPS = 1e-05
MASKED = -1e30


def from_partner(array, axis, apart):
    return lax.ppermute(array, axis, [(i, i ^ 1 << apart) for i in range(lax.axis_size(axis))])


def layer_norm(values, gain, shift):
    centre = values - jnp.mean(values, -1, keepdims=True)
    spread = jnp.mean(centre * centre, -1, keepdims=True)
    return centre * lax.rsqrt(spread + NORM_EPS) * gain + shift


def unpack(flat, count):
    shapes = ((D, 3 * D), (D, D), (D, D), (D, 2 * D), (D, D), (D, FF), (FF, D), (NV, D))
    sliced = flat.reshape(count, flat.shape[0] // count)
    pieces = []
    offset = 0
    for rows_in, cols_out in shapes:
        width = rows_in * cols_out // count
        pieces.append(sliced[:, offset : offset + width].reshape(rows_in, cols_out))
        offset += width
    return pieces


def split_heads(tensor):
    return tensor.reshape(tensor.shape[0], HEADS, HEAD_DIM)


def matmul(left, right):
    return jnp.dot(left, right, preferred_element_type=jnp.float32)


def weight_grad(inputs, grads):
    return jnp.einsum("ri,rj->ij", inputs, grads, preferred_element_type=jnp.float32)


def back_input(grads, weight):
    return jnp.einsum("rj,ij->ri", grads, weight, preferred_element_type=jnp.float32)


def masked_scores(queries, keys_in, allowed, scale):
    scores = (
        jnp.einsum("qhe,khe->hqk", queries, keys_in, preferred_element_type=jnp.float32) * scale
    )
    return jnp.where(allowed[None], scores, MASKED)


def attend(queries, keys_in, values_in, allowed, scale):
    scores = masked_scores(queries, keys_in, allowed, scale)
    row_max = jnp.max(scores, -1, keepdims=True)
    raised = jnp.exp(scores - row_max)
    row_sum = jnp.sum(raised, -1, keepdims=True)
    weights = (raised / row_sum).astype(jnp.bfloat16)
    output = jnp.einsum("hqk,khe->qhe", weights, values_in, preferred_element_type=jnp.float32)
    return (output, row_max + jnp.log(row_sum))


def attend_back(queries, keys_in, values_in, allowed, scale, log_sum, grad_out):
    probs = jnp.exp(masked_scores(queries, keys_in, allowed, scale) - log_sum)
    grad_probs = jnp.einsum("qhe,khe->hqk", grad_out, values_in, preferred_element_type=jnp.float32)
    grad_values = jnp.einsum(
        "hqk,qhe->khe", probs.astype(jnp.bfloat16), grad_out, preferred_element_type=jnp.float32
    )
    centred = grad_probs - jnp.sum(probs * grad_probs, -1, keepdims=True)
    grad_scores = (probs * centred).astype(jnp.bfloat16)
    grad_queries = (
        jnp.einsum("hqk,khe->qhe", grad_scores, keys_in, preferred_element_type=jnp.float32) * scale
    )
    grad_keys = (
        jnp.einsum("hqk,qhe->khe", grad_scores, queries, preferred_element_type=jnp.float32) * scale
    )
    return (
        grad_queries.astype(jnp.bfloat16),
        grad_keys.astype(jnp.bfloat16),
        grad_values.astype(jnp.bfloat16),
    )


def on_device(frames_in, seg_ids, cotangent, params, first_moment, second_moment):
    frames = frames_in[0].astype(jnp.float32)
    rows = frames.shape[0]
    count = lax.axis_size("frames")
    side = lax.axis_index("branch")
    own_seg = jnp.where(side == 0, seg_ids[0], seg_ids[1])
    far_seg = jnp.where(side == 0, seg_ids[1], seg_ids[0])
    self_mask = own_seg[:, None] == own_seg[None, :]
    cross_mask = own_seg[:, None] == far_seg[None, :]
    scale = 1.0 / math.sqrt(HEAD_DIM)
    shard16 = params.astype(jnp.bfloat16)
    whole = lax.all_gather(shard16, "frames", axis=1, tiled=True)[0]
    w_qkv, w_self, w_query, w_keyval, w_cross, w_up, w_down, vec16 = unpack(whole, count)
    vectors = vec16.astype(jnp.float32)
    normed, norm1_back = jax.vjp(layer_norm, frames, vectors[0], vectors[1])
    normed16 = normed.astype(jnp.bfloat16)
    joined16 = matmul(normed16, w_qkv).astype(jnp.bfloat16)
    query16 = split_heads(joined16[:, :D])
    key16 = split_heads(joined16[:, D : 2 * D])
    value16 = split_heads(joined16[:, 2 * D :])
    attended, self_lse = attend(query16, key16, value16, self_mask, scale)
    attended16 = attended.reshape(rows, D).astype(jnp.bfloat16)
    self_out = matmul(attended16, w_self)
    hidden = frames + vectors[8] * self_out
    cross_in, norm2_back = jax.vjp(layer_norm, hidden, vectors[2], vectors[3])
    cross_in16 = cross_in.astype(jnp.bfloat16)
    cross_q16 = matmul(cross_in16, w_query).astype(jnp.bfloat16)
    source, norm3_back = jax.vjp(layer_norm, hidden, vectors[4], vectors[5])
    source16 = source.astype(jnp.bfloat16)
    keyval16 = matmul(source16, w_keyval).astype(jnp.bfloat16)
    far_kv = from_partner(keyval16, "branch", 0)
    far_keys = split_heads(far_kv[:, :D])
    far_values = split_heads(far_kv[:, D:])
    cross_heads = split_heads(cross_q16)
    mixed, cross_lse = attend(cross_heads, far_keys, far_values, cross_mask, scale)
    mixed16 = mixed.reshape(rows, D).astype(jnp.bfloat16)
    cross_out = matmul(mixed16, w_cross)
    second_h = hidden + vectors[9] * cross_out
    ffn_in, norm4_back = jax.vjp(layer_norm, second_h, vectors[6], vectors[7])
    ffn_in16 = ffn_in.astype(jnp.bfloat16)
    pre_act = matmul(ffn_in16, w_up)
    activated, gelu_back = jax.vjp(partial(jax.nn.gelu, approximate=False), pre_act)
    activated16 = activated.astype(jnp.bfloat16)
    ffn_out = matmul(activated16, w_down)
    result = second_h + vectors[10] * ffn_out
    grad_out = cotangent[0].astype(jnp.float32)
    grad_ls3 = jnp.sum(grad_out * ffn_out, 0)
    grad_ffn16 = (grad_out * vectors[10]).astype(jnp.bfloat16)
    grad_down = weight_grad(activated16, grad_ffn16)
    grad_act = back_input(grad_ffn16, w_down)
    grad_pre16 = gelu_back(grad_act)[0].astype(jnp.bfloat16)
    grad_up = weight_grad(ffn_in16, grad_pre16)
    grad_h2_ln, grad_g4, grad_c4 = norm4_back(back_input(grad_pre16, w_up))
    grad_h2 = grad_out + grad_h2_ln
    grad_ls2 = jnp.sum(grad_h2 * cross_out, 0)
    grad_cross16 = (grad_h2 * vectors[9]).astype(jnp.bfloat16)
    grad_wcross = weight_grad(mixed16, grad_cross16)
    grad_mixed16 = back_input(grad_cross16, w_cross).astype(jnp.bfloat16)
    grad_cq16, grad_far_keys, grad_far_values = attend_back(
        cross_heads, far_keys, far_values, cross_mask, scale, cross_lse, split_heads(grad_mixed16)
    )
    returned = jnp.concatenate(
        [grad_far_keys.reshape(rows, D), grad_far_values.reshape(rows, D)], 1
    )
    grad_keyval16 = from_partner(returned, "branch", 0)
    grad_wkeyval = weight_grad(source16, grad_keyval16)
    grad_h_kv, grad_g3, grad_c3 = norm3_back(back_input(grad_keyval16, w_keyval))
    grad_cq_flat = grad_cq16.reshape(rows, D)
    grad_wquery = weight_grad(cross_in16, grad_cq_flat)
    grad_h_q, grad_g2, grad_c2 = norm2_back(back_input(grad_cq_flat, w_query))
    grad_hidden = grad_h2 + grad_h_q + grad_h_kv
    grad_ls1 = jnp.sum(grad_hidden * self_out, 0)
    grad_self16 = (grad_hidden * vectors[8]).astype(jnp.bfloat16)
    grad_wself = weight_grad(attended16, grad_self16)
    grad_att16 = back_input(grad_self16, w_self).astype(jnp.bfloat16)
    grad_q16, grad_k16, grad_v16 = attend_back(
        query16, key16, value16, self_mask, scale, self_lse, split_heads(grad_att16)
    )
    grad_joined16 = jnp.concatenate(
        [grad_q16.reshape(rows, D), grad_k16.reshape(rows, D), grad_v16.reshape(rows, D)], 1
    )
    grad_wqkv = weight_grad(normed16, grad_joined16)
    grad_x_ln, grad_g1, grad_c1 = norm1_back(back_input(grad_joined16, w_qkv))
    input_grad = grad_hidden + grad_x_ln
    grad_vectors = jnp.stack(
        [
            grad_g1,
            grad_c1,
            grad_g2,
            grad_c2,
            grad_g3,
            grad_c3,
            grad_g4,
            grad_c4,
            grad_ls1,
            grad_ls2,
            grad_ls3,
        ]
    )
    pieces = [
        grad_wqkv,
        grad_wself,
        grad_wquery,
        grad_wkeyval,
        grad_wcross,
        grad_up,
        grad_down,
        grad_vectors,
    ]
    flat_grad = jnp.concatenate([piece.reshape(count, -1) for piece in pieces], 1).reshape(1, -1)
    reduced = lax.psum_scatter(flat_grad, "frames", scatter_dimension=1, tiled=True)
    local_square = jnp.sum(reduced * reduced)
    square_sum = lax.psum(local_square, ("branch", "frames"))
    grad_norm = jnp.sqrt(square_sum)
    total_params = params.shape[1] * count
    total_rows = rows * count
    threshold = 0.01 * math.sqrt(2.0 * total_params * total_rows)
    clipped = reduced * jnp.minimum(1.0, threshold / grad_norm)
    vec_width = NV * D // count
    vector_grad = clipped[:, clipped.shape[1] - vec_width :]
    first_new = BETA_ONE * first_moment + (1.0 - BETA_ONE) * clipped
    second_new = BETA_TWO * second_moment + (1.0 - BETA_TWO) * clipped * clipped
    mean_hat = first_new / (1.0 - BETA_ONE**STEP)
    square_hat = second_new / (1.0 - BETA_TWO**STEP)
    new_params = params - LEARN_RATE * (
        mean_hat / (jnp.sqrt(square_hat) + ADAM_EPS) + DECAY_RATE * params
    )
    return (
        result.astype(jnp.bfloat16)[None],
        input_grad[None],
        clipped,
        vector_grad,
        grad_norm,
        first_new,
        second_new,
        new_params,
    )


MESH = pl.DeviceIdType.MESH
BF = jnp.bfloat16
F32 = jnp.float32
C2 = math.log2(math.e) / math.sqrt(HEAD_DIM)
SCALE = 1.0 / math.sqrt(HEAD_DIM)
N = 1024
TILE = 512
TILES = N // TILE
LEAD = 16
DOWN = LEAD + 36 * 24
ROWS = DOWN + 288
FLAT = 1160
QKV, SELF, QUERY, KEYVAL, CROSS, UP = (0, 9), (216, 3), (288, 3), (360, 6), (504, 3), (576, 12)
ORDER = [e for s in range(3) for e in ((QKV, s), (QKV, 3 + s), (QKV, 6 + s), (SELF, s))]
ORDER += [(m, c) for m in (QUERY, KEYVAL, CROSS, UP) for c in range(m[1])]
OUT_PIECES = ((0, 112), (112, 96), (208, 96), (304, 288), (592, 288), (880, 128), (1008, 160))
BACK_PIECES = ((880, 288), (592, 288), (304, 288), (16, 96), (112, 96), (208, 96))


def remote(src, dst, send, recv, **device):
    return pltpu.make_async_remote_copy(
        src_ref=src, dst_ref=dst, send_sem=send, recv_sem=recv, device_id=device, device_id_type=MESH
    )


def mm(a, b):
    return lax.dot_general(a, b, (((1,), (0,)), ((), ())), preferred_element_type=F32)


def mm_nt(a, b):
    return lax.dot_general(a, b, (((1,), (1,)), ((), ())), preferred_element_type=F32)


def loop(start, stop, body):
    lax.fori_loop(start, stop, lambda i, _: (body(i), 0)[1], 0)


def rows_at(i, size):
    return pl.ds(pl.multiple_of(i * size, size), size)


def normalise(values):
    centre = values - jnp.mean(values, -1, keepdims=True)
    scale = lax.rsqrt(jnp.mean(centre * centre, -1, keepdims=True) + NORM_EPS)
    return centre * scale, scale


def normalise_back(unit, scale, grad):
    return scale * (grad - jnp.mean(grad, -1, keepdims=True) - unit * jnp.mean(grad * unit, -1, keepdims=True))


def att_back_head(q, k, v, o, do, e, inv, e_turned, ds_turned):
    n = k.shape[1]
    values = jnp.concatenate([v, v, jnp.ones((32, n), BF)], 0).T
    do = do.astype(F32)
    minus = -jnp.sum(do * o, 0, keepdims=True) * inv
    do = do * inv
    high = do.astype(BF)
    low = (do - high.astype(F32)).astype(BF)
    minus_high = minus.astype(BF).astype(F32)
    row = lax.broadcasted_iota(jnp.int32, (32, n), 0)
    extra = jnp.where(row == 0, minus_high, jnp.where(row == 1, minus - minus_high, 0.0)).astype(BF)
    grads = jnp.concatenate([high, low, extra], 0)
    e_turned[...] = e.T
    ds = (e.astype(F32) * mm(values, grads)).astype(BF)
    ds_turned[...] = ds.T
    dq = mm(k, ds)
    dk = mm(q, ds_turned[...])
    dv = mm(high, e_turned[...])
    return (dq * SCALE).astype(BF), (dk * SCALE).astype(BF), dv.astype(BF)


def step_kernel(*refs):
    it = iter(refs)
    (x_hbm, cot_hbm, params, seg) = (next(it) for _ in range(4))
    (out_hbm, gin_hbm, flat, norm, e1_hbm, e2_hbm) = (next(it) for _ in range(6))
    (net, r1, s2, r2, vec, vflat, vg, vg0, vsum, vr1, vr2, late, nb) = (next(it) for _ in range(13))
    (wqkv, wself, wquery, wkv, wcross, wup, wdown) = (next(it) for _ in range(7))
    (at, qkv, o1, h, n2t, n3t, cq, kv, far, o2) = (next(it) for _ in range(10))
    (n4t, zt, du, dffn, dh, dcr, dot, dkv_far, gself) = (next(it) for _ in range(9))
    dkv = kv
    (ring, keys, scores, inv1, inv2, hot1, hot2, mask, stage16, x, cot, sq, praw) = (next(it) for _ in range(13))
    (as1, ar1, as2, ar2, as3, ar3, bs1, br1, bs2, br2, bs3, br3, ks, kr, vs, vr, ls, lr, ns, nr, es, os, gs, xs) = (
        next(it) for _ in range(24)
    )
    j = lax.axis_index("frames")
    b = lax.axis_index("branch")
    z, p = j // 4, j % 4

    def zp(k):
        return (z + k) % 4 * 4 + p

    def pp(k):
        return z * 4 + (p + k) % 4

    bar = pltpu.get_barrier_semaphore()
    for k in (1, 2, 3):
        pl.semaphore_signal(bar, inc=1, device_id={"frames": zp(k)}, device_id_type=MESH)
        pl.semaphore_signal(bar, inc=1, device_id={"frames": pp(k)}, device_id_type=MESH)
    for k in range(4):
        pl.semaphore_signal(bar, inc=1, device_id={"branch": 1 - b, "frames": pp(k)}, device_id_type=MESH)

    x_copy = pltpu.make_async_copy(x_hbm, x, xs.at[0])
    cot_copy = pltpu.make_async_copy(cot_hbm, cot, xs.at[1])
    main = params.shape[1] // 1024 * 1024
    urgent = SELF[0] + 24 * SELF[1]
    spans = ((0, urgent * 128), (urgent * 128, params.shape[1] - urgent * 128))
    p_copies = [
        pltpu.make_async_copy(params.at[:, pl.ds(*span)], praw.at[:, pl.ds(*span)], xs.at[2 + i])
        for i, span in enumerate(spans)
    ]

    pflat = flat

    def lay_out(i):
        pflat[rows_at(i, 8), :] = praw[:, pl.ds(pl.multiple_of(i * 1024, 1024), 1024)].reshape(8, 128)

    for c in (*p_copies, x_copy):
        c.start()

    def pack_pairs(start, stop):
        for m in range(start, stop):
            pair = [pflat[pl.ds(mat[0] + c, 24, stride=mat[1]), :] for mat, c in ORDER[2 * m : 2 * m + 2]]
            net[z, p, pl.ds(LEAD + 48 * m, 48), :] = jnp.concatenate(pair, 0).astype(BF)

    p_copies[0].wait()
    loop(0, urgent // 8, lay_out)
    p_copies[1].wait()
    tail = jnp.concatenate([praw[:, main:], jnp.zeros((1, 120), F32)], 1)
    tail = [tail[:, 128 * i : 128 * i + 128] for i in range(3)]
    net[z, p, pl.ds(0, 16), :] = jnp.concatenate(tail + [jnp.zeros((13, 128), F32)], 0).astype(BF)
    pack_pairs(0, 2)
    pl.semaphore_wait(bar, 10)

    others = (1, 2, 3)

    beside = (p + 1 - 2 * (p % 2), (p + 2) % 4, 3 - p)
    turned = len(OUT_PIECES) - 1

    def a1(i, k):
        part = net.at[z, slice(None) if i == turned else p, pl.ds(*OUT_PIECES[i])]
        return remote(part, part, as1.at[i, k - 1], ar1.at[i, k - 1], frames=zp(k))

    def a2(i, k):
        part = net.at[z if i == turned else slice(None), p, pl.ds(*OUT_PIECES[i])]
        return remote(part, part, as2.at[i, k], ar2.at[i, k], frames=z * 4 + beside[k])

    def a3(i, k):
        first, count = OUT_PIECES[i]
        part = net.at[z if i == turned else slice(None), beside[k], pl.ds(first + k * (count // 2), count // 2)]
        return remote(part, part, as3.at[i, k], ar3.at[i, k], frames=z * 4 + beside[1 - k])

    direct = len(BACK_PIECES) - 1

    def b1(i, k):
        first, count = BACK_PIECES[i]
        if i == direct:
            rows = pl.ds(first, count)
            return remote(
                net.at[:, beside[k], rows], r1.at[k, :, rows], bs1.at[i, k], br1.at[i, k], frames=z * 4 + beside[k]
            )
        way, across = k % 2, k // 2
        rows = pl.ds(first + way * (count // 2), count // 2)
        return remote(
            net.at[:, beside[2 if across else way], rows], r1.at[across, :, rows], bs1.at[i, k], br1.at[i, k],
            frames=z * 4 + beside[way],
        )

    def b3(i, k):
        first, count = BACK_PIECES[i]
        rows = pl.ds(first + k * (count // 2), count // 2)
        part = net.at[:, beside[1 - k], rows]
        return remote(part, r1.at[2, :, rows], bs3.at[i, k], br3.at[i, k], frames=z * 4 + beside[1 - k])

    def back_ways(i):
        return range(3 if i == direct else 4)

    def b2(i, k):
        rows = pl.ds(*BACK_PIECES[i])
        return remote(s2.at[k - 1, rows], r2.at[k - 1, rows], bs2.at[i, k - 1], br2.at[i, k - 1], frames=zp(k))

    def out_first(i):
        if i == turned:
            for k in range(2):
                a3(i, k).wait_recv()
        for k in others:
            a1(i, k).start()

    def out_second(i):
        if i != turned:
            for k in others:
                a1(i, k).wait_recv()
        for k in range(2 if i else 3):
            a2(i, k).start()

    def out_third(i):
        for k in range(2):
            a2(i, k).wait_recv()
        for k in range(2):
            a3(i, k).start()

    def out_ready(i):
        if i == turned:
            for k in others:
                a1(i, k).wait_recv()
            return
        for k in range(2 if i else 3):
            (a3 if i else a2)(i, k).wait_recv()

    def back_first(i):
        for k in back_ways(i):
            b1(i, k).start()

    def back_middle(i):
        first, count = BACK_PIECES[i]
        for k in back_ways(i):
            b1(i, k).wait_recv()
        for k in range(2):
            rows = pl.ds(first + k * (count // 2), count // 2)
            to = beside[1 - k]
            for q in range(4):
                net[q, to, rows, :] = (net[q, to, rows, :].astype(F32) + r1[1, q, rows, :].astype(F32)).astype(BF)
            b3(i, k).start()

    def plane_sum(i, to):
        rows = pl.ds(*BACK_PIECES[i])
        total = net[to, p, rows, :].astype(F32) + r1[0, to, rows, :].astype(F32) + r1[2, to, rows, :].astype(F32)
        return total + r1[1, to, rows, :].astype(F32) if i == direct else total

    def back_second(i):
        rows = pl.ds(*BACK_PIECES[i])
        if i == direct:
            for k in back_ways(i):
                b1(i, k).wait_recv()
        else:
            for k in range(2):
                b3(i, k).wait_recv()
        for k in others:
            s2[k - 1, rows, :] = plane_sum(i, (z + k) % 4).astype(BF)
            b2(i, k).start()

    def back_ready(i):
        first, count = BACK_PIECES[i]
        for k in others:
            b2(i, k).wait_recv()
        total = plane_sum(i, z)
        for k in range(3):
            total = total + r2[k, pl.ds(first, count), :].astype(F32)
        if first == DOWN:
            for c in range(3):
                flat[pl.ds(864 + c, 96, stride=3), :] = total[96 * c : 96 * c + 96]
        else:
            for c in range(count // 24):
                mat, col = ORDER[(first - LEAD) // 24 + c]
                flat[pl.ds(mat[0] + col, 24, stride=mat[1]), :] = total[24 * c : 24 * c + 24]
        sq[...] += jnp.sum((total * total).reshape(count // 8, 8, 128), 0)

    def block_pair(m):
        got = net[:, :, pl.ds(LEAD + 48 * m, 48), :].astype(F32).reshape(16, 48, 128)
        return got[:, :24].reshape(384, 128).astype(BF), got[:, 24:].reshape(384, 128).astype(BF)

    weights = {QKV: wqkv, SELF: wself, QUERY: wquery, KEYVAL: wkv, CROSS: wcross, UP: wup}

    def unpack_pairs(start, stop):
        for m in range(start, stop):
            for (mat, c), block in zip(ORDER[2 * m : 2 * m + 2], block_pair(m)):
                if mat in (QKV, QUERY, KEYVAL):
                    weights[mat][pl.ds(128 * c, 128), :] = block.T
                else:
                    weights[mat][:, pl.ds(128 * c, 128)] = block

    def put_pair(first_row, left, right):
        both = jnp.concatenate([left.reshape(16, 24, 128), right.reshape(16, 24, 128)], 1)
        net[:, :, pl.ds(first_row, 48), :] = both.astype(BF).reshape(4, 4, 48, 128)

    out_first(0)
    loop(urgent // 8, main // 1024, lay_out)
    for c in range(3):
        net[z, p, pl.ds(DOWN + 96 * c, 96), :] = pflat[pl.ds(864 + c, 96, stride=3), :].astype(BF)
    out_second(turned)
    pack_pairs(2, 6)
    out_first(1)
    out_first(2)
    pack_pairs(6, 18)
    own = seg[pl.ds(b, 1), :]
    other = seg[pl.ds(1 - b, 1), :]
    number = lax.broadcasted_iota(jnp.int32, (32, N), 0)
    same = number + 4 * j == own
    hot1[...] = jnp.where(same, 1.0, 0.0).astype(BF)
    hot2[...] = jnp.where(number + 4 * j == other, 1.0, 0.0).astype(BF)
    mask[...] = jnp.where(same | (number >= 4), 0.0, MASKED).astype(BF)
    vg[...] = jnp.zeros((16, D), F32)
    vg0[...] = jnp.zeros((8, D), F32)
    sq[...] = jnp.zeros((8, 128), F32)
    out_third(turned)
    out_second(0)
    out_first(3)
    out_second(1)
    out_second(2)
    out_ready(0)

    vflat[...] = jnp.zeros((48, 128), F32)
    lane = lax.broadcasted_iota(jnp.int32, (8, 128), 1)
    sub = lax.broadcasted_iota(jnp.int32, (8, 128), 0)
    for i in range(16):
        got = net[i // 4, i % 4, pl.ds(0, 16), :].astype(F32)[:8]
        got = jnp.where(sub * 128 + lane < 264, got, 0.0)
        if i:
            got = pltpu.roll(got, 8 * i, 1)
            got = jnp.where(lane < 8 * i, pltpu.roll(got, 1, 0), got)
        vflat[pl.ds(2 * i, 8), :] += got
    for c in range(3):
        vec[:, pl.ds(128 * c, 128)] = vflat[pl.ds(c, 16, stride=3), :]
    unpack_pairs(0, 2)

    def vector(i):
        return vec[pl.ds(i, 1), :]

    def add_vector(i, grad):
        vg[pl.ds(i, 1), :] += jnp.sum(grad, 0, keepdims=True)

    def first_norm(t):
        rows = rows_at(t, TILE)
        unit, _ = normalise(x[rows, :].astype(F32))
        at[:, rows] = (unit * vector(0) + vector(1)).astype(BF).T

    x_copy.wait()
    cot_copy.start()
    loop(0, TILES, first_norm)

    def project(w, n_ref, to):
        def part(i):
            rows = rows_at(i, D)
            to[rows, :] = mm(w[rows, :], n_ref[...]).astype(BF)

        loop(0, to.shape[0] // D, part)


    def project_round(i):
        parts = [pl.ds(D * m + 128 * i, 128) for m in range(3)]
        got = mm(jnp.concatenate([wqkv[part, :] for part in parts], 0), at[...]).astype(BF)
        for m, part in enumerate(parts):
            qkv[part, :] = got[128 * m : 128 * m + 128]

    project_round(0)

    def head(ref, first, i):
        return ref[pl.ds(pl.multiple_of(first + i * 48, 16), 48), :]

    def set_head(ref, first, i, value):
        ref[pl.ds(pl.multiple_of(first + i * 48, 16), 48), :] = value

    def e_out(e_hbm, i):
        return pltpu.make_async_copy(ring.at[i % 2], e_hbm.at[i], es.at[i % 2])

    def e_in(e_hbm, i):
        return pltpu.make_async_copy(e_hbm.at[i], ring.at[i % 2], es.at[i % 2])

    half, chunk = N // 2, 256

    def attend(q, kvs, kfirst, hot, o_ref, inv_ref, e_hbm, before):
        def make_keys(i):
            k32 = head(kvs, kfirst, i).astype(F32) * C2
            high = k32.astype(BF)
            low = (k32 - high.astype(F32)).astype(BF)
            keys[i % 2] = jnp.concatenate([high, low, hot[...]], 0).T

        def make_queries(i, t):
            at_t = slice(t * half, (t + 1) * half)
            mine = q[pl.ds(pl.multiple_of(i * 48, 16), 48), at_t]
            return jnp.concatenate([mine, mine, mask[:, at_t]], 0)

        def score(i, t, c, queries, top):
            rows = slice(c * chunk, (c + 1) * chunk)
            got = mm(keys[i % 2, rows, :], queries)
            scores[t, rows, :] = got
            got = jnp.max(got.reshape(chunk // 8, 8, half), 0)
            return got if c == 0 else jnp.maximum(top, got)

        make_keys(0)
        top = None
        queries = make_queries(0, 0)
        for c in range(N // chunk):
            top = score(0, 0, c, queries, top)

        def one(i, top):
            after = jnp.minimum(i + 1, HEADS - 1)
            @pl.when(i >= 2)
            def _():
                e_out(e_hbm, i - 2).wait()

            values = jnp.concatenate([head(kvs, kfirst + D, i), jnp.ones((16, N), BF)], 0)
            for t in range(2):
                if t:
                    before(i)
                    make_keys(after)
                next_head, next_half = (after, 0) if t else (i, 1)
                peak = jnp.max(top, 0, keepdims=True)
                queries = make_queries(next_head, next_half)
                at_t = slice(t * half, (t + 1) * half)
                o = jnp.zeros((64, half), F32)
                for c in range(N // chunk):
                    rows = slice(c * chunk, (c + 1) * chunk)
                    top = score(next_head, next_half, c, queries, top)
                    e = jnp.exp2(scores[t, rows, :] - peak).astype(BF)
                    ring[i % 2, rows, at_t] = e
                    o = o + mm(values[:, rows], e)
                inv = 1.0 / o[48:49]
                o_ref[pl.ds(pl.multiple_of(i * 48, 16), 48), at_t] = o[:48] * inv
                inv_ref[pl.ds(i, 1), at_t] = inv
            e_out(e_hbm, i).start()
            return top

        lax.fori_loop(0, HEADS, one, top)
        for i in (6, 7):
            e_out(e_hbm, i).wait()

    def attend_back(q, kvs, kfirst, o_ref, inv_ref, e_hbm, dk_ref, dfirst, before):
        e_in(e_hbm, 0).start()

        def one(i):
            @pl.when(i + 1 < HEADS)
            def _():
                e_in(e_hbm, i + 1).start()

            before(i)
            e_in(e_hbm, i).wait()
            dq, dk, dv = att_back_head(
                head(q, 0, i), head(kvs, kfirst, i), head(kvs, kfirst + D, i), head(o_ref, 0, i), head(dot, 0, i),
                ring[i % 2], inv_ref[pl.ds(i, 1), :], zt.at[pl.ds(0, N)], du.at[:, pl.ds(0, N)],
            )
            set_head(q, 0, i, dq)
            set_head(dk_ref, dfirst, i, dk)
            set_head(dk_ref, dfirst + D, i, dv)

        loop(0, HEADS, one)

    def at_head(i, **steps):
        for name, step in steps.items():
            pl.when(i == int(name[1:]))(step)

    def second_round():
        out_ready(1)
        out_third(2)
        unpack_pairs(2, 4)
        project_round(1)

    def third_round():
        out_ready(2)
        unpack_pairs(4, 6)
        project_round(2)

    def steps(*calls):
        def run():
            for f, i in calls:
                f(i)

        return run

    attend(
        qkv, qkv, D, hot1, o1, inv1, e1_hbm,
        lambda i: at_head(
            i, h0=steps((out_third, 1), (out_second, 3), (out_first, 4)), h1=second_round,
            h2=steps((out_first, 5), (out_first, turned)), h4=third_round, h5=steps((out_third, 3), (out_second, 4)),
        ),
    )
    out_ready(3)
    unpack_pairs(6, 12)

    def second_norm(t):
        rows = rows_at(t, TILE)
        self_out = mm(o1[:, rows].astype(BF).T, wself[...])
        hidden = x[rows, :].astype(F32) + vector(8) * self_out
        h[rows, :] = hidden
        unit, _ = normalise(hidden)
        n2t[:, rows] = (unit * vector(2) + vector(3)).astype(BF).T
        n3t[:, rows] = (unit * vector(4) + vector(5)).astype(BF).T

    loop(0, TILES, second_norm)
    project(wkv, n3t, kv)
    send_kv = remote(kv, far, ks.at[0], kr.at[0], branch=1 - b)
    send_kv.start()
    project(wquery, n2t, cq)
    send_kv.wait_recv()
    attend(
        cq, far, 0, hot2, o2, inv2, e2_hbm,
        lambda i: at_head(i, h1=steps((out_third, 4), (out_second, 5)), h5=steps((out_third, 5))),
    )
    out_ready(4)
    unpack_pairs(12, 18)
    out_ready(5)
    out_ready(turned)
    for c in range(3):
        wdown[:, pl.ds(128 * c, 128)] = net[:, :, pl.ds(DOWN + 96 * c, 96), :].reshape(1536, 128)
    send_kv.wait_send()
    for i in range(len(OUT_PIECES)):
        for k in others:
            a1(i, k).wait_send()
        for k in range(2 if i else 3):
            a2(i, k).wait_send()
            if i:
                a3(i, k).wait_send()

    def out_copy(t):
        return pltpu.make_async_copy(stage16.at[t % 2], out_hbm.at[rows_at(t, TILE)], os.at[t % 2])

    def feed_forward(t):
        rows = rows_at(t, TILE)
        cross_out = mm(o2[:, rows].astype(BF).T, wcross[...])
        second_h = h[rows, :] + vector(9) * cross_out
        unit, scale = normalise(second_h)
        n4 = (unit * vector(6) + vector(7)).astype(BF)
        n4t[:, rows] = n4.T
        grad_out = cot[rows, :].astype(F32)
        dffn16 = (grad_out * vector(10)).astype(BF)
        dffn[rows, :] = dffn16
        ffn_out = jnp.zeros((TILE, D), F32)
        dn4 = jnp.zeros((TILE, D), F32)
        for c in range(FF // 512):
            part = slice(c * 512, (c + 1) * 512)
            u = mm(n4, wup[:, part])
            share = 0.5 * (1.0 + lax.erf(u * math.sqrt(0.5)))
            slope = share + u * (jnp.exp(-0.5 * u * u) * (1.0 / math.sqrt(2.0 * math.pi)))
            z16 = (u * share).astype(BF)
            zt[part, rows] = z16.T
            ffn_out = ffn_out + mm(z16, wdown[part, :])
            du16 = (mm_nt(dffn16, wdown[part, :]) * slope).astype(BF)
            du[rows, part] = du16
            dn4 = dn4 + mm_nt(du16, wup[:, part])

        @pl.when(t >= 2)
        def _():
            out_copy(t - 2).wait()

        stage16[t % 2] = (second_h + vector(10) * ffn_out).astype(BF)
        out_copy(t).start()
        add_vector(10, grad_out * ffn_out)
        add_vector(6, dn4 * unit)
        add_vector(7, dn4)
        dh2 = grad_out + normalise_back(unit, scale, dn4 * vector(6))
        dh[rows, :] = dh2
        add_vector(9, dh2 * cross_out)
        dcross16 = (dh2 * vector(9)).astype(BF)
        dcr[rows, :] = dcross16
        dot[:, rows] = mm_nt(wcross[...], dcross16).astype(BF)

    cot_copy.wait()
    loop(0, TILES, feed_forward)
    for i in (TILES - 2, TILES - 1):
        out_copy(i).wait()

    def down_grad(i):
        grad = mm(zt[rows_at(i, D), :], dffn[...])
        for c in range(3):
            net[i, :, pl.ds(DOWN + 96 * c, 96), :] = grad[:, 128 * c : 128 * c + 128].astype(BF).reshape(4, 96, 128)

    loop(0, 4, down_grad)
    back_first(0)

    def up_grad(i):
        grad = mm(n4t[...], du[:, rows_at(i, 256)])
        put_pair(pl.multiple_of(LEAD + 24 * 24 + 48 * i, 16), grad[:, :128], grad[:, 128:])

    loop(0, 6, up_grad)
    back_first(1)
    attend_back(
        cq, far, 0, o2, inv2, e2_hbm, dkv, 0, lambda i: at_head(i, h4=lambda: back_middle(0), h7=lambda: back_middle(1))
    )
    send_dkv = remote(dkv, dkv_far, ks.at[1], kr.at[1], branch=1 - b)
    send_dkv.start()
    back_second(0)
    g_query = mm_nt(n2t[...], cq[...])
    g_cross = mm(o2[...].astype(BF), dcr[...])
    put_pair(LEAD + 24 * 12, g_query[:, :128], g_query[:, 128:256])
    put_pair(LEAD + 24 * 22, g_cross[:, 128:256], g_cross[:, 256:])
    send_dkv.wait_recv()

    def third_back(t):
        rows = rows_at(t, TILE)
        dn2 = mm(cq[:, rows].T, wquery[...])
        dn3 = mm(dkv_far[:, rows].T, wkv[...])
        unit, scale = normalise(h[rows, :])
        add_vector(2, dn2 * unit)
        add_vector(3, dn2)
        add_vector(4, dn3 * unit)
        add_vector(5, dn3)
        hidden_grad = dh[rows, :] + normalise_back(unit, scale, dn2 * vector(2) + dn3 * vector(4))
        dh[rows, :] = hidden_grad
        self_out = mm(o1[:, rows].astype(BF).T, wself[...])
        add_vector(8, hidden_grad * self_out)
        dself16 = (hidden_grad * vector(8)).astype(BF)
        dcr[rows, :] = dself16
        dot[:, rows] = mm_nt(wself[...], dself16).astype(BF)

    g_kv = mm_nt(n3t[...], dkv_far[...])
    put_pair(LEAD + 24 * 14, g_query[:, 256:], g_kv[:, :128])
    put_pair(LEAD + 24 * 16, g_kv[:, 128:256], g_kv[:, 256:384])
    put_pair(LEAD + 24 * 18, g_kv[:, 384:512], g_kv[:, 512:640])
    put_pair(LEAD + 24 * 20, g_kv[:, 640:], g_cross[:, :128])
    back_first(2)
    back_second(1)
    loop(0, TILES, third_back)
    gself[...] = mm(o1[...].astype(BF), dcr[...])
    back_ready(0)

    def v1(k):
        return remote(vg, vr1.at[k - 1], vs.at[0, k - 1], vr.at[0, k - 1], frames=pp(k))

    def v2(k):
        return remote(vsum, vr2.at[k - 1], vs.at[1, k - 1], vr.at[1, k - 1], frames=zp(k))

    for k in others:
        v1(k).start()

    def round_grad(i):
        parts = [qkv[pl.ds(D * m + 128 * i, 128), :] for m in range(3)]
        g = mm_nt(at[...], jnp.concatenate(parts, 0))
        put_pair(LEAD + 96 * i, g[:, :128], g[:, 128:256])
        put_pair(LEAD + 96 * i + 48, g[:, 256:], gself[:, 128 * i : 128 * i + 128])
        back_first(3 + i)

    def vectors_on():
        for k in others:
            v1(k).wait_recv()
        vsum[...] = vg[...] + vr1[0] + vr1[1] + vr1[2]
        for k in others:
            v2(k).start()

    def vectors_there():
        for k in others:
            v2(k).wait_recv()
        total = vsum[...] + vr2[0] + vr2[1] + vr2[2]
        for c in range(3):
            vflat[pl.ds(c, 16, stride=3), :] = total[:, 128 * c : 128 * c + 128]

    def ahead(i):
        @pl.when(i == 2)
        def _():
            back_middle(2)
            back_ready(1)

        @pl.when(i == 3)
        def _():
            round_grad(0)
            vectors_on()

        @pl.when(i == 4)
        def _():
            back_second(2)

        @pl.when(i == 5)
        def _():
            back_middle(3)
            vectors_there()

        @pl.when(i == 6)
        def _():
            round_grad(1)

        @pl.when(i == 7)
        def _():
            back_second(3)
            back_middle(4)
            back_ready(2)

    attend_back(qkv, qkv, D, o1, inv1, e1_hbm, qkv, D, ahead)
    round_grad(2)
    back_second(4)

    def gin_copy(t):
        return pltpu.make_async_copy(dh.at[rows_at(t, TILE)], gin_hbm.at[rows_at(t, TILE)], gs.at[t])

    def first_back(t):
        rows = rows_at(t, TILE)
        dn1 = mm(qkv[:, rows].T, wqkv[...])
        unit, scale = normalise(x[rows, :].astype(F32))
        vg0[0:1, :] += jnp.sum(dn1 * unit, 0, keepdims=True)
        vg0[1:2, :] += jnp.sum(dn1, 0, keepdims=True)
        dh[rows, :] = dh[rows, :] + normalise_back(unit, scale, dn1 * vector(0))
        gin_copy(t).start()

    loop(0, TILES, first_back)
    blocks = [vg0[r : r + 1, 128 * c : 128 * c + 128] for r in range(2) for c in range(3)]
    late[pl.ds(j, 1)] = jnp.concatenate(blocks + [jnp.zeros((2, 128), F32)], 0)[None]

    def far_vector(k):
        return remote(late.at[j], late.at[j], ls.at[k - 1], lr.at[k - 1], frames=(j + k) % 16)

    for k in range(1, 16):
        far_vector(k).start()
    back_second(5)
    back_ready(3)
    back_ready(4)
    for k in range(1, 16):
        far_vector(k).wait_recv()
    vflat[pl.ds(0, 8), :] += jnp.sum(late[...], 0)
    near = vflat[pl.ds(2 * j, 8), :]
    turn = (128 - 8 * j) % 128
    near = pltpu.roll(near, turn, 1)
    near = jnp.where(lane < 128 - 8 * j, near, pltpu.roll(near, 7, 0))
    near = jnp.where(sub * 128 + lane < 264, near, 0.0)
    flat[pl.ds(1152, 8), :] = near
    back_ready(5)
    squares = sq[...] + near * near
    me = 16 * b + j
    nb[pl.ds(me, 1), 0:1, :] = jnp.sum(squares, 0, keepdims=True)[None]

    def far_square(k):
        to = (me + k) % 32
        part = nb.at[me, pl.ds(0, 1)]
        return remote(part, part, ns.at[k - 1], nr.at[k - 1], branch=to // 16, frames=to % 16)

    for k in range(1, 32):
        far_square(k).start()
    for k in range(1, 32):
        far_square(k).wait_recv()
    norm[...] = jnp.sum(nb[:, 0, :], 0, keepdims=True)
    for i in range(len(BACK_PIECES)):
        for k in others:
            b2(i, k).wait_send()
        for k in back_ways(i):
            b1(i, k).wait_send()
        if i != direct:
            for k in range(2):
                b3(i, k).wait_send()
    for k in others:
        v1(k).wait_send()
        v2(k).wait_send()
    for k in range(1, 16):
        far_vector(k).wait_send()
    for k in range(1, 32):
        far_square(k).wait_send()
    send_dkv.wait_send()
    for i in range(TILES):
        gin_copy(i).wait()


def step(x, cot, params, seg):
    dma = pltpu.SemaphoreType.DMA
    v = pltpu.VMEM
    whole = pl.BlockSpec(memory_space=v)
    hbm = pl.BlockSpec(memory_space=pl.ANY)
    shape = jax.ShapeDtypeStruct
    n_out, n_back = len(OUT_PIECES), len(BACK_PIECES)
    return pl.pallas_call(
        step_kernel,
        out_shape=(
            shape((N, D), BF), shape((N, D), F32), shape((FLAT, 128), F32), shape((1, 128), F32),
            shape((HEADS, N, N), BF), shape((HEADS, N, N), BF),
        ),
        in_specs=[hbm, hbm, hbm, whole],
        out_specs=(hbm, hbm, whole, whole, hbm, hbm),
        scratch_shapes=[
            v((4, 4, ROWS, 128), BF), v((3, 4, ROWS, 128), BF), v((3, ROWS, 128), BF), v((3, ROWS, 128), BF),
            v((16, D), F32), v((48, 128), F32), v((16, D), F32), v((8, D), F32), v((16, D), F32), v((3, 16, D), F32),
            v((3, 16, D), F32), v((16, 8, 128), F32), v((32, 8, 128), F32),
            v((3 * D, D), BF), v((D, D), BF), v((D, D), BF), v((2 * D, D), BF), v((D, D), BF), v((D, FF), BF),
            v((FF, D), BF),
            v((D, N), BF), v((3 * D, N), BF), v((D, N), F32), v((N, D), F32), v((D, N), BF), v((D, N), BF),
            v((D, N), BF), v((2 * D, N), BF), v((2 * D, N), BF), v((D, N), F32),
            v((D, N), BF), v((FF, N), BF), v((N, FF), BF), v((N, D), BF), v((N, D), F32), v((N, D), BF),
            v((D, N), BF), v((2 * D, N), BF), v((D, D), F32),
            v((2, N, N), BF), v((2, N, 128), BF), v((2, N, N // 2), F32), v((HEADS, N), F32), v((HEADS, N), F32), v((32, N), BF), v((32, N), BF), v((32, N), BF),
            v((2, TILE, D), BF), v((N, D), BF), v((N, D), BF), v((8, 128), F32),
            v(params.shape, F32),
            dma((n_out, 3)), dma((n_out, 3)), dma((n_out, 3)), dma((n_out, 3)), dma((n_out, 2)), dma((n_out, 2)),
            dma((n_back, 4)), dma((n_back, 4)), dma((n_back, 3)), dma((n_back, 3)), dma((n_back, 2)), dma((n_back, 2)),
            dma((2,)), dma((2,)), dma((2, 3)), dma((2, 3)), dma((15,)), dma((15,)), dma((31,)), dma((31,)),
            dma((2,)), dma((2,)), dma((2,)), dma((5,)),
        ],
        compiler_params=pltpu.CompilerParams(
            collective_id=0, has_side_effects=True, vmem_limit_bytes=63 * 1024 * 1024
        ),
        name="step",
    )(x, cot, params, seg)


def finish_kernel(threshold, flat, square, params, first, second, out, grad_in, *rest):
    (clip_o, vector_o, norm_o, first_o, second_o, params_o, out_o, grad_in_o) = rest[:8]
    (p, m, v, c_s, tail_p, tail_m, tail_v, tail_c, o_s, g_s, big_in, big_out, tail_in, tail_out, way_in, way_out) = rest[8:]
    size = params.shape[1]
    main = size // 1024 * 1024
    parts = 4
    rows = main // 128 // parts
    moves = []
    for i, (src, by, dst) in enumerate(((out, o_s, out_o), (grad_in, g_s, grad_in_o))):
        count = src.shape[0] // 2
        for k in range(2):
            at = pl.ds(k * count, count)
            moves.append((
                pltpu.make_async_copy(src.at[at], by.at[at], way_in.at[i, k]),
                pltpu.make_async_copy(by.at[at], dst.at[at], way_out.at[i, k]),
            ))
    reads = []
    for i in range(parts):
        at = pl.ds(i * rows * 128, rows * 128)
        here = pl.ds(i * rows, rows)
        for k, (src, dst) in enumerate(((params, p), (first, m), (second, v))):
            c = pltpu.make_async_copy(src.at[:, at].reshape(rows, 128), dst.at[here], big_in.at[i, k])
            c.start()
            reads.append(c)
        moves[i][0].start()
    for k, (src, dst) in enumerate(((params, tail_p), (first, tail_m), (second, tail_v))):
        c = pltpu.make_async_copy(src.at[:, pl.ds(main, size - main)], dst, tail_in.at[k])
        c.start()
        reads.append(c)
    norm = jnp.sqrt(jnp.sum(square[...], keepdims=True))
    norm_o[...] = norm
    share = jnp.minimum(1.0, threshold / norm)

    def update(grad, p_ref, m_ref, v_ref):
        clipped = grad * share
        first_new = BETA_ONE * m_ref[...] + (1.0 - BETA_ONE) * clipped
        second_new = BETA_TWO * v_ref[...] + (1.0 - BETA_TWO) * clipped * clipped
        mean_hat = first_new / (1.0 - BETA_ONE**STEP)
        square_hat = second_new / (1.0 - BETA_TWO**STEP)
        old = p_ref[...]
        p_ref[...] = old - LEARN_RATE * (mean_hat / (jnp.sqrt(square_hat) + ADAM_EPS) + DECAY_RATE * old)
        m_ref[...] = first_new
        v_ref[...] = second_new
        return clipped

    writes = []
    for i in range(parts):
        for c in reads[3 * i : 3 * i + 3]:
            c.wait()
        here = pl.ds(i * rows, rows)
        c_s[here] = update(flat[here], p.at[here], m.at[here], v.at[here])
        at = pl.ds(i * rows * 128, rows * 128)
        for k, (src, dst) in enumerate(((c_s, clip_o), (m, first_o), (v, second_o), (p, params_o))):
            c = pltpu.make_async_copy(
                src.at[here], dst.at[:, at].reshape(rows, 128), big_out.at[i, k]
            )
            c.start()
            writes.append(c)
        come, go = moves[i]
        come.wait()
        go.start()
        writes.append(go)
    for c in reads[3 * parts :]:
        c.wait()
    wide = jnp.concatenate([flat[main // 128 + i : main // 128 + i + 1] for i in range(3)], 1)
    tail_c[...] = update(wide[:, : size - main], tail_p, tail_m, tail_v)
    vector_o[...] = tail_c[...]
    for k, (src, dst) in enumerate(((tail_c, clip_o), (tail_m, first_o), (tail_v, second_o), (tail_p, params_o))):
        c = pltpu.make_async_copy(src, dst.at[:, pl.ds(main, size - main)], tail_out.at[k])
        c.start()
        writes.append(c)
    for c in writes:
        c.wait()


def finish(threshold, flat, square, params, first, second, out, grad_in):
    size = params.shape[1]
    main = size // 1024 * 1024
    dma = pltpu.SemaphoreType.DMA
    v = pltpu.VMEM
    whole = pl.BlockSpec(memory_space=v)
    hbm = pl.BlockSpec(memory_space=pl.ANY)
    shape = jax.ShapeDtypeStruct
    like = shape(params.shape, F32)
    return pl.pallas_call(
        partial(finish_kernel, threshold),
        out_shape=(
            like, shape((1, size - main), F32), shape((1, 1), F32), like, like, like, shape(out.shape, BF),
            shape(grad_in.shape, F32),
        ),
        in_specs=[whole, whole, hbm, hbm, hbm, hbm, hbm],
        out_specs=(hbm, whole, whole, hbm, hbm, hbm, hbm, hbm),
        scratch_shapes=[v((main // 128, 128), F32)] * 4 + [v((1, size - main), F32)] * 4
        + [v(out.shape, BF), v(grad_in.shape, F32)]
        + [dma((4, 3)), dma((4, 4)), dma((3,)), dma((4,)), dma((2, 2)), dma((2, 2))],
        name="finish",
    )(flat, square, params, first, second, out, grad_in)


def fast_device(frames_in, seg_ids, cotangent, params, first_moment, second_moment):
    count = lax.axis_size("frames")
    size = params.shape[1]
    result, input_grad, flat, square, _, _ = step(frames_in[0], cotangent[0], params, seg_ids)
    total_params = size * count
    total_rows = frames_in.shape[1] * count
    threshold = 0.01 * math.sqrt(2.0 * total_params * total_rows)
    clipped, vector_grad, norm, first_new, second_new, new_params, result, input_grad = finish(
        threshold, flat, square, params, first_moment, second_moment, result, input_grad
    )
    return (
        result[None], input_grad[None], clipped, vector_grad, norm.reshape(()), first_new, second_new, new_params,
    )


def solution(mesh):
    placed = (
        P("branch", "frames", None),
        P(None, "frames"),
        P("branch", "frames", None),
        P("branch", "frames"),
        P("branch", "frames"),
        P("branch", "frames"),
    )
    return jax.shard_map(
        fast_device if mesh.shape["frames"] == 16 else on_device,
        mesh=mesh,
        in_specs=placed,
        out_specs=(
            P("branch", "frames", None),
            P("branch", "frames", None),
            P("branch", "frames"),
            P("branch", "frames"),
            P(),
            P("branch", "frames"),
            P("branch", "frames"),
            P("branch", "frames"),
        ),
        check_vma=False,
    )
```

```python
from functools import partial
import math

import jax
import jax.numpy as jnp
from jax import lax
from jax.experimental import pallas as pl
from jax.experimental.pallas import tpu as pltpu
from jax.sharding import PartitionSpec as P

HEADS = 8
HEAD_DIM = 48
D = 384
FF = 1536
NV = 11
STEP = 5


BETA_ONE = 0.9
BETA_TWO = 0.999
LEARN_RATE = 0.05
DECAY_RATE = 0.01
ADAM_EPS = 1e-08
NORM_EPS = 1e-05
MASKED = -1e30


def from_partner(array, axis, apart):
    return lax.ppermute(array, axis, [(i, i ^ 1 << apart) for i in range(lax.axis_size(axis))])


def layer_norm(values, gain, shift):
    centre = values - jnp.mean(values, -1, keepdims=True)
    spread = jnp.mean(centre * centre, -1, keepdims=True)
    return centre * lax.rsqrt(spread + NORM_EPS) * gain + shift


def unpack(flat, count):
    shapes = ((D, 3 * D), (D, D), (D, D), (D, 2 * D), (D, D), (D, FF), (FF, D), (NV, D))
    sliced = flat.reshape(count, flat.shape[0] // count)
    pieces = []
    offset = 0
    for rows_in, cols_out in shapes:
        width = rows_in * cols_out // count
        pieces.append(sliced[:, offset : offset + width].reshape(rows_in, cols_out))
        offset += width
    return pieces


def split_heads(tensor):
    return tensor.reshape(tensor.shape[0], HEADS, HEAD_DIM)


def matmul(left, right):
    return jnp.dot(left, right, preferred_element_type=jnp.float32)


def weight_grad(inputs, grads):
    return jnp.einsum("ri,rj->ij", inputs, grads, preferred_element_type=jnp.float32)


def back_input(grads, weight):
    return jnp.einsum("rj,ij->ri", grads, weight, preferred_element_type=jnp.float32)


def masked_scores(queries, keys_in, allowed, scale):
    scores = (
        jnp.einsum("qhe,khe->hqk", queries, keys_in, preferred_element_type=jnp.float32) * scale
    )
    return jnp.where(allowed[None], scores, MASKED)


def attend(queries, keys_in, values_in, allowed, scale):
    scores = masked_scores(queries, keys_in, allowed, scale)
    row_max = jnp.max(scores, -1, keepdims=True)
    raised = jnp.exp(scores - row_max)
    row_sum = jnp.sum(raised, -1, keepdims=True)
    weights = (raised / row_sum).astype(jnp.bfloat16)
    output = jnp.einsum("hqk,khe->qhe", weights, values_in, preferred_element_type=jnp.float32)
    return (output, row_max + jnp.log(row_sum))


def attend_back(queries, keys_in, values_in, allowed, scale, log_sum, grad_out):
    probs = jnp.exp(masked_scores(queries, keys_in, allowed, scale) - log_sum)
    grad_probs = jnp.einsum("qhe,khe->hqk", grad_out, values_in, preferred_element_type=jnp.float32)
    grad_values = jnp.einsum(
        "hqk,qhe->khe", probs.astype(jnp.bfloat16), grad_out, preferred_element_type=jnp.float32
    )
    centred = grad_probs - jnp.sum(probs * grad_probs, -1, keepdims=True)
    grad_scores = (probs * centred).astype(jnp.bfloat16)
    grad_queries = (
        jnp.einsum("hqk,khe->qhe", grad_scores, keys_in, preferred_element_type=jnp.float32) * scale
    )
    grad_keys = (
        jnp.einsum("hqk,qhe->khe", grad_scores, queries, preferred_element_type=jnp.float32) * scale
    )
    return (
        grad_queries.astype(jnp.bfloat16),
        grad_keys.astype(jnp.bfloat16),
        grad_values.astype(jnp.bfloat16),
    )


def on_device(frames_in, seg_ids, cotangent, params, first_moment, second_moment):
    frames = frames_in[0].astype(jnp.float32)
    rows = frames.shape[0]
    count = lax.axis_size("frames")
    side = lax.axis_index("branch")
    own_seg = jnp.where(side == 0, seg_ids[0], seg_ids[1])
    far_seg = jnp.where(side == 0, seg_ids[1], seg_ids[0])
    self_mask = own_seg[:, None] == own_seg[None, :]
    cross_mask = own_seg[:, None] == far_seg[None, :]
    scale = 1.0 / math.sqrt(HEAD_DIM)
    shard16 = params.astype(jnp.bfloat16)
    whole = lax.all_gather(shard16, "frames", axis=1, tiled=True)[0]
    w_qkv, w_self, w_query, w_keyval, w_cross, w_up, w_down, vec16 = unpack(whole, count)
    vectors = vec16.astype(jnp.float32)
    normed, norm1_back = jax.vjp(layer_norm, frames, vectors[0], vectors[1])
    normed16 = normed.astype(jnp.bfloat16)
    joined16 = matmul(normed16, w_qkv).astype(jnp.bfloat16)
    query16 = split_heads(joined16[:, :D])
    key16 = split_heads(joined16[:, D : 2 * D])
    value16 = split_heads(joined16[:, 2 * D :])
    attended, self_lse = attend(query16, key16, value16, self_mask, scale)
    attended16 = attended.reshape(rows, D).astype(jnp.bfloat16)
    self_out = matmul(attended16, w_self)
    hidden = frames + vectors[8] * self_out
    cross_in, norm2_back = jax.vjp(layer_norm, hidden, vectors[2], vectors[3])
    cross_in16 = cross_in.astype(jnp.bfloat16)
    cross_q16 = matmul(cross_in16, w_query).astype(jnp.bfloat16)
    source, norm3_back = jax.vjp(layer_norm, hidden, vectors[4], vectors[5])
    source16 = source.astype(jnp.bfloat16)
    keyval16 = matmul(source16, w_keyval).astype(jnp.bfloat16)
    far_kv = from_partner(keyval16, "branch", 0)
    far_keys = split_heads(far_kv[:, :D])
    far_values = split_heads(far_kv[:, D:])
    cross_heads = split_heads(cross_q16)
    mixed, cross_lse = attend(cross_heads, far_keys, far_values, cross_mask, scale)
    mixed16 = mixed.reshape(rows, D).astype(jnp.bfloat16)
    cross_out = matmul(mixed16, w_cross)
    second_h = hidden + vectors[9] * cross_out
    ffn_in, norm4_back = jax.vjp(layer_norm, second_h, vectors[6], vectors[7])
    ffn_in16 = ffn_in.astype(jnp.bfloat16)
    pre_act = matmul(ffn_in16, w_up)
    activated, gelu_back = jax.vjp(partial(jax.nn.gelu, approximate=False), pre_act)
    activated16 = activated.astype(jnp.bfloat16)
    ffn_out = matmul(activated16, w_down)
    result = second_h + vectors[10] * ffn_out
    grad_out = cotangent[0].astype(jnp.float32)
    grad_ls3 = jnp.sum(grad_out * ffn_out, 0)
    grad_ffn16 = (grad_out * vectors[10]).astype(jnp.bfloat16)
    grad_down = weight_grad(activated16, grad_ffn16)
    grad_act = back_input(grad_ffn16, w_down)
    grad_pre16 = gelu_back(grad_act)[0].astype(jnp.bfloat16)
    grad_up = weight_grad(ffn_in16, grad_pre16)
    grad_h2_ln, grad_g4, grad_c4 = norm4_back(back_input(grad_pre16, w_up))
    grad_h2 = grad_out + grad_h2_ln
    grad_ls2 = jnp.sum(grad_h2 * cross_out, 0)
    grad_cross16 = (grad_h2 * vectors[9]).astype(jnp.bfloat16)
    grad_wcross = weight_grad(mixed16, grad_cross16)
    grad_mixed16 = back_input(grad_cross16, w_cross).astype(jnp.bfloat16)
    grad_cq16, grad_far_keys, grad_far_values = attend_back(
        cross_heads, far_keys, far_values, cross_mask, scale, cross_lse, split_heads(grad_mixed16)
    )
    returned = jnp.concatenate(
        [grad_far_keys.reshape(rows, D), grad_far_values.reshape(rows, D)], 1
    )
    grad_keyval16 = from_partner(returned, "branch", 0)
    grad_wkeyval = weight_grad(source16, grad_keyval16)
    grad_h_kv, grad_g3, grad_c3 = norm3_back(back_input(grad_keyval16, w_keyval))
    grad_cq_flat = grad_cq16.reshape(rows, D)
    grad_wquery = weight_grad(cross_in16, grad_cq_flat)
    grad_h_q, grad_g2, grad_c2 = norm2_back(back_input(grad_cq_flat, w_query))
    grad_hidden = grad_h2 + grad_h_q + grad_h_kv
    grad_ls1 = jnp.sum(grad_hidden * self_out, 0)
    grad_self16 = (grad_hidden * vectors[8]).astype(jnp.bfloat16)
    grad_wself = weight_grad(attended16, grad_self16)
    grad_att16 = back_input(grad_self16, w_self).astype(jnp.bfloat16)
    grad_q16, grad_k16, grad_v16 = attend_back(
        query16, key16, value16, self_mask, scale, self_lse, split_heads(grad_att16)
    )
    grad_joined16 = jnp.concatenate(
        [grad_q16.reshape(rows, D), grad_k16.reshape(rows, D), grad_v16.reshape(rows, D)], 1
    )
    grad_wqkv = weight_grad(normed16, grad_joined16)
    grad_x_ln, grad_g1, grad_c1 = norm1_back(back_input(grad_joined16, w_qkv))
    input_grad = grad_hidden + grad_x_ln
    grad_vectors = jnp.stack(
        [
            grad_g1,
            grad_c1,
            grad_g2,
            grad_c2,
            grad_g3,
            grad_c3,
            grad_g4,
            grad_c4,
            grad_ls1,
            grad_ls2,
            grad_ls3,
        ]
    )
    pieces = [
        grad_wqkv,
        grad_wself,
        grad_wquery,
        grad_wkeyval,
        grad_wcross,
        grad_up,
        grad_down,
        grad_vectors,
    ]
    flat_grad = jnp.concatenate([piece.reshape(count, -1) for piece in pieces], 1).reshape(1, -1)
    reduced = lax.psum_scatter(flat_grad, "frames", scatter_dimension=1, tiled=True)
    local_square = jnp.sum(reduced * reduced)
    square_sum = lax.psum(local_square, ("branch", "frames"))
    grad_norm = jnp.sqrt(square_sum)
    total_params = params.shape[1] * count
    total_rows = rows * count
    threshold = 0.01 * math.sqrt(2.0 * total_params * total_rows)
    clipped = reduced * jnp.minimum(1.0, threshold / grad_norm)
    vec_width = NV * D // count
    vector_grad = clipped[:, clipped.shape[1] - vec_width :]
    first_new = BETA_ONE * first_moment + (1.0 - BETA_ONE) * clipped
    second_new = BETA_TWO * second_moment + (1.0 - BETA_TWO) * clipped * clipped
    mean_hat = first_new / (1.0 - BETA_ONE**STEP)
    square_hat = second_new / (1.0 - BETA_TWO**STEP)
    new_params = params - LEARN_RATE * (
        mean_hat / (jnp.sqrt(square_hat) + ADAM_EPS) + DECAY_RATE * params
    )
    return (
        result.astype(jnp.bfloat16)[None],
        input_grad[None],
        clipped,
        vector_grad,
        grad_norm,
        first_new,
        second_new,
        new_params,
    )


MESH = pl.DeviceIdType.MESH
BF = jnp.bfloat16
F32 = jnp.float32
C2 = math.log2(math.e) / math.sqrt(HEAD_DIM)
SCALE = 1.0 / math.sqrt(HEAD_DIM)
N = 1024
TILE = 512
TILES = N // TILE
LEAD = 16
DOWN = LEAD + 36 * 24
ROWS = DOWN + 288
FLAT = 1160
QKV, SELF, QUERY, KEYVAL, CROSS, UP = (0, 9), (216, 3), (288, 3), (360, 6), (504, 3), (576, 12)
ORDER = [e for s in range(3) for e in ((QKV, s), (QKV, 3 + s), (QKV, 6 + s), (SELF, s))]
ORDER += [(m, c) for m in (QUERY, KEYVAL, CROSS, UP) for c in range(m[1])]
OUT_PIECES = ((0, 112), (112, 96), (208, 96), (304, 288), (592, 288), (880, 128), (1008, 160))
BACK_PIECES = ((880, 288), (592, 288), (304, 288), (16, 96), (112, 96), (208, 96))


def remote(src, dst, send, recv, **device):
    return pltpu.make_async_remote_copy(
        src_ref=src, dst_ref=dst, send_sem=send, recv_sem=recv, device_id=device, device_id_type=MESH
    )


def mm(a, b):
    return lax.dot_general(a, b, (((1,), (0,)), ((), ())), preferred_element_type=F32)


def mm_nt(a, b):
    return lax.dot_general(a, b, (((1,), (1,)), ((), ())), preferred_element_type=F32)


def loop(start, stop, body):
    lax.fori_loop(start, stop, lambda i, _: (body(i), 0)[1], 0)


def rows_at(i, size):
    return pl.ds(pl.multiple_of(i * size, size), size)


def normalise(values):
    centre = values - jnp.mean(values, -1, keepdims=True)
    scale = lax.rsqrt(jnp.mean(centre * centre, -1, keepdims=True) + NORM_EPS)
    return centre * scale, scale


def normalise_back(unit, scale, grad):
    return scale * (grad - jnp.mean(grad, -1, keepdims=True) - unit * jnp.mean(grad * unit, -1, keepdims=True))


def att_back_head(q, k, v, o, do, e, inv, e_turned, ds_turned):
    n = k.shape[1]
    values = jnp.concatenate([v, v, jnp.ones((32, n), BF)], 0).T
    do = do.astype(F32)
    minus = -jnp.sum(do * o, 0, keepdims=True) * inv
    do = do * inv
    high = do.astype(BF)
    low = (do - high.astype(F32)).astype(BF)
    minus_high = minus.astype(BF).astype(F32)
    row = lax.broadcasted_iota(jnp.int32, (32, n), 0)
    extra = jnp.where(row == 0, minus_high, jnp.where(row == 1, minus - minus_high, 0.0)).astype(BF)
    grads = jnp.concatenate([high, low, extra], 0)
    e_turned[...] = e.T
    ds = (e.astype(F32) * mm(values, grads)).astype(BF)
    ds_turned[...] = ds.T
    dq = mm(k, ds)
    dk = mm(q, ds_turned[...])
    dv = mm(high, e_turned[...])
    return (dq * SCALE).astype(BF), (dk * SCALE).astype(BF), dv.astype(BF)


def step_kernel(*refs):
    it = iter(refs)
    (x_hbm, cot_hbm, params, seg) = (next(it) for _ in range(4))
    (out_hbm, gin_hbm, flat, norm, e1_hbm, e2_hbm) = (next(it) for _ in range(6))
    (net, r1, s2, r2, vec, vflat, vg, vg0, vsum, vr1, vr2, late, nb) = (next(it) for _ in range(13))
    (wqkv, wself, wquery, wkv, wcross, wup, wdown) = (next(it) for _ in range(7))
    (at, qkv, o1, h, n2t, n3t, cq, kv, far, o2) = (next(it) for _ in range(10))
    (n4t, zt, du, dffn, dh, dcr, dot, dkv_far, gself) = (next(it) for _ in range(9))
    dkv = kv
    (ring, keys, scores, inv1, inv2, hot1, hot2, mask, stage16, x, cot, sq, praw) = (next(it) for _ in range(13))
    (as1, ar1, as2, ar2, as3, ar3, bs1, br1, bs2, br2, bs3, br3, ks, kr, vs, vr, ls, lr, ns, nr, es, os, gs, xs) = (
        next(it) for _ in range(24)
    )
    j = lax.axis_index("frames")
    b = lax.axis_index("branch")
    z, p = j // 4, j % 4

    def zp(k):
        return (z + k) % 4 * 4 + p

    def pp(k):
        return z * 4 + (p + k) % 4

    bar = pltpu.get_barrier_semaphore()
    for k in (1, 2, 3):
        pl.semaphore_signal(bar, inc=1, device_id={"frames": zp(k)}, device_id_type=MESH)
        pl.semaphore_signal(bar, inc=1, device_id={"frames": pp(k)}, device_id_type=MESH)
    for k in range(4):
        pl.semaphore_signal(bar, inc=1, device_id={"branch": 1 - b, "frames": pp(k)}, device_id_type=MESH)

    x_copy = pltpu.make_async_copy(x_hbm, x, xs.at[0])
    cot_copy = pltpu.make_async_copy(cot_hbm, cot, xs.at[1])
    main = params.shape[1] // 1024 * 1024
    urgent = SELF[0] + 24 * SELF[1]
    spans = ((0, urgent * 128), (urgent * 128, params.shape[1] - urgent * 128))
    p_copies = [
        pltpu.make_async_copy(params.at[:, pl.ds(*span)], praw.at[:, pl.ds(*span)], xs.at[2 + i])
        for i, span in enumerate(spans)
    ]

    pflat = flat

    def lay_out(i):
        pflat[rows_at(i, 8), :] = praw[:, pl.ds(pl.multiple_of(i * 1024, 1024), 1024)].reshape(8, 128)

    for c in (*p_copies, x_copy):
        c.start()

    def pack_pairs(start, stop):
        for m in range(start, stop):
            pair = [pflat[pl.ds(mat[0] + c, 24, stride=mat[1]), :] for mat, c in ORDER[2 * m : 2 * m + 2]]
            net[z, p, pl.ds(LEAD + 48 * m, 48), :] = jnp.concatenate(pair, 0).astype(BF)

    p_copies[0].wait()
    loop(0, urgent // 8, lay_out)
    p_copies[1].wait()
    tail = jnp.concatenate([praw[:, main:], jnp.zeros((1, 120), F32)], 1)
    tail = [tail[:, 128 * i : 128 * i + 128] for i in range(3)]
    net[z, p, pl.ds(0, 16), :] = jnp.concatenate(tail + [jnp.zeros((13, 128), F32)], 0).astype(BF)
    pack_pairs(0, 2)
    pl.semaphore_wait(bar, 10)

    others = (1, 2, 3)

    beside = (p + 1 - 2 * (p % 2), (p + 2) % 4, 3 - p)
    turned = len(OUT_PIECES) - 1

    def a1(i, k):
        part = net.at[z, slice(None) if i == turned else p, pl.ds(*OUT_PIECES[i])]
        return remote(part, part, as1.at[i, k - 1], ar1.at[i, k - 1], frames=zp(k))

    def a2(i, k):
        part = net.at[z if i == turned else slice(None), p, pl.ds(*OUT_PIECES[i])]
        return remote(part, part, as2.at[i, k], ar2.at[i, k], frames=z * 4 + beside[k])

    def a3(i, k):
        first, count = OUT_PIECES[i]
        part = net.at[z if i == turned else slice(None), beside[k], pl.ds(first + k * (count // 2), count // 2)]
        return remote(part, part, as3.at[i, k], ar3.at[i, k], frames=z * 4 + beside[1 - k])

    direct = len(BACK_PIECES) - 1

    def b1(i, k):
        first, count = BACK_PIECES[i]
        if i == direct:
            rows = pl.ds(first, count)
            return remote(
                net.at[:, beside[k], rows], r1.at[k, :, rows], bs1.at[i, k], br1.at[i, k], frames=z * 4 + beside[k]
            )
        way, across = k % 2, k // 2
        rows = pl.ds(first + way * (count // 2), count // 2)
        return remote(
            net.at[:, beside[2 if across else way], rows], r1.at[across, :, rows], bs1.at[i, k], br1.at[i, k],
            frames=z * 4 + beside[way],
        )

    def b3(i, k):
        first, count = BACK_PIECES[i]
        rows = pl.ds(first + k * (count // 2), count // 2)
        part = net.at[:, beside[1 - k], rows]
        return remote(part, r1.at[2, :, rows], bs3.at[i, k], br3.at[i, k], frames=z * 4 + beside[1 - k])

    def back_ways(i):
        return range(3 if i == direct else 4)

    def b2(i, k):
        rows = pl.ds(*BACK_PIECES[i])
        return remote(s2.at[k - 1, rows], r2.at[k - 1, rows], bs2.at[i, k - 1], br2.at[i, k - 1], frames=zp(k))

    def out_first(i):
        if i == turned:
            for k in range(2):
                a3(i, k).wait_recv()
        for k in others:
            a1(i, k).start()

    def out_second(i):
        if i != turned:
            for k in others:
                a1(i, k).wait_recv()
        for k in range(2 if i else 3):
            a2(i, k).start()

    def out_third(i):
        for k in range(2):
            a2(i, k).wait_recv()
        for k in range(2):
            a3(i, k).start()

    def out_ready(i):
        if i == turned:
            for k in others:
                a1(i, k).wait_recv()
            return
        for k in range(2 if i else 3):
            (a3 if i else a2)(i, k).wait_recv()

    def back_first(i):
        for k in back_ways(i):
            b1(i, k).start()

    def back_middle(i):
        first, count = BACK_PIECES[i]
        for k in back_ways(i):
            b1(i, k).wait_recv()
        for k in range(2):
            rows = pl.ds(first + k * (count // 2), count // 2)
            to = beside[1 - k]
            for q in range(4):
                net[q, to, rows, :] = (net[q, to, rows, :].astype(F32) + r1[1, q, rows, :].astype(F32)).astype(BF)
            b3(i, k).start()

    def plane_sum(i, to):
        rows = pl.ds(*BACK_PIECES[i])
        total = net[to, p, rows, :].astype(F32) + r1[0, to, rows, :].astype(F32) + r1[2, to, rows, :].astype(F32)
        return total + r1[1, to, rows, :].astype(F32) if i == direct else total

    def back_second(i):
        rows = pl.ds(*BACK_PIECES[i])
        if i == direct:
            for k in back_ways(i):
                b1(i, k).wait_recv()
        else:
            for k in range(2):
                b3(i, k).wait_recv()
        for k in others:
            s2[k - 1, rows, :] = plane_sum(i, (z + k) % 4).astype(BF)
            b2(i, k).start()

    def back_ready(i):
        first, count = BACK_PIECES[i]
        for k in others:
            b2(i, k).wait_recv()
        total = plane_sum(i, z)
        for k in range(3):
            total = total + r2[k, pl.ds(first, count), :].astype(F32)
        if first == DOWN:
            for c in range(3):
                flat[pl.ds(864 + c, 96, stride=3), :] = total[96 * c : 96 * c + 96]
        else:
            for c in range(count // 24):
                mat, col = ORDER[(first - LEAD) // 24 + c]
                flat[pl.ds(mat[0] + col, 24, stride=mat[1]), :] = total[24 * c : 24 * c + 24]
        sq[...] += jnp.sum((total * total).reshape(count // 8, 8, 128), 0)

    def block_pair(m):
        got = net[:, :, pl.ds(LEAD + 48 * m, 48), :].astype(F32).reshape(16, 48, 128)
        return got[:, :24].reshape(384, 128).astype(BF), got[:, 24:].reshape(384, 128).astype(BF)

    weights = {QKV: wqkv, SELF: wself, QUERY: wquery, KEYVAL: wkv, CROSS: wcross, UP: wup}

    def unpack_pairs(start, stop):
        for m in range(start, stop):
            for (mat, c), block in zip(ORDER[2 * m : 2 * m + 2], block_pair(m)):
                if mat in (QKV, QUERY, KEYVAL):
                    weights[mat][pl.ds(128 * c, 128), :] = block.T
                else:
                    weights[mat][:, pl.ds(128 * c, 128)] = block

    def put_pair(first_row, left, right):
        both = jnp.concatenate([left.reshape(16, 24, 128), right.reshape(16, 24, 128)], 1)
        net[:, :, pl.ds(first_row, 48), :] = both.astype(BF).reshape(4, 4, 48, 128)

    out_first(0)
    loop(urgent // 8, main // 1024, lay_out)
    for c in range(3):
        net[z, p, pl.ds(DOWN + 96 * c, 96), :] = pflat[pl.ds(864 + c, 96, stride=3), :].astype(BF)
    out_second(turned)
    pack_pairs(2, 6)
    out_first(1)
    out_first(2)
    pack_pairs(6, 18)
    own = seg[pl.ds(b, 1), :]
    other = seg[pl.ds(1 - b, 1), :]
    number = lax.broadcasted_iota(jnp.int32, (32, N), 0)
    same = number + 4 * j == own
    hot1[...] = jnp.where(same, 1.0, 0.0).astype(BF)
    hot2[...] = jnp.where(number + 4 * j == other, 1.0, 0.0).astype(BF)
    mask[...] = jnp.where(same | (number >= 4), 0.0, MASKED).astype(BF)
    vg[...] = jnp.zeros((16, D), F32)
    vg0[...] = jnp.zeros((8, D), F32)
    sq[...] = jnp.zeros((8, 128), F32)
    out_third(turned)
    out_second(0)
    out_first(3)
    out_second(1)
    out_second(2)
    out_ready(0)

    vflat[...] = jnp.zeros((56, 128), F32)
    lane = lax.broadcasted_iota(jnp.int32, (8, 128), 1)
    sub = lax.broadcasted_iota(jnp.int32, (8, 128), 0)
    for i in range(16):
        got = net[i // 4, i % 4, pl.ds(0, 16), :].astype(F32)[:8]
        got = jnp.where(sub * 128 + lane < 264, got, 0.0)
        if i:
            got = pltpu.roll(got, 8 * i, 1)
            got = jnp.where(lane < 8 * i, pltpu.roll(got, 1, 0), got)
        vflat[pl.ds(2 * i, 8), :] += got
    for c in range(3):
        vec[:, pl.ds(128 * c, 128)] = vflat[pl.ds(c, 16, stride=3), :]
    unpack_pairs(0, 2)

    def vector(i):
        return vec[pl.ds(i, 1), :]

    def add_vector(i, grad):
        vg[pl.ds(i, 1), :] += jnp.sum(grad, 0, keepdims=True)

    def first_norm(t):
        rows = rows_at(t, TILE)
        unit, _ = normalise(x[rows, :].astype(F32))
        at[:, rows] = (unit * vector(0) + vector(1)).astype(BF).T

    x_copy.wait()
    cot_copy.start()
    loop(0, TILES, first_norm)

    def project(w, n_ref, to):
        def part(i):
            rows = rows_at(i, D)
            to[rows, :] = mm(w[rows, :], n_ref[...]).astype(BF)

        loop(0, to.shape[0] // D, part)


    def project_round(i):
        parts = [pl.ds(D * m + 128 * i, 128) for m in range(3)]
        got = mm(jnp.concatenate([wqkv[part, :] for part in parts], 0), at[...]).astype(BF)
        for m, part in enumerate(parts):
            qkv[part, :] = got[128 * m : 128 * m + 128]

    project_round(0)

    def head(ref, first, i):
        return ref[pl.ds(pl.multiple_of(first + i * 48, 16), 48), :]

    def set_head(ref, first, i, value):
        ref[pl.ds(pl.multiple_of(first + i * 48, 16), 48), :] = value

    def e_out(e_hbm, i):
        return pltpu.make_async_copy(ring.at[i % 2], e_hbm.at[i], es.at[i % 2])

    def e_in(e_hbm, i):
        return pltpu.make_async_copy(e_hbm.at[i], ring.at[i % 2], es.at[i % 2])

    half, chunk = N // 2, 256

    def attend(q, kvs, kfirst, hot, o_ref, inv_ref, e_hbm, before):
        def make_keys(i):
            k32 = head(kvs, kfirst, i).astype(F32) * C2
            high = k32.astype(BF)
            low = (k32 - high.astype(F32)).astype(BF)
            keys[i % 2] = jnp.concatenate([high, low, hot[...]], 0).T

        def make_queries(i, t):
            at_t = slice(t * half, (t + 1) * half)
            mine = q[pl.ds(pl.multiple_of(i * 48, 16), 48), at_t]
            return jnp.concatenate([mine, mine, mask[:, at_t]], 0)

        def score(i, t, c, queries, top):
            rows = slice(c * chunk, (c + 1) * chunk)
            got = mm(keys[i % 2, rows, :], queries)
            scores[t, rows, :] = got
            got = jnp.max(got.reshape(chunk // 8, 8, half), 0)
            return got if c == 0 else jnp.maximum(top, got)

        make_keys(0)
        top = None
        queries = make_queries(0, 0)
        for c in range(N // chunk):
            top = score(0, 0, c, queries, top)

        def one(i, top):
            after = jnp.minimum(i + 1, HEADS - 1)
            @pl.when(i >= 2)
            def _():
                e_out(e_hbm, i - 2).wait()

            values = jnp.concatenate([head(kvs, kfirst + D, i), jnp.ones((16, N), BF)], 0)
            for t in range(2):
                if t:
                    before(i)
                    make_keys(after)
                next_head, next_half = (after, 0) if t else (i, 1)
                peak = jnp.max(top, 0, keepdims=True)
                queries = make_queries(next_head, next_half)
                at_t = slice(t * half, (t + 1) * half)
                o = jnp.zeros((64, half), F32)
                for c in range(N // chunk):
                    rows = slice(c * chunk, (c + 1) * chunk)
                    top = score(next_head, next_half, c, queries, top)
                    e = jnp.exp2(scores[t, rows, :] - peak).astype(BF)
                    ring[i % 2, rows, at_t] = e
                    o = o + mm(values[:, rows], e)
                inv = 1.0 / o[48:49]
                o_ref[pl.ds(pl.multiple_of(i * 48, 16), 48), at_t] = o[:48] * inv
                inv_ref[pl.ds(i, 1), at_t] = inv
            e_out(e_hbm, i).start()
            return top

        lax.fori_loop(0, HEADS, one, top)
        for i in (6, 7):
            e_out(e_hbm, i).wait()

    def attend_back(q, kvs, kfirst, o_ref, inv_ref, e_hbm, dk_ref, dfirst, before):
        e_in(e_hbm, 0).start()

        def one(i):
            @pl.when(i + 1 < HEADS)
            def _():
                e_in(e_hbm, i + 1).start()

            before(i)
            e_in(e_hbm, i).wait()
            dq, dk, dv = att_back_head(
                head(q, 0, i), head(kvs, kfirst, i), head(kvs, kfirst + D, i), head(o_ref, 0, i), head(dot, 0, i),
                ring[i % 2], inv_ref[pl.ds(i, 1), :], zt.at[pl.ds(0, N)], du.at[:, pl.ds(0, N)],
            )
            set_head(q, 0, i, dq)
            set_head(dk_ref, dfirst, i, dk)
            set_head(dk_ref, dfirst + D, i, dv)

        loop(0, HEADS, one)

    def at_head(i, **steps):
        for name, step in steps.items():
            pl.when(i == int(name[1:]))(step)

    def second_round():
        out_ready(1)
        out_third(2)
        unpack_pairs(2, 4)
        project_round(1)

    def third_round():
        out_ready(2)
        unpack_pairs(4, 6)
        project_round(2)

    def steps(*calls):
        def run():
            for f, i in calls:
                f(i)

        return run

    attend(
        qkv, qkv, D, hot1, o1, inv1, e1_hbm,
        lambda i: at_head(
            i, h0=steps((out_third, 1), (out_second, 3), (out_first, 4)), h1=second_round,
            h2=steps((out_first, 5), (out_first, turned)), h4=third_round, h5=steps((out_third, 3), (out_second, 4)),
        ),
    )
    out_ready(3)
    unpack_pairs(6, 12)

    def second_norm(t):
        rows = rows_at(t, TILE)
        self_out = mm(o1[:, rows].astype(BF).T, wself[...])
        hidden = x[rows, :].astype(F32) + vector(8) * self_out
        h[rows, :] = hidden
        unit, _ = normalise(hidden)
        n2t[:, rows] = (unit * vector(2) + vector(3)).astype(BF).T
        n3t[:, rows] = (unit * vector(4) + vector(5)).astype(BF).T

    loop(0, TILES, second_norm)
    project(wkv, n3t, kv)
    send_kv = remote(kv, far, ks.at[0], kr.at[0], branch=1 - b)
    send_kv.start()
    project(wquery, n2t, cq)
    send_kv.wait_recv()
    attend(
        cq, far, 0, hot2, o2, inv2, e2_hbm,
        lambda i: at_head(i, h1=steps((out_third, 4), (out_second, 5)), h5=steps((out_third, 5))),
    )
    out_ready(4)
    unpack_pairs(12, 18)
    out_ready(5)
    out_ready(turned)
    for c in range(3):
        wdown[:, pl.ds(128 * c, 128)] = net[:, :, pl.ds(DOWN + 96 * c, 96), :].reshape(1536, 128)
    send_kv.wait_send()
    for i in range(len(OUT_PIECES)):
        for k in others:
            a1(i, k).wait_send()
        for k in range(2 if i else 3):
            a2(i, k).wait_send()
            if i:
                a3(i, k).wait_send()

    def out_copy(t):
        return pltpu.make_async_copy(stage16.at[t % 2], out_hbm.at[rows_at(t, TILE)], os.at[t % 2])

    def feed_forward(t):
        rows = rows_at(t, TILE)
        cross_out = mm(o2[:, rows].astype(BF).T, wcross[...])
        second_h = h[rows, :] + vector(9) * cross_out
        unit, scale = normalise(second_h)
        n4 = (unit * vector(6) + vector(7)).astype(BF)
        n4t[:, rows] = n4.T
        grad_out = cot[rows, :].astype(F32)
        dffn16 = (grad_out * vector(10)).astype(BF)
        dffn[rows, :] = dffn16
        ffn_out = jnp.zeros((TILE, D), F32)
        dn4 = jnp.zeros((TILE, D), F32)
        for c in range(FF // 512):
            part = slice(c * 512, (c + 1) * 512)
            u = mm(n4, wup[:, part])
            share = 0.5 * (1.0 + lax.erf(u * math.sqrt(0.5)))
            slope = share + u * (jnp.exp(-0.5 * u * u) * (1.0 / math.sqrt(2.0 * math.pi)))
            z16 = (u * share).astype(BF)
            zt[part, rows] = z16.T
            ffn_out = ffn_out + mm(z16, wdown[part, :])
            du16 = (mm_nt(dffn16, wdown[part, :]) * slope).astype(BF)
            du[rows, part] = du16
            dn4 = dn4 + mm_nt(du16, wup[:, part])

        @pl.when(t >= 2)
        def _():
            out_copy(t - 2).wait()

        stage16[t % 2] = (second_h + vector(10) * ffn_out).astype(BF)
        out_copy(t).start()
        add_vector(10, grad_out * ffn_out)
        add_vector(6, dn4 * unit)
        add_vector(7, dn4)
        dh2 = grad_out + normalise_back(unit, scale, dn4 * vector(6))
        dh[rows, :] = dh2
        add_vector(9, dh2 * cross_out)
        dcross16 = (dh2 * vector(9)).astype(BF)
        dcr[rows, :] = dcross16
        dot[:, rows] = mm_nt(wcross[...], dcross16).astype(BF)

    cot_copy.wait()
    loop(0, TILES, feed_forward)
    for i in (TILES - 2, TILES - 1):
        out_copy(i).wait()

    def down_grad(i):
        grad = mm(zt[rows_at(i, D), :], dffn[...])
        for c in range(3):
            net[i, :, pl.ds(DOWN + 96 * c, 96), :] = grad[:, 128 * c : 128 * c + 128].astype(BF).reshape(4, 96, 128)

    loop(0, 4, down_grad)
    back_first(0)

    def up_grad(i):
        grad = mm(n4t[...], du[:, rows_at(i, 256)])
        put_pair(pl.multiple_of(LEAD + 24 * 24 + 48 * i, 16), grad[:, :128], grad[:, 128:])

    loop(0, 6, up_grad)
    back_first(1)
    attend_back(
        cq, far, 0, o2, inv2, e2_hbm, dkv, 0, lambda i: at_head(i, h4=lambda: back_middle(0), h7=lambda: back_middle(1))
    )
    send_dkv = remote(dkv, dkv_far, ks.at[1], kr.at[1], branch=1 - b)
    send_dkv.start()
    back_second(0)
    g_query = mm_nt(n2t[...], cq[...])
    g_cross = mm(o2[...].astype(BF), dcr[...])
    put_pair(LEAD + 24 * 12, g_query[:, :128], g_query[:, 128:256])
    put_pair(LEAD + 24 * 22, g_cross[:, 128:256], g_cross[:, 256:])
    send_dkv.wait_recv()

    def third_back(t):
        rows = rows_at(t, TILE)
        dn2 = mm(cq[:, rows].T, wquery[...])
        dn3 = mm(dkv_far[:, rows].T, wkv[...])
        unit, scale = normalise(h[rows, :])
        add_vector(2, dn2 * unit)
        add_vector(3, dn2)
        add_vector(4, dn3 * unit)
        add_vector(5, dn3)
        hidden_grad = dh[rows, :] + normalise_back(unit, scale, dn2 * vector(2) + dn3 * vector(4))
        dh[rows, :] = hidden_grad
        self_out = mm(o1[:, rows].astype(BF).T, wself[...])
        add_vector(8, hidden_grad * self_out)
        dself16 = (hidden_grad * vector(8)).astype(BF)
        dcr[rows, :] = dself16
        dot[:, rows] = mm_nt(wself[...], dself16).astype(BF)

    g_kv = mm_nt(n3t[...], dkv_far[...])
    put_pair(LEAD + 24 * 14, g_query[:, 256:], g_kv[:, :128])
    put_pair(LEAD + 24 * 16, g_kv[:, 128:256], g_kv[:, 256:384])
    put_pair(LEAD + 24 * 18, g_kv[:, 384:512], g_kv[:, 512:640])
    put_pair(LEAD + 24 * 20, g_kv[:, 640:], g_cross[:, :128])
    back_first(2)
    back_second(1)
    loop(0, TILES, third_back)
    gself[...] = mm(o1[...].astype(BF), dcr[...])
    back_ready(0)

    def v1(k):
        return remote(vg, vr1.at[k - 1], vs.at[0, k - 1], vr.at[0, k - 1], frames=pp(k))

    def v2(k):
        return remote(vsum, vr2.at[k - 1], vs.at[1, k - 1], vr.at[1, k - 1], frames=zp(k))

    for k in others:
        v1(k).start()

    def round_grad(i):
        parts = [qkv[pl.ds(D * m + 128 * i, 128), :] for m in range(3)]
        g = mm_nt(at[...], jnp.concatenate(parts, 0))
        put_pair(LEAD + 96 * i, g[:, :128], g[:, 128:256])
        put_pair(LEAD + 96 * i + 48, g[:, 256:], gself[:, 128 * i : 128 * i + 128])
        back_first(3 + i)

    def vectors_on():
        for k in others:
            v1(k).wait_recv()
        vsum[...] = vg[...] + vr1[0] + vr1[1] + vr1[2]
        for k in others:
            v2(k).start()

    def vectors_there():
        for k in others:
            v2(k).wait_recv()
        total = vsum[...] + vr2[0] + vr2[1] + vr2[2]
        for c in range(3):
            vflat[pl.ds(c, 16, stride=3), :] = total[:, 128 * c : 128 * c + 128]

    def ahead(i):
        @pl.when(i == 2)
        def _():
            back_middle(2)
            back_ready(1)

        @pl.when(i == 3)
        def _():
            round_grad(0)
            vectors_on()

        @pl.when(i == 4)
        def _():
            back_second(2)

        @pl.when(i == 5)
        def _():
            back_middle(3)
            vectors_there()

        @pl.when(i == 6)
        def _():
            round_grad(1)

        @pl.when(i == 7)
        def _():
            back_second(3)
            back_middle(4)
            back_ready(2)

    attend_back(qkv, qkv, D, o1, inv1, e1_hbm, qkv, D, ahead)
    round_grad(2)
    back_second(4)

    def gin_copy(t):
        return pltpu.make_async_copy(dh.at[rows_at(t, TILE)], gin_hbm.at[rows_at(t, TILE)], gs.at[t])

    def first_back(t):
        rows = rows_at(t, TILE)
        dn1 = mm(qkv[:, rows].T, wqkv[...])
        unit, scale = normalise(x[rows, :].astype(F32))
        vg0[0:1, :] += jnp.sum(dn1 * unit, 0, keepdims=True)
        vg0[1:2, :] += jnp.sum(dn1, 0, keepdims=True)
        dh[rows, :] = dh[rows, :] + normalise_back(unit, scale, dn1 * vector(0))
        gin_copy(t).start()

    loop(0, TILES, first_back)
    blocks = [vg0[r : r + 1, 128 * c : 128 * c + 128] for r in range(2) for c in range(3)]
    late[pl.ds(j, 1)] = jnp.concatenate(blocks + [jnp.zeros((2, 128), F32)], 0)[None]

    def far_vector(k):
        return remote(late.at[j], late.at[j], ls.at[k - 1], lr.at[k - 1], frames=(j + k) % 16)

    for k in range(1, 16):
        far_vector(k).start()
    back_second(5)
    back_ready(3)
    back_ready(4)
    for k in range(1, 16):
        far_vector(k).wait_recv()
    vflat[pl.ds(0, 8), :] += jnp.sum(late[...], 0)
    near = vflat[pl.ds(2 * j, 8), :]
    turn = (128 - 8 * j) % 128
    near = pltpu.roll(near, turn, 1)
    near = jnp.where(lane < 128 - 8 * j, near, pltpu.roll(near, 7, 0))
    near = jnp.where(sub * 128 + lane < 264, near, 0.0)
    flat[pl.ds(1152, 8), :] = near
    back_ready(5)
    squares = sq[...] + near * near
    me = 16 * b + j
    nb[pl.ds(me, 1), 0:1, :] = jnp.sum(squares, 0, keepdims=True)[None]

    def far_square(k):
        to = (me + k) % 32
        part = nb.at[me, pl.ds(0, 1)]
        return remote(part, part, ns.at[k - 1], nr.at[k - 1], branch=to // 16, frames=to % 16)

    for k in range(1, 32):
        far_square(k).start()
    for k in range(1, 32):
        far_square(k).wait_recv()
    norm[...] = jnp.sum(nb[:, 0, :], 0, keepdims=True)
    for i in range(len(BACK_PIECES)):
        for k in others:
            b2(i, k).wait_send()
        for k in back_ways(i):
            b1(i, k).wait_send()
        if i != direct:
            for k in range(2):
                b3(i, k).wait_send()
    for k in others:
        v1(k).wait_send()
        v2(k).wait_send()
    for k in range(1, 16):
        far_vector(k).wait_send()
    for k in range(1, 32):
        far_square(k).wait_send()
    send_dkv.wait_send()
    for i in range(TILES):
        gin_copy(i).wait()


def step(x, cot, params, seg):
    dma = pltpu.SemaphoreType.DMA
    v = pltpu.VMEM
    whole = pl.BlockSpec(memory_space=v)
    hbm = pl.BlockSpec(memory_space=pl.ANY)
    shape = jax.ShapeDtypeStruct
    n_out, n_back = len(OUT_PIECES), len(BACK_PIECES)
    return pl.pallas_call(
        step_kernel,
        out_shape=(
            shape((N, D), BF), shape((N, D), F32), shape((FLAT, 128), F32), shape((1, 128), F32),
            shape((HEADS, N, N), BF), shape((HEADS, N, N), BF),
        ),
        in_specs=[hbm, hbm, hbm, whole],
        out_specs=(hbm, hbm, whole, whole, hbm, hbm),
        scratch_shapes=[
            v((4, 4, ROWS, 128), BF), v((3, 4, ROWS, 128), BF), v((3, ROWS, 128), BF), v((3, ROWS, 128), BF),
            v((16, D), F32), v((56, 128), F32), v((16, D), F32), v((8, D), F32), v((16, D), F32), v((3, 16, D), F32),
            v((3, 16, D), F32), v((16, 8, 128), F32), v((32, 8, 128), F32),
            v((3 * D, D), BF), v((D, D), BF), v((D, D), BF), v((2 * D, D), BF), v((D, D), BF), v((D, FF), BF),
            v((FF, D), BF),
            v((D, N), BF), v((3 * D, N), BF), v((D, N), F32), v((N, D), F32), v((D, N), BF), v((D, N), BF),
            v((D, N), BF), v((2 * D, N), BF), v((2 * D, N), BF), v((D, N), F32),
            v((D, N), BF), v((FF, N), BF), v((N, FF), BF), v((N, D), BF), v((N, D), F32), v((N, D), BF),
            v((D, N), BF), v((2 * D, N), BF), v((D, D), F32),
            v((2, N, N), BF), v((2, N, 128), BF), v((2, N, N // 2), F32), v((HEADS, N), F32), v((HEADS, N), F32), v((32, N), BF), v((32, N), BF), v((32, N), BF),
            v((2, TILE, D), BF), v((N, D), BF), v((N, D), BF), v((8, 128), F32),
            v(params.shape, F32),
            dma((n_out, 3)), dma((n_out, 3)), dma((n_out, 3)), dma((n_out, 3)), dma((n_out, 2)), dma((n_out, 2)),
            dma((n_back, 4)), dma((n_back, 4)), dma((n_back, 3)), dma((n_back, 3)), dma((n_back, 2)), dma((n_back, 2)),
            dma((2,)), dma((2,)), dma((2, 3)), dma((2, 3)), dma((15,)), dma((15,)), dma((31,)), dma((31,)),
            dma((2,)), dma((2,)), dma((2,)), dma((5,)),
        ],
        compiler_params=pltpu.CompilerParams(
            collective_id=0, has_side_effects=True, vmem_limit_bytes=63 * 1024 * 1024
        ),
        name="step",
    )(x, cot, params, seg)


def finish_kernel(threshold, flat, square, params, first, second, out, grad_in, *rest):
    (clip_o, vector_o, norm_o, first_o, second_o, params_o, out_o, grad_in_o) = rest[:8]
    (p, m, v, c_s, tail_p, tail_m, tail_v, tail_c, o_s, g_s, big_in, big_out, tail_in, tail_out, way_in, way_out) = rest[8:]
    size = params.shape[1]
    main = size // 1024 * 1024
    parts = 4
    rows = main // 128 // parts
    moves = []
    for i, (src, by, dst) in enumerate(((out, o_s, out_o), (grad_in, g_s, grad_in_o))):
        count = src.shape[0] // 2
        for k in range(2):
            at = pl.ds(k * count, count)
            moves.append((
                pltpu.make_async_copy(src.at[at], by.at[at], way_in.at[i, k]),
                pltpu.make_async_copy(by.at[at], dst.at[at], way_out.at[i, k]),
            ))
    reads = []
    for i in range(parts):
        at = pl.ds(i * rows * 128, rows * 128)
        here = pl.ds(i * rows, rows)
        for k, (src, dst) in enumerate(((params, p), (first, m), (second, v))):
            c = pltpu.make_async_copy(src.at[:, at].reshape(rows, 128), dst.at[here], big_in.at[i, k])
            c.start()
            reads.append(c)
        moves[i][0].start()
    for k, (src, dst) in enumerate(((params, tail_p), (first, tail_m), (second, tail_v))):
        c = pltpu.make_async_copy(src.at[:, pl.ds(main, size - main)], dst, tail_in.at[k])
        c.start()
        reads.append(c)
    norm = jnp.sqrt(jnp.sum(square[...], keepdims=True))
    norm_o[...] = norm
    share = jnp.minimum(1.0, threshold / norm)

    def update(grad, p_ref, m_ref, v_ref):
        clipped = grad * share
        first_new = BETA_ONE * m_ref[...] + (1.0 - BETA_ONE) * clipped
        second_new = BETA_TWO * v_ref[...] + (1.0 - BETA_TWO) * clipped * clipped
        mean_hat = first_new / (1.0 - BETA_ONE**STEP)
        square_hat = second_new / (1.0 - BETA_TWO**STEP)
        old = p_ref[...]
        p_ref[...] = old - LEARN_RATE * (mean_hat / (jnp.sqrt(square_hat) + ADAM_EPS) + DECAY_RATE * old)
        m_ref[...] = first_new
        v_ref[...] = second_new
        return clipped

    writes = []
    for i in range(parts):
        for c in reads[3 * i : 3 * i + 3]:
            c.wait()
        here = pl.ds(i * rows, rows)
        c_s[here] = update(flat[here], p.at[here], m.at[here], v.at[here])
        at = pl.ds(i * rows * 128, rows * 128)
        for k, (src, dst) in enumerate(((c_s, clip_o), (m, first_o), (v, second_o), (p, params_o))):
            c = pltpu.make_async_copy(
                src.at[here], dst.at[:, at].reshape(rows, 128), big_out.at[i, k]
            )
            c.start()
            writes.append(c)
        come, go = moves[i]
        come.wait()
        go.start()
        writes.append(go)
    for c in reads[3 * parts :]:
        c.wait()
    wide = jnp.concatenate([flat[main // 128 + i : main // 128 + i + 1] for i in range(3)], 1)
    tail_c[...] = update(wide[:, : size - main], tail_p, tail_m, tail_v)
    vector_o[...] = tail_c[...]
    for k, (src, dst) in enumerate(((tail_c, clip_o), (tail_m, first_o), (tail_v, second_o), (tail_p, params_o))):
        c = pltpu.make_async_copy(src, dst.at[:, pl.ds(main, size - main)], tail_out.at[k])
        c.start()
        writes.append(c)
    for c in writes:
        c.wait()


def finish(threshold, flat, square, params, first, second, out, grad_in):
    size = params.shape[1]
    main = size // 1024 * 1024
    dma = pltpu.SemaphoreType.DMA
    v = pltpu.VMEM
    whole = pl.BlockSpec(memory_space=v)
    hbm = pl.BlockSpec(memory_space=pl.ANY)
    shape = jax.ShapeDtypeStruct
    like = shape(params.shape, F32)
    return pl.pallas_call(
        partial(finish_kernel, threshold),
        out_shape=(
            like, shape((1, size - main), F32), shape((1, 1), F32), like, like, like, shape(out.shape, BF),
            shape(grad_in.shape, F32),
        ),
        in_specs=[whole, whole, hbm, hbm, hbm, hbm, hbm],
        out_specs=(hbm, whole, whole, hbm, hbm, hbm, hbm, hbm),
        scratch_shapes=[v((main // 128, 128), F32)] * 4 + [v((1, size - main), F32)] * 4
        + [v(out.shape, BF), v(grad_in.shape, F32)]
        + [dma((4, 3)), dma((4, 4)), dma((3,)), dma((4,)), dma((2, 2)), dma((2, 2))],
        name="finish",
    )(flat, square, params, first, second, out, grad_in)


def fast_device(frames_in, seg_ids, cotangent, params, first_moment, second_moment):
    count = lax.axis_size("frames")
    size = params.shape[1]
    result, input_grad, flat, square, _, _ = step(frames_in[0], cotangent[0], params, seg_ids)
    total_params = size * count
    total_rows = frames_in.shape[1] * count
    threshold = 0.01 * math.sqrt(2.0 * total_params * total_rows)
    clipped, vector_grad, norm, first_new, second_new, new_params, result, input_grad = finish(
        threshold, flat, square, params, first_moment, second_moment, result, input_grad
    )
    return (
        result[None], input_grad[None], clipped, vector_grad, norm.reshape(()), first_new, second_new, new_params,
    )


def solution(mesh):
    placed = (
        P("branch", "frames", None),
        P(None, "frames"),
        P("branch", "frames", None),
        P("branch", "frames"),
        P("branch", "frames"),
        P("branch", "frames"),
    )
    return jax.shard_map(
        fast_device if mesh.shape["frames"] == 16 else on_device,
        mesh=mesh,
        in_specs=placed,
        out_specs=(
            P("branch", "frames", None),
            P("branch", "frames", None),
            P("branch", "frames"),
            P("branch", "frames"),
            P(),
            P("branch", "frames"),
            P("branch", "frames"),
            P("branch", "frames"),
        ),
        check_vma=False,
    )
```
